32 devices in a mesh: sec: 2 (over y), ty: 4 (over x, core), tx: 4 (over z).
Axes of the slice: x: 2, y: 2, z: 4, core: 2. Of those that a mesh axis runs over, the one named last changes fastest.
Arguments:
- images: float32 [2, 1024, 2048], P('sec', 'ty', 'tx'), may hold values from -12 to 12
Outputs:
- relaxed: float32 [2, 2, 16, 32], P('sec', None, 'ty', 'tx')
- cumulative: float32 [2, 2, 16, 32], P('sec', None, 'ty', 'tx')
The draws below stay inside these ranges and needn't reach their ends.
All inputs are finite; a program needn't handle non-finite values.
Results may differ from the reference program's by a relative error of at most 0.0003.
Values sent between devices are 32-bit elements; how exact they have to be, the bound alone decides.
No kernel may reach another device: no remote copies, remote signals or barrier semaphores. Data moves between devices by JAX's collectives and lax.ppermute only.
A program may use at most 64 MiB of HBM per device.

```python
import jax
import jax.numpy as jnp
from jax import lax

PATCH = 128
STRIDE = 64
SECTIONS = 2
NY = 1024
NX = 2048
NODES_Y = 16


def draw_images(key, part):
    shifts = jax.random.randint(jax.random.fold_in(key, 11), (SECTIONS, 2, 2), -20, 21)
    base = jax.random.normal(jax.random.fold_in(key, 12), (SECTIONS, NY, NX), jnp.float32)
    layers = [base[0]]
    for index in range(1, SECTIONS):
        previous = layers[-1]
        moved_one = jnp.roll(jnp.roll(previous, shifts[index, 0, 0], axis=0), shifts[index, 0, 1], axis=1)
        layers.append(0.03 * moved_one + 0.9995 * base[index])
    stacked = jnp.stack(layers)
    return jnp.clip(stacked, -12.0, 12.0).astype(jnp.float32)


def setup_inputs(seed: int = 0) -> dict:
    arg_keys = jax.random.split(jax.random.key(seed), 2)
    return {
        "images": draw_images(jax.random.fold_in(arg_keys[1], 71), 0),
    }


stiffness = 1.0
rate = 0.25


def soft_flow(corr):
    count = corr.shape[0]
    scores = corr / PATCH
    weights = jax.nn.softmax(scores.reshape(count, PATCH * PATCH), axis=-1).reshape(count, PATCH, PATCH)
    offsets = jnp.arange(PATCH)
    offsets = jnp.where(offsets < PATCH // 2, offsets, offsets - PATCH).astype(jnp.float32)
    flow_y = jnp.sum(weights * offsets[:, None], axis=(1, 2))
    flow_x = jnp.sum(weights * offsets[None, :], axis=(1, 2))
    return jnp.stack([flow_y, flow_x])


def band_patches(band):
    nodes = band.shape[1] // STRIDE - 1
    columns = band.reshape(PATCH, nodes + 1, STRIDE)
    pieces = jnp.concatenate([columns[:, :-1], columns[:, 1:]], axis=2)
    pieces = jnp.transpose(pieces, (1, 0, 2))
    return pieces - jnp.mean(pieces, axis=(1, 2), keepdims=True)


def section_flow(pair):
    first_img, second_img = pair
    half = STRIDE // 2
    first_pad = jnp.pad(first_img, half)
    second_pad = jnp.pad(second_img, half)

    def row_flow(row_index):
        start = (row_index * STRIDE).astype(jnp.int32)
        first_band = lax.dynamic_slice_in_dim(first_pad, start, PATCH, 0)
        second_band = lax.dynamic_slice_in_dim(second_pad, start, PATCH, 0)
        first_freq = jnp.fft.fft2(band_patches(first_band))
        second_freq = jnp.fft.fft2(band_patches(second_band))
        corr = jnp.real(jnp.fft.ifft2(jnp.conj(first_freq) * second_freq)).astype(jnp.float32)
        return soft_flow(corr)

    rows = lax.map(row_flow, jnp.arange(NODES_Y, dtype=jnp.int32))
    return jnp.transpose(rows, (1, 0, 2))


def relax_step(field, flow):
    padded = jnp.pad(field, ((0, 0), (0, 0), (1, 1), (1, 1)))
    lap = padded[:, :, :-2, 1:-1] + padded[:, :, 2:, 1:-1] + padded[:, :, 1:-1, :-2] + padded[:, :, 1:-1, 2:] - 4.0 * field
    return field + rate * (stiffness * lap + flow - field)


def reference(images):
    following = jnp.concatenate([images[1:], jnp.zeros_like(images[:1])], axis=0)
    flows = lax.map(section_flow, (images, following))
    keep = (jnp.arange(SECTIONS) < SECTIONS - 1).astype(jnp.float32)
    flows = flows * keep[:, None, None, None]
    relaxed = flows
    for step in range(2):
        relaxed = relax_step(relaxed, flows)
    totals = jnp.cumsum(relaxed, axis=0)
    cumulative = jnp.concatenate([jnp.zeros_like(relaxed[:1]), totals[:-1]], axis=0)
    return relaxed, cumulative
```

```python
import functools

import jax
import jax.numpy as jnp
import numpy as np
from jax import lax
from jax.experimental import pallas as pl
from jax.experimental.pallas import tpu as pltpu
from jax.sharding import PartitionSpec as P

PATCH = 128
STRIDE = 64
HALF = STRIDE // 2
FREQ = -(-(PATCH // 2 + 1) // 8) * 8

stiffness = 1.0
rate = 0.25


def two_parts(table):
    high = table.astype(jnp.bfloat16)
    low = (table - high.astype(np.float64)).astype(jnp.bfloat16)
    return high, low


def tables():
    angle = 2.0 * np.pi * (np.outer(np.arange(PATCH), np.arange(PATCH)) % PATCH) / PATCH
    cosine, sine = np.cos(angle), np.sin(angle)
    kept = np.arange(FREQ)[:, None] <= PATCH // 2
    left = np.concatenate([cosine[:FREQ] * kept, -sine[:FREQ] * kept])
    right = np.block([[cosine, -sine], [sine, cosine]])
    share = np.where((np.arange(FREQ) == 0) | (np.arange(FREQ) == PATCH // 2), 1.0, 2.0)
    scaled = (share * kept[:, 0])[None, :] / float(PATCH) ** 3
    back = np.concatenate([cosine[:, :FREQ] * scaled, sine[:, :FREQ] * scaled], axis=1)
    left_hi, left_lo = two_parts(left)
    back_hi, back_lo = two_parts(back)
    right_hi, right_lo = two_parts(right)
    return (
        np.concatenate([left_hi, left_hi, left_lo], axis=1),
        np.stack([right_hi, right_lo]),
        np.concatenate([back_hi, back_hi, back_lo], axis=1),
    )


def split(values):
    high = values.astype(jnp.bfloat16)
    return high, (values - high.astype(jnp.float32)).astype(jnp.bfloat16)


def mul(a, b):
    return jnp.dot(a, b, preferred_element_type=jnp.float32)


def right_dft(values, right_ref):
    high, low = split(values)
    return mul(high, right_ref[0]) + mul(low, right_ref[0]) + mul(high, right_ref[1])


def flow_kernel(rows, cols, group, region_ref, left_ref, right_ref, back_ref, flow_ref,
                high_ref, low_ref, half_ref, peak_ref, mass_ref, tilt_ref):
    wide = cols * STRIDE
    for z in range(2):
        even, odd = region_ref[z, :, :wide], region_ref[z, :, STRIDE:STRIDE + wide]
        for part, values in enumerate((even, odd)):
            high, low = split(values)
            high_ref[z, :, part * wide:(part + 1) * wide] = high
            low_ref[z, :, part * wide:(part + 1) * wide] = low
    order = [2 * t for t in range(cols // 2)] + [2 * t + 1 for t in range(cols // 2)]
    for z in range(2):
        for i in range(rows):
            band = pl.ds(i * STRIDE, PATCH)
            high = high_ref[z, band, :]
            stacked = jnp.concatenate([high, low_ref[z, band, :], high], axis=0)
            out = mul(left_ref[...], stacked)
            for t, j in enumerate(order):
                lanes = slice(t * PATCH, (t + 1) * PATCH)
                half_ref[z, i * cols + j, :, :PATCH] = out[:FREQ, lanes]
                half_ref[z, i * cols + j, :, PATCH:] = out[FREQ:, lanes]
    row = lax.broadcasted_iota(jnp.int32, (group, FREQ, PATCH), 1)
    lane = lax.broadcasted_iota(jnp.int32, (group, FREQ, PATCH), 2)
    varies = ((row + lane) > 0).astype(jnp.float32).reshape(group * FREQ, PATCH)
    lag = lax.broadcasted_iota(jnp.int32, (PATCH, 1), 0)
    lag = jnp.where(lag < PATCH // 2, lag, lag - PATCH).astype(jnp.float32)
    for n in range(0, rows * cols, group):
        both = half_ref[:, n:n + group].reshape(2 * group * FREQ, 2 * PATCH)
        freq = right_dft(both, right_ref)
        first, second = freq[:group * FREQ], freq[group * FREQ:]
        re1, im1 = first[:, :PATCH] * varies, first[:, PATCH:] * varies
        re2, im2 = second[:, :PATCH] * varies, second[:, PATCH:] * varies
        cross = jnp.concatenate([re1 * re2 + im1 * im2, im1 * re2 - re1 * im2], axis=1)
        mixed = right_dft(cross, right_ref)
        columns = []
        for m in range(group):
            part = mixed[m * FREQ:(m + 1) * FREQ]
            columns.append(jnp.concatenate([part[:, :PATCH], part[:, PATCH:]], axis=0))
        high, low = split(jnp.concatenate(columns, axis=1))
        scores = mul(back_ref[...], jnp.concatenate([high, low, high], axis=0))
        peak = jnp.max(scores, axis=0, keepdims=True)
        weight = jnp.exp(scores - peak)
        mass = jnp.sum(weight, axis=0, keepdims=True)
        tilt = jnp.sum(weight * lag, axis=0, keepdims=True)
        for m in range(group):
            lanes = slice(m * PATCH, (m + 1) * PATCH)
            peak_ref[n + m:n + m + 1, :] = peak[:, lanes]
            mass_ref[n + m:n + m + 1, :] = mass[:, lanes]
            tilt_ref[n + m:n + m + 1, :] = tilt[:, lanes]
    peak = peak_ref[...]
    share = jnp.exp(peak - jnp.max(peak, axis=1, keepdims=True))
    mass = mass_ref[...] * share
    lag = lax.broadcasted_iota(jnp.int32, mass.shape, 1)
    place = lax.broadcasted_iota(jnp.int32, mass.shape, 0) % cols
    here = lag == place
    lag = jnp.where(lag < PATCH // 2, lag, lag - PATCH).astype(jnp.float32)
    total = jnp.sum(mass, axis=1, keepdims=True)
    flow_y = jnp.sum(tilt_ref[...] * share, axis=1, keepdims=True) / total
    flow_x = jnp.sum(mass * lag, axis=1, keepdims=True) / total
    for c, value in enumerate((flow_y, flow_x)):
        spread = jnp.where(here, value, 0.0)
        for i in range(rows):
            flow_ref[c * rows + i:c * rows + i + 1, :] = jnp.sum(
                spread[i * cols:(i + 1) * cols], axis=0, keepdims=True
            )


def flow_of(region, rows, cols, group=4):
    left, right, back = tables()
    count = rows * cols
    return pl.pallas_call(
        functools.partial(flow_kernel, rows, cols, group),
        out_shape=jax.ShapeDtypeStruct((2 * rows, PATCH), jnp.float32),
        in_specs=[pl.BlockSpec(memory_space=pltpu.VMEM)] * 4,
        out_specs=pl.BlockSpec(memory_space=pltpu.VMEM),
        scratch_shapes=[
            pltpu.VMEM((2, region.shape[1], 2 * cols * STRIDE), jnp.bfloat16),
            pltpu.VMEM((2, region.shape[1], 2 * cols * STRIDE), jnp.bfloat16),
            pltpu.VMEM((2, count, FREQ, 2 * PATCH), jnp.float32),
            pltpu.VMEM((count, PATCH), jnp.float32),
            pltpu.VMEM((count, PATCH), jnp.float32),
            pltpu.VMEM((count, PATCH), jnp.float32),
        ],
        name="flow",
    )(region, left, right, back)


def shifted(value, axis, by):
    length = lax.axis_size(axis)
    pairs = [(i, i + by) for i in range(length) if 0 <= i + by < length]
    return lax.ppermute(value, axis, pairs)


def padded_2(value, sides, width):
    for axis, dim in sides:
        size, length = (lax.axis_size(axis), value.shape[dim])
        up = [(i, (i + 1) % size) for i in range(size - 1)]
        down = [(j, i) for i, j in up]
        last = lax.slice_in_dim(value, length - width, length, axis=dim)
        first = lax.slice_in_dim(value, 0, width, axis=dim)
        before = lax.ppermute(last, axis, up)
        after = lax.ppermute(first, axis, down)
        value = jnp.concatenate([before, value, after], axis=dim)
    return value


def lap_of(padded, center):
    return (
        padded[:, :-2, 1:-1]
        + padded[:, 2:, 1:-1]
        + padded[:, 1:-1, :-2]
        + padded[:, 1:-1, 2:]
        - 4.0 * center
    )


def whole_sections(images):
    tile = images[0]
    rows, cols = tile.shape[0] // STRIDE, tile.shape[1] // STRIDE
    region = padded_2(jnp.stack([tile, shifted(tile, "sec", -1)]), (("ty", 1), ("tx", 2)), HALF)
    flow = flow_of(region, rows, cols)[:, :cols].reshape(2, rows, cols)
    keep = (lax.axis_index("sec") < lax.axis_size("sec") - 1).astype(jnp.float32)
    flow = flow * keep
    padded = padded_2(flow, (("ty", 1), ("tx", 2)), 2)
    inner = padded[:, 1:-1, 1:-1]
    first = inner + rate * (stiffness * lap_of(padded, inner) + inner - inner)
    row_ids = lax.axis_index("ty") * rows + jnp.arange(-1, rows + 1, dtype=jnp.int32)
    col_ids = lax.axis_index("tx") * cols + jnp.arange(-1, cols + 1, dtype=jnp.int32)
    row_ok = (row_ids >= 0) & (row_ids < rows * lax.axis_size("ty"))
    col_ok = (col_ids >= 0) & (col_ids < cols * lax.axis_size("tx"))
    first = first * (row_ok[:, None] & col_ok[None, :]).astype(jnp.float32)[None]
    center = first[:, 1:-1, 1:-1]
    mesh = center + rate * (stiffness * lap_of(first, center) + flow - center)
    everything = lax.all_gather(mesh, "sec")
    earlier = jnp.arange(lax.axis_size("sec")) < lax.axis_index("sec")
    before = jnp.sum(jnp.where(earlier[:, None, None, None], everything, 0.0), axis=0)
    return (mesh[None], before[None])


AXES = ("sec", "ty", "tx")


def placed(half, y, x):
    ny, nx = lax.axis_size("ty"), lax.axis_size("tx")
    return (((half + x) % 2) * ny + y) * nx + x


def along(value, step):
    ny, nx = lax.axis_size("ty"), lax.axis_size("tx")
    pairs = []
    for y in range(ny):
        for g in range(2 * nx):
            to = step(g) % (2 * nx)
            pairs.append((placed(g % 2, y, g // 2), placed(to % 2, y, to // 2)))
    return lax.ppermute(value, AXES, pairs)


def ring(value, axis, by):
    size = lax.axis_size(axis)
    return lax.ppermute(value, axis, [(i, (i + by) % size) for i in range(size)])


def mate(g):
    return g ^ 1


def near(g):
    return g - 1 if g % 2 == 0 else g + 1


def far(g):
    return g - 2 if g % 2 == 0 else g + 2


def window_kernel(width, place_ref, own_ref, mate_ref, near_ref, far_ref, out_ref):
    half = place_ref[0] == 1
    own, other, close, beyond = own_ref[...], mate_ref[...], near_ref[...], far_ref[...]
    lane = lax.broadcasted_iota(jnp.int32, own.shape, 1)
    begin = jnp.where(half, beyond, close)
    left = jnp.where(half, other, own)
    right = jnp.where(half, own, other)
    end = jnp.where(half, close, beyond)
    begin = jnp.where(place_ref[2] == 0, 0.0, begin)
    end = jnp.where(place_ref[2] == place_ref[4] - 1, 0.0, end)
    begin = pltpu.roll(begin, PATCH + 2 - width, 1)
    left, right, end = pltpu.roll(left, 2, 1), pltpu.roll(right, 2 + width, 1), pltpu.roll(end, 2 + 2 * width, 1)
    value = jnp.where(lane < 2, begin, jnp.where(lane < 2 + width, left, right))
    value = jnp.where(lane < 2 + 2 * width, value, jnp.where(lane < 4 + 2 * width, end, 0.0))
    out_ref[...] = value


def relax_kernel(rows, cols, place_ref, own_ref, above_ref, below_ref, mesh_ref, earlier_ref):
    section, y, x = place_ref[1], place_ref[3], place_ref[2]
    tall = rows + 4
    shape = (tall, PATCH)
    row = lax.broadcasted_iota(jnp.int32, shape, 0) - 2 + y * rows
    col = lax.broadcasted_iota(jnp.int32, shape, 1) - 2 + x * cols
    inside = (row >= 0) & (row < place_ref[5] * rows) & (col >= 0) & (col < place_ref[4] * cols)

    def step(mesh, flow):
        around = (
            pltpu.roll(mesh, 1, 0) + pltpu.roll(mesh, tall - 1, 0)
            + pltpu.roll(mesh, 1, 1) + pltpu.roll(mesh, PATCH - 1, 1)
        )
        lap = around - 4.0 * mesh
        return jnp.where(inside, mesh + rate * (stiffness * lap + flow - mesh), 0.0)

    for c in range(2):
        flow = jnp.concatenate(
            [above_ref[(c + 1) * rows - 2:(c + 1) * rows], own_ref[c * rows:(c + 1) * rows],
             below_ref[c * rows:c * rows + 2]], axis=0)
        flow = jnp.where(inside, flow, 0.0)
        mesh = step(step(flow, flow), flow)
        mesh = pltpu.roll(pltpu.roll(mesh, tall - 2, 0), PATCH - 2, 1)[:rows, :cols]
        mesh_ref[0, c] = jnp.where(section == 0, mesh, 0.0)
        earlier_ref[0, c] = jnp.where(section == 0, 0.0, mesh)


def shared_section(images):
    tile = images[0]
    section, y, x = lax.axis_index("sec"), lax.axis_index("ty"), lax.axis_index("tx")
    ny, nx = lax.axis_size("ty"), lax.axis_size("tx")
    half = (section + x) % 2
    rows, cols = tile.shape[0] // STRIDE, tile.shape[1] // STRIDE
    width = cols // 2
    core = width * STRIDE + HALF
    skip = tile.shape[1] - core
    place = jnp.stack([half, section, x, y, nx * jnp.ones_like(x), ny * jnp.ones_like(x)]).astype(jnp.int32)

    own = lax.dynamic_slice_in_dim(tile, half * skip, core, 1)
    got = along(lax.dynamic_slice_in_dim(tile, (1 - half) * skip, core, 1), mate)
    pair = jnp.stack([jnp.where(section == 0, own, got), jnp.where(section == 0, got, own)])
    above = jnp.where(y > 0, ring(pair[:, -HALF:], "ty", 1), 0.0)
    below = jnp.where(y < ny - 1, ring(pair[:, :HALF], "ty", -1), 0.0)
    pair = jnp.concatenate([above, pair, below], axis=1)
    edge = along(jnp.where(half == 0, pair[:, :, :HALF], pair[:, :, -HALF:]), near)
    at_end = jnp.where(half == 0, x == 0, x == nx - 1)
    edge = jnp.where(at_end, 0.0, edge)
    region = jnp.where(
        half == 0, jnp.concatenate([edge, pair], axis=2), jnp.concatenate([pair, edge], axis=2)
    )
    flow = flow_of(region, rows, width)
    smem, vmem = pl.BlockSpec(memory_space=pltpu.SMEM), pl.BlockSpec(memory_space=pltpu.VMEM)
    window = pl.pallas_call(
        functools.partial(window_kernel, width),
        out_shape=jax.ShapeDtypeStruct(flow.shape, jnp.float32),
        in_specs=[smem] + [vmem] * 4,
        out_specs=vmem,
        name="window",
    )(place, flow, along(flow, mate), along(flow, near), along(flow, far))
    out = jax.ShapeDtypeStruct((1, 2, rows, cols), jnp.float32)
    return pl.pallas_call(
        functools.partial(relax_kernel, rows, cols),
        out_shape=(out, out),
        in_specs=[smem] + [vmem] * 3,
        out_specs=(vmem, vmem),
        name="relax",
    )(place, window, ring(window, "ty", 1), ring(window, "ty", -1))


def solution(mesh):
    in_specs = (P("sec", "ty", "tx"),)
    out_specs = (P("sec", None, "ty", "tx"), P("sec", None, "ty", "tx"))
    shared = mesh.shape["sec"] == 2
    return jax.shard_map(
        shared_section if shared else whole_sections,
        mesh=mesh, in_specs=in_specs, out_specs=out_specs, check_vma=False,
    )
```

```python
import functools

import jax
import jax.numpy as jnp
import numpy as np
from jax import lax
from jax.experimental import pallas as pl
from jax.experimental.pallas import tpu as pltpu
from jax.sharding import PartitionSpec as P

PATCH = 128
STRIDE = 64
HALF = STRIDE // 2
FREQ = -(-(PATCH // 2 + 1) // 8) * 8

stiffness = 1.0
rate = 0.25


def two_parts(table):
    high = table.astype(jnp.bfloat16)
    low = (table - high.astype(np.float64)).astype(jnp.bfloat16)
    return high, low


def tables():
    angle = 2.0 * np.pi * (np.outer(np.arange(PATCH), np.arange(PATCH)) % PATCH) / PATCH
    cosine, sine = np.cos(angle), np.sin(angle)
    kept = np.arange(FREQ)[:, None] <= PATCH // 2
    left = np.concatenate([cosine[:FREQ] * kept, -sine[:FREQ] * kept])
    right = np.block([[cosine, -sine], [sine, cosine]])
    share = np.where((np.arange(FREQ) == 0) | (np.arange(FREQ) == PATCH // 2), 1.0, 2.0)
    scaled = (share * kept[:, 0])[None, :] / float(PATCH) ** 3
    back = np.concatenate([cosine[:, :FREQ] * scaled, sine[:, :FREQ] * scaled], axis=1)
    left_hi, left_lo = two_parts(left)
    back_hi, back_lo = two_parts(back)
    right_hi, right_lo = two_parts(right)
    return (
        np.concatenate([left_hi, left_hi, left_lo], axis=1),
        np.stack([right_hi, right_lo]),
        np.concatenate([back_hi, back_hi, back_lo], axis=1),
    )


def split(values):
    high = values.astype(jnp.bfloat16)
    return high, (values - high.astype(jnp.float32)).astype(jnp.bfloat16)


def mul(a, b):
    return jnp.dot(a, b, preferred_element_type=jnp.float32)


def right_dft(values, right_ref):
    high, low = split(values)
    return mul(high, right_ref[0]) + mul(low, right_ref[0]) + mul(high, right_ref[1])


def keep_region(region, z, wide, high_ref, low_ref):
    even, odd = region[:, :wide], region[:, STRIDE:STRIDE + wide]
    for part, values in enumerate((even, odd)):
        high, low = split(values)
        high_ref[z, :, part * wide:(part + 1) * wide] = high
        low_ref[z, :, part * wide:(part + 1) * wide] = low


def flow_kernel(rows, cols, group, region_ref, left_ref, right_ref, back_ref, flow_ref,
                high_ref, low_ref, *scratch):
    for z in range(2):
        keep_region(region_ref[z], z, cols * STRIDE, high_ref, low_ref)
    correlate(rows, cols, group, left_ref, right_ref, back_ref, flow_ref, high_ref, low_ref, *scratch)


def correlate(rows, cols, group, left_ref, right_ref, back_ref, flow_ref,
              high_ref, low_ref, half_ref, peak_ref, mass_ref, tilt_ref):
    order = [2 * t for t in range(cols // 2)] + [2 * t + 1 for t in range(cols // 2)]
    for z in range(2):
        for i in range(rows):
            band = pl.ds(i * STRIDE, PATCH)
            high = high_ref[z, band, :]
            stacked = jnp.concatenate([high, low_ref[z, band, :], high], axis=0)
            out = mul(left_ref[...], stacked)
            for t, j in enumerate(order):
                lanes = slice(t * PATCH, (t + 1) * PATCH)
                half_ref[z, i * cols + j, :, :PATCH] = out[:FREQ, lanes]
                half_ref[z, i * cols + j, :, PATCH:] = out[FREQ:, lanes]
    row = lax.broadcasted_iota(jnp.int32, (group, FREQ, PATCH), 1)
    lane = lax.broadcasted_iota(jnp.int32, (group, FREQ, PATCH), 2)
    varies = ((row + lane) > 0).astype(jnp.float32).reshape(group * FREQ, PATCH)
    lag = lax.broadcasted_iota(jnp.int32, (PATCH, 1), 0)
    lag = jnp.where(lag < PATCH // 2, lag, lag - PATCH).astype(jnp.float32)
    for n in range(0, rows * cols, group):
        both = half_ref[:, n:n + group].reshape(2 * group * FREQ, 2 * PATCH)
        freq = right_dft(both, right_ref)
        first, second = freq[:group * FREQ], freq[group * FREQ:]
        re1, im1 = first[:, :PATCH] * varies, first[:, PATCH:] * varies
        re2, im2 = second[:, :PATCH] * varies, second[:, PATCH:] * varies
        cross = jnp.concatenate([re1 * re2 + im1 * im2, im1 * re2 - re1 * im2], axis=1)
        mixed = right_dft(cross, right_ref)
        columns = []
        for m in range(group):
            part = mixed[m * FREQ:(m + 1) * FREQ]
            columns.append(jnp.concatenate([part[:, :PATCH], part[:, PATCH:]], axis=0))
        high, low = split(jnp.concatenate(columns, axis=1))
        scores = mul(back_ref[...], jnp.concatenate([high, low, high], axis=0))
        peak = jnp.max(scores, axis=0, keepdims=True)
        weight = jnp.exp(scores - peak)
        mass = jnp.sum(weight, axis=0, keepdims=True)
        tilt = jnp.sum(weight * lag, axis=0, keepdims=True)
        for m in range(group):
            lanes = slice(m * PATCH, (m + 1) * PATCH)
            peak_ref[n + m:n + m + 1, :] = peak[:, lanes]
            mass_ref[n + m:n + m + 1, :] = mass[:, lanes]
            tilt_ref[n + m:n + m + 1, :] = tilt[:, lanes]
    peak = peak_ref[...]
    share = jnp.exp(peak - jnp.max(peak, axis=1, keepdims=True))
    mass = mass_ref[...] * share
    lag = lax.broadcasted_iota(jnp.int32, mass.shape, 1)
    place = lax.broadcasted_iota(jnp.int32, mass.shape, 0) % cols
    here = lag == place
    lag = jnp.where(lag < PATCH // 2, lag, lag - PATCH).astype(jnp.float32)
    total = jnp.sum(mass, axis=1, keepdims=True)
    flow_y = jnp.sum(tilt_ref[...] * share, axis=1, keepdims=True) / total
    flow_x = jnp.sum(mass * lag, axis=1, keepdims=True) / total
    for c, value in enumerate((flow_y, flow_x)):
        spread = jnp.where(here, value, 0.0)
        for i in range(rows):
            flow_ref[c * rows + i:c * rows + i + 1, :] = jnp.sum(
                spread[i * cols:(i + 1) * cols], axis=0, keepdims=True
            )


def flow_scratch(rows, cols):
    tall, count = (rows + 1) * STRIDE, rows * cols
    return [
        pltpu.VMEM((2, tall, 2 * cols * STRIDE), jnp.bfloat16),
        pltpu.VMEM((2, tall, 2 * cols * STRIDE), jnp.bfloat16),
        pltpu.VMEM((2, count, FREQ, 2 * PATCH), jnp.float32),
        pltpu.VMEM((count, PATCH), jnp.float32),
        pltpu.VMEM((count, PATCH), jnp.float32),
        pltpu.VMEM((count, PATCH), jnp.float32),
    ]


IN_VMEM = pl.BlockSpec(memory_space=pltpu.VMEM)


def kernel_call(body, outs, *args, scratch=(), name=None):
    return pl.pallas_call(
        body,
        out_shape=outs,
        in_specs=[IN_VMEM] * len(args),
        out_specs=jax.tree.map(lambda _: IN_VMEM, outs),
        scratch_shapes=scratch,
        name=name,
    )(*args)


def floats(*shape):
    return jax.ShapeDtypeStruct(shape, jnp.float32)


def flow_of(region, rows, cols, group=4):
    return kernel_call(
        functools.partial(flow_kernel, rows, cols, group),
        floats(2 * rows, PATCH), region, *tables(),
        scratch=flow_scratch(rows, cols), name="flow",
    )


def shifted(value, axis, by):
    length = lax.axis_size(axis)
    pairs = [(i, i + by) for i in range(length) if 0 <= i + by < length]
    return lax.ppermute(value, axis, pairs)


def padded_2(value, sides, width):
    for axis, dim in sides:
        size, length = (lax.axis_size(axis), value.shape[dim])
        up = [(i, (i + 1) % size) for i in range(size - 1)]
        down = [(j, i) for i, j in up]
        last = lax.slice_in_dim(value, length - width, length, axis=dim)
        first = lax.slice_in_dim(value, 0, width, axis=dim)
        before = lax.ppermute(last, axis, up)
        after = lax.ppermute(first, axis, down)
        value = jnp.concatenate([before, value, after], axis=dim)
    return value


def lap_of(padded, center):
    return (
        padded[:, :-2, 1:-1]
        + padded[:, 2:, 1:-1]
        + padded[:, 1:-1, :-2]
        + padded[:, 1:-1, 2:]
        - 4.0 * center
    )


def whole_sections(images):
    tile = images[0]
    rows, cols = tile.shape[0] // STRIDE, tile.shape[1] // STRIDE
    region = padded_2(jnp.stack([tile, shifted(tile, "sec", -1)]), (("ty", 1), ("tx", 2)), HALF)
    flow = flow_of(region, rows, cols)[:, :cols].reshape(2, rows, cols)
    keep = (lax.axis_index("sec") < lax.axis_size("sec") - 1).astype(jnp.float32)
    flow = flow * keep
    padded = padded_2(flow, (("ty", 1), ("tx", 2)), 2)
    inner = padded[:, 1:-1, 1:-1]
    first = inner + rate * (stiffness * lap_of(padded, inner) + inner - inner)
    row_ids = lax.axis_index("ty") * rows + jnp.arange(-1, rows + 1, dtype=jnp.int32)
    col_ids = lax.axis_index("tx") * cols + jnp.arange(-1, cols + 1, dtype=jnp.int32)
    row_ok = (row_ids >= 0) & (row_ids < rows * lax.axis_size("ty"))
    col_ok = (col_ids >= 0) & (col_ids < cols * lax.axis_size("tx"))
    first = first * (row_ok[:, None] & col_ok[None, :]).astype(jnp.float32)[None]
    center = first[:, 1:-1, 1:-1]
    mesh = center + rate * (stiffness * lap_of(first, center) + flow - center)
    everything = lax.all_gather(mesh, "sec")
    earlier = jnp.arange(lax.axis_size("sec")) < lax.axis_index("sec")
    before = jnp.sum(jnp.where(earlier[:, None, None, None], everything, 0.0), axis=0)
    return (mesh[None], before[None])


AXES = ("sec", "ty", "tx")


def placed(half, y, x):
    ny, nx = lax.axis_size("ty"), lax.axis_size("tx")
    return (((half + x) % 2) * ny + y) * nx + x


def along(value, step):
    ny, nx = lax.axis_size("ty"), lax.axis_size("tx")
    pairs = []
    for y in range(ny):
        for g in range(2 * nx):
            to = step(g) % (2 * nx)
            pairs.append((placed(g % 2, y, g // 2), placed(to % 2, y, to // 2)))
    return lax.ppermute(value, AXES, pairs)


def ring(value, axis, by):
    size = lax.axis_size(axis)
    return lax.ppermute(value, axis, [(i, (i + by) % size) for i in range(size)])


def mate(g):
    return g ^ 1


def near(g):
    return g - 1 if g % 2 == 0 else g + 1


def far(g):
    return g - 2 if g % 2 == 0 else g + 2


def past(g):
    return g + 2 if g % 2 == 0 else g - 2


def where_am_i():
    section, y, x = lax.axis_index("sec"), lax.axis_index("ty"), lax.axis_index("tx")
    return section, y, x, (section + x) % 2


def cut_kernel(core, tile_ref, out_ref):
    _, _, _, half = where_am_i()
    width = tile_ref.shape[1]

    @pl.when(half == 0)
    def _():
        out_ref[...] = tile_ref[:, width - core:]

    @pl.when(half == 1)
    def _():
        out_ref[...] = tile_ref[:, :core]


def strips_kernel(tile_ref, first_ref, last_ref):
    first_ref[...] = tile_ref[:HALF]
    last_ref[...] = tile_ref[tile_ref.shape[0] - HALF:]


def packed(column):
    quarter = column.shape[0] // 4
    return jnp.concatenate([column[q * quarter:(q + 1) * quarter] for q in range(4)], axis=1)


def unpacked(block):
    return jnp.concatenate([block[:, q * HALF:(q + 1) * HALF] for q in range(4)], axis=0)


def borders_kernel(core, ny, tile_ref, above_ref, below_ref, strips_ref, near_ref, past_ref):
    _, y, _, half = where_am_i()
    width = tile_ref.shape[1]
    above = jnp.where(y == 0, 0.0, above_ref[...])
    below = jnp.where(y == ny - 1, 0.0, below_ref[...])

    def column(lanes):
        return packed(jnp.concatenate([above[:, lanes], tile_ref[:, lanes], below[:, lanes]], axis=0))

    start, end = slice(0, HALF), slice(width - HALF, width)
    first, last = column(start), column(end)

    @pl.when(half == 0)
    def _():
        strips_ref[:HALF], strips_ref[HALF:] = above[:, width - core:], below[:, width - core:]
        near_ref[...], past_ref[...] = first, last

    @pl.when(half == 1)
    def _():
        strips_ref[:HALF], strips_ref[HALF:] = above[:, :core], below[:, :core]
        near_ref[...], past_ref[...] = last, first


def shared_kernel(rows, cols, group, ny, nx, tile_ref, above_ref, below_ref, side_ref,
                  other_ref, strips_ref, other_side_ref, left_ref, right_ref, back_ref, flow_ref,
                  high_ref, low_ref, *scratch):
    section, y, x, half = where_am_i()
    core, width = other_ref.shape[1], tile_ref.shape[1]
    wide = cols * STRIDE
    at_end = jnp.where(half == 0, x == 0, x == nx - 1)
    own_side = jnp.where(at_end, 0.0, unpacked(side_ref[...]))
    other_side = jnp.where(at_end, 0.0, unpacked(other_side_ref[...]))
    above = jnp.where(y == 0, 0.0, above_ref[...])
    below = jnp.where(y == ny - 1, 0.0, below_ref[...])
    other = jnp.concatenate([strips_ref[:HALF], other_ref[...], strips_ref[HALF:]], axis=0)

    @pl.when(half == 0)
    def _():
        own = jnp.concatenate([above[:, :core], tile_ref[:, :core], below[:, :core]], axis=0)
        keep_region(jnp.concatenate([own_side, own], axis=1), section, wide, high_ref, low_ref)
        keep_region(jnp.concatenate([other_side, other], axis=1), 1 - section, wide, high_ref, low_ref)

    @pl.when(half == 1)
    def _():
        lanes = slice(width - core, width)
        own = jnp.concatenate([above[:, lanes], tile_ref[:, lanes], below[:, lanes]], axis=0)
        keep_region(jnp.concatenate([own, own_side], axis=1), section, wide, high_ref, low_ref)
        keep_region(jnp.concatenate([other, other_side], axis=1), 1 - section, wide, high_ref, low_ref)

    correlate(rows, cols, group, left_ref, right_ref, back_ref, flow_ref, high_ref, low_ref, *scratch)


def window_kernel(width, nx, own_ref, mate_ref, near_ref, far_ref, out_ref):
    _, _, x, place = where_am_i()
    half = place == 1
    own, other, close, beyond = own_ref[...], mate_ref[...], near_ref[...], far_ref[...]
    lane = lax.broadcasted_iota(jnp.int32, own.shape, 1)
    begin = jnp.where(x == 0, 0.0, jnp.where(half, beyond, close))
    left = jnp.where(half, other, own)
    right = jnp.where(half, own, other)
    end = jnp.where(x == nx - 1, 0.0, jnp.where(half, close, beyond))
    begin, left = pltpu.roll(begin, PATCH + 2 - width, 1), pltpu.roll(left, 2, 1)
    right, end = pltpu.roll(right, 2 + width, 1), pltpu.roll(end, 2 + 2 * width, 1)
    value = jnp.where(lane < 2, begin, jnp.where(lane < 2 + width, left, right))
    value = jnp.where(lane < 2 + 2 * width, value, jnp.where(lane < 4 + 2 * width, end, 0.0))
    out_ref[...] = value


def relax_kernel(rows, cols, ny, nx, own_ref, above_ref, below_ref, mesh_ref, earlier_ref):
    section, y, x, _ = where_am_i()
    tall = rows + 4
    shape = (tall, PATCH)
    row = lax.broadcasted_iota(jnp.int32, shape, 0) - 2 + y * rows
    col = lax.broadcasted_iota(jnp.int32, shape, 1) - 2 + x * cols
    inside = (row >= 0) & (row < ny * rows) & (col >= 0) & (col < nx * cols)

    def step(mesh, flow):
        around = (
            pltpu.roll(mesh, 1, 0) + pltpu.roll(mesh, tall - 1, 0)
            + pltpu.roll(mesh, 1, 1) + pltpu.roll(mesh, PATCH - 1, 1)
        )
        lap = around - 4.0 * mesh
        return jnp.where(inside, mesh + rate * (stiffness * lap + flow - mesh), 0.0)

    for c in range(2):
        flow = jnp.concatenate(
            [above_ref[(c + 1) * rows - 2:(c + 1) * rows], own_ref[c * rows:(c + 1) * rows],
             below_ref[c * rows:c * rows + 2]], axis=0)
        flow = jnp.where(inside, flow, 0.0)
        mesh = step(step(flow, flow), flow)
        mesh = pltpu.roll(pltpu.roll(mesh, tall - 2, 0), PATCH - 2, 1)[:rows, :cols]
        mesh_ref[0, c] = jnp.where(section == 0, mesh, 0.0)
        earlier_ref[0, c] = jnp.where(section == 0, 0.0, mesh)


def shared_section(images):
    tile = images[0]
    ny, nx = lax.axis_size("ty"), lax.axis_size("tx")
    rows, cols = tile.shape[0] // STRIDE, tile.shape[1] // STRIDE
    half = cols // 2
    core = half * STRIDE + HALF
    tall = tile.shape[0] + 2 * HALF

    payload = kernel_call(functools.partial(cut_kernel, core), floats(tile.shape[0], core), tile, name="cut")
    other = along(payload, mate)
    strip = floats(HALF, tile.shape[1])
    first, last = kernel_call(strips_kernel, (strip, strip), tile, name="strips")
    above, below = ring(last, "ty", 1), ring(first, "ty", -1)
    edge = floats(tall // 4, 4 * HALF)
    strips, edge_near, edge_past = kernel_call(
        functools.partial(borders_kernel, core, ny), (floats(2 * HALF, core), edge, edge),
        tile, above, below, name="borders",
    )
    strips, side, other_side = along(strips, mate), along(edge_near, near), along(edge_past, past)
    flow = kernel_call(
        functools.partial(shared_kernel, rows, half, 4, ny, nx), floats(2 * rows, PATCH),
        tile, above, below, side, other, strips, other_side, *tables(),
        scratch=flow_scratch(rows, half), name="flow",
    )
    window = kernel_call(
        functools.partial(window_kernel, half, nx), floats(*flow.shape),
        flow, along(flow, mate), along(flow, near), along(flow, far), name="window",
    )
    out = floats(1, 2, rows, cols)
    return kernel_call(
        functools.partial(relax_kernel, rows, cols, ny, nx), (out, out),
        window, ring(window, "ty", 1), ring(window, "ty", -1), name="relax",
    )


def solution(mesh):
    in_specs = (P("sec", "ty", "tx"),)
    out_specs = (P("sec", None, "ty", "tx"), P("sec", None, "ty", "tx"))
    shared = mesh.shape["sec"] == 2
    return jax.shard_map(
        shared_section if shared else whole_sections,
        mesh=mesh, in_specs=in_specs, out_specs=out_specs, check_vma=False,
    )
```

```python
import functools

import jax
import jax.numpy as jnp
import numpy as np
from jax import lax
from jax.experimental import pallas as pl
from jax.experimental.pallas import tpu as pltpu
from jax.sharding import PartitionSpec as P

PATCH = 128
STRIDE = 64
HALF = STRIDE // 2
FREQ = -(-(PATCH // 2 + 1) // 8) * 8

stiffness = 1.0
rate = 0.25


def two_parts(table):
    high = table.astype(jnp.bfloat16)
    low = (table - high.astype(np.float64)).astype(jnp.bfloat16)
    return high, low


def tables():
    angle = 2.0 * np.pi * (np.outer(np.arange(PATCH), np.arange(PATCH)) % PATCH) / PATCH
    cosine, sine = np.cos(angle), np.sin(angle)
    kept = np.arange(FREQ)[:, None] <= PATCH // 2
    left = np.concatenate([cosine[:FREQ] * kept, -sine[:FREQ] * kept])
    right = np.block([[cosine, -sine], [sine, cosine]])
    share = np.where((np.arange(FREQ) == 0) | (np.arange(FREQ) == PATCH // 2), 1.0, 2.0)
    scaled = (share * kept[:, 0])[None, :] / float(PATCH) ** 3
    back = np.concatenate([cosine[:, :FREQ] * scaled, sine[:, :FREQ] * scaled], axis=1)
    left_hi, left_lo = two_parts(left)
    back_hi, back_lo = two_parts(back)
    right_hi, right_lo = two_parts(right)
    return (
        np.concatenate([left_hi, left_hi, left_lo], axis=1),
        np.stack([right_hi, right_lo]),
        np.concatenate([back_hi, back_hi, back_lo], axis=1),
    )


def split(values):
    high = values.astype(jnp.bfloat16)
    return high, (values - high.astype(jnp.float32)).astype(jnp.bfloat16)


def mul(a, b):
    return jnp.dot(a, b, preferred_element_type=jnp.float32)


def right_dft(values, right_ref):
    high, low = split(values)
    return mul(high, right_ref[0]) + mul(low, right_ref[0]) + mul(high, right_ref[1])


def keep_region(region, z, wide, high_ref, low_ref):
    even, odd = region[:, :wide], region[:, STRIDE:STRIDE + wide]
    for part, values in enumerate((even, odd)):
        high, low = split(values)
        high_ref[z, :, part * wide:(part + 1) * wide] = high
        low_ref[z, :, part * wide:(part + 1) * wide] = low


def flow_kernel(rows, cols, group, region_ref, left_ref, right_ref, back_ref, flow_ref,
                high_ref, low_ref, *scratch):
    for z in range(2):
        keep_region(region_ref[z], z, cols * STRIDE, high_ref, low_ref)
    correlate(rows, cols, group, left_ref, right_ref, back_ref, flow_ref, high_ref, low_ref, *scratch)


def correlate(rows, cols, group, left_ref, right_ref, back_ref, flow_ref,
              high_ref, low_ref, half_ref, peak_ref, mass_ref, tilt_ref):
    order = [2 * t for t in range(cols // 2)] + [2 * t + 1 for t in range(cols // 2)]
    for z in range(2):
        for i in range(rows):
            band = pl.ds(i * STRIDE, PATCH)
            high = high_ref[z, band, :]
            stacked = jnp.concatenate([high, low_ref[z, band, :], high], axis=0)
            out = mul(left_ref[...], stacked)
            for t, j in enumerate(order):
                lanes = slice(t * PATCH, (t + 1) * PATCH)
                half_ref[z, i * cols + j, :, :PATCH] = out[:FREQ, lanes]
                half_ref[z, i * cols + j, :, PATCH:] = out[FREQ:, lanes]
    row = lax.broadcasted_iota(jnp.int32, (group, FREQ, PATCH), 1)
    lane = lax.broadcasted_iota(jnp.int32, (group, FREQ, PATCH), 2)
    varies = ((row + lane) > 0).astype(jnp.float32).reshape(group * FREQ, PATCH)
    lag = lax.broadcasted_iota(jnp.int32, (PATCH, 1), 0)
    lag = jnp.where(lag < PATCH // 2, lag, lag - PATCH).astype(jnp.float32)
    for n in range(0, rows * cols, group):
        both = half_ref[:, n:n + group].reshape(2 * group * FREQ, 2 * PATCH)
        freq = right_dft(both, right_ref)
        first, second = freq[:group * FREQ], freq[group * FREQ:]
        re1, im1 = first[:, :PATCH] * varies, first[:, PATCH:] * varies
        re2, im2 = second[:, :PATCH] * varies, second[:, PATCH:] * varies
        cross = jnp.concatenate([re1 * re2 + im1 * im2, im1 * re2 - re1 * im2], axis=1)
        mixed = right_dft(cross, right_ref)
        columns = []
        for m in range(group):
            part = mixed[m * FREQ:(m + 1) * FREQ]
            columns.append(jnp.concatenate([part[:, :PATCH], part[:, PATCH:]], axis=0))
        high, low = split(jnp.concatenate(columns, axis=1))
        scores = mul(back_ref[...], jnp.concatenate([high, low, high], axis=0))
        peak = jnp.max(scores, axis=0, keepdims=True)
        weight = jnp.exp(scores - peak)
        mass = jnp.sum(weight, axis=0, keepdims=True)
        tilt = jnp.sum(weight * lag, axis=0, keepdims=True)
        for m in range(group):
            lanes = slice(m * PATCH, (m + 1) * PATCH)
            peak_ref[n + m:n + m + 1, :] = peak[:, lanes]
            mass_ref[n + m:n + m + 1, :] = mass[:, lanes]
            tilt_ref[n + m:n + m + 1, :] = tilt[:, lanes]
    peak = peak_ref[...]
    share = jnp.exp(peak - jnp.max(peak, axis=1, keepdims=True))
    mass = mass_ref[...] * share
    lag = lax.broadcasted_iota(jnp.int32, mass.shape, 1)
    place = lax.broadcasted_iota(jnp.int32, mass.shape, 0) % cols
    here = lag == place
    lag = jnp.where(lag < PATCH // 2, lag, lag - PATCH).astype(jnp.float32)
    total = jnp.sum(mass, axis=1, keepdims=True)
    flow_y = jnp.sum(tilt_ref[...] * share, axis=1, keepdims=True) / total
    flow_x = jnp.sum(mass * lag, axis=1, keepdims=True) / total
    for c, value in enumerate((flow_y, flow_x)):
        spread = jnp.where(here, value, 0.0)
        for i in range(rows):
            flow_ref[c * rows + i:c * rows + i + 1, :] = jnp.sum(
                spread[i * cols:(i + 1) * cols], axis=0, keepdims=True
            )


def flow_scratch(rows, cols):
    tall, count = (rows + 1) * STRIDE, rows * cols
    return [
        pltpu.VMEM((2, tall, 2 * cols * STRIDE), jnp.bfloat16),
        pltpu.VMEM((2, tall, 2 * cols * STRIDE), jnp.bfloat16),
        pltpu.VMEM((2, count, FREQ, 2 * PATCH), jnp.float32),
        pltpu.VMEM((count, PATCH), jnp.float32),
        pltpu.VMEM((count, PATCH), jnp.float32),
        pltpu.VMEM((count, PATCH), jnp.float32),
    ]


IN_VMEM = pl.BlockSpec(memory_space=pltpu.VMEM)


def kernel_call(body, outs, *args, scratch=(), name=None, last=False):
    args = [pltpu.with_memory_space_constraint(a, pltpu.VMEM) if isinstance(a, jax.Array) else a for a in args]
    shapes = outs if last else jax.tree.map(lambda out: pltpu.VMEM(out.shape, out.dtype), outs)
    return pl.pallas_call(
        body,
        out_shape=shapes,
        in_specs=[IN_VMEM] * len(args),
        out_specs=jax.tree.map(lambda _: IN_VMEM, outs),
        scratch_shapes=scratch,
        compiler_params=pltpu.CompilerParams(vmem_limit_bytes=24 << 20),
        name=name,
    )(*args)


def floats(*shape):
    return jax.ShapeDtypeStruct(shape, jnp.float32)


def flow_of(region, rows, cols, group=4):
    return kernel_call(
        functools.partial(flow_kernel, rows, cols, group),
        floats(2 * rows, PATCH), region, *tables(),
        scratch=flow_scratch(rows, cols), name="flow",
    )


def shifted(value, axis, by):
    length = lax.axis_size(axis)
    pairs = [(i, i + by) for i in range(length) if 0 <= i + by < length]
    return lax.ppermute(value, axis, pairs)


def padded_2(value, sides, width):
    for axis, dim in sides:
        size, length = (lax.axis_size(axis), value.shape[dim])
        up = [(i, (i + 1) % size) for i in range(size - 1)]
        down = [(j, i) for i, j in up]
        last = lax.slice_in_dim(value, length - width, length, axis=dim)
        first = lax.slice_in_dim(value, 0, width, axis=dim)
        before = lax.ppermute(last, axis, up)
        after = lax.ppermute(first, axis, down)
        value = jnp.concatenate([before, value, after], axis=dim)
    return value


def lap_of(padded, center):
    return (
        padded[:, :-2, 1:-1]
        + padded[:, 2:, 1:-1]
        + padded[:, 1:-1, :-2]
        + padded[:, 1:-1, 2:]
        - 4.0 * center
    )


def whole_sections(images):
    tile = images[0]
    rows, cols = tile.shape[0] // STRIDE, tile.shape[1] // STRIDE
    region = padded_2(jnp.stack([tile, shifted(tile, "sec", -1)]), (("ty", 1), ("tx", 2)), HALF)
    flow = flow_of(region, rows, cols)[:, :cols].reshape(2, rows, cols)
    keep = (lax.axis_index("sec") < lax.axis_size("sec") - 1).astype(jnp.float32)
    flow = flow * keep
    padded = padded_2(flow, (("ty", 1), ("tx", 2)), 2)
    inner = padded[:, 1:-1, 1:-1]
    first = inner + rate * (stiffness * lap_of(padded, inner) + inner - inner)
    row_ids = lax.axis_index("ty") * rows + jnp.arange(-1, rows + 1, dtype=jnp.int32)
    col_ids = lax.axis_index("tx") * cols + jnp.arange(-1, cols + 1, dtype=jnp.int32)
    row_ok = (row_ids >= 0) & (row_ids < rows * lax.axis_size("ty"))
    col_ok = (col_ids >= 0) & (col_ids < cols * lax.axis_size("tx"))
    first = first * (row_ok[:, None] & col_ok[None, :]).astype(jnp.float32)[None]
    center = first[:, 1:-1, 1:-1]
    mesh = center + rate * (stiffness * lap_of(first, center) + flow - center)
    everything = lax.all_gather(mesh, "sec")
    earlier = jnp.arange(lax.axis_size("sec")) < lax.axis_index("sec")
    before = jnp.sum(jnp.where(earlier[:, None, None, None], everything, 0.0), axis=0)
    return (mesh[None], before[None])


AXES = ("sec", "ty", "tx")


def placed(half, y, x):
    ny, nx = lax.axis_size("ty"), lax.axis_size("tx")
    return (((half + x) % 2) * ny + y) * nx + x


def along(value, step):
    ny, nx = lax.axis_size("ty"), lax.axis_size("tx")
    pairs = []
    for y in range(ny):
        for g in range(2 * nx):
            to = step(g) % (2 * nx)
            pairs.append((placed(g % 2, y, g // 2), placed(to % 2, y, to // 2)))
    return lax.ppermute(value, AXES, pairs)


def ring(value, axis, by):
    size = lax.axis_size(axis)
    return lax.ppermute(value, axis, [(i, (i + by) % size) for i in range(size)])


def mate(g):
    return g ^ 1


def near(g):
    return g - 1 if g % 2 == 0 else g + 1


def far(g):
    return g - 2 if g % 2 == 0 else g + 2


def past(g):
    return g + 2 if g % 2 == 0 else g - 2


def where_am_i():
    section, y, x = lax.axis_index("sec"), lax.axis_index("ty"), lax.axis_index("tx")
    return section, y, x, (section + x) % 2


def cut_kernel(core, tile_ref, out_ref):
    _, _, _, half = where_am_i()
    width = tile_ref.shape[1]

    @pl.when(half == 0)
    def _():
        out_ref[...] = tile_ref[:, width - core:]

    @pl.when(half == 1)
    def _():
        out_ref[...] = tile_ref[:, :core]


def strips_kernel(tile_ref, first_ref, last_ref):
    first_ref[...] = tile_ref[:HALF]
    last_ref[...] = tile_ref[tile_ref.shape[0] - HALF:]


def packed(column):
    quarter = column.shape[0] // 4
    return jnp.concatenate([column[q * quarter:(q + 1) * quarter] for q in range(4)], axis=1)


def unpacked(block):
    return jnp.concatenate([block[:, q * HALF:(q + 1) * HALF] for q in range(4)], axis=0)


def borders_kernel(core, ny, tile_ref, above_ref, below_ref, strips_ref, near_ref, past_ref):
    _, y, _, half = where_am_i()
    width = tile_ref.shape[1]
    above = jnp.where(y == 0, 0.0, above_ref[...])
    below = jnp.where(y == ny - 1, 0.0, below_ref[...])

    def column(lanes):
        return packed(jnp.concatenate([above[:, lanes], tile_ref[:, lanes], below[:, lanes]], axis=0))

    start, end = slice(0, HALF), slice(width - HALF, width)
    first, last = column(start), column(end)

    @pl.when(half == 0)
    def _():
        strips_ref[:HALF], strips_ref[HALF:] = above[:, width - core:], below[:, width - core:]
        near_ref[...], past_ref[...] = first, last

    @pl.when(half == 1)
    def _():
        strips_ref[:HALF], strips_ref[HALF:] = above[:, :core], below[:, :core]
        near_ref[...], past_ref[...] = last, first


def shared_kernel(rows, cols, group, ny, nx, tile_ref, above_ref, below_ref, side_ref,
                  other_ref, strips_ref, other_side_ref, left_ref, right_ref, back_ref, flow_ref,
                  high_ref, low_ref, *scratch):
    section, y, x, half = where_am_i()
    core, width = other_ref.shape[1], tile_ref.shape[1]
    wide = cols * STRIDE
    at_end = jnp.where(half == 0, x == 0, x == nx - 1)
    own_side = jnp.where(at_end, 0.0, unpacked(side_ref[...]))
    other_side = jnp.where(at_end, 0.0, unpacked(other_side_ref[...]))
    above = jnp.where(y == 0, 0.0, above_ref[...])
    below = jnp.where(y == ny - 1, 0.0, below_ref[...])
    other = jnp.concatenate([strips_ref[:HALF], other_ref[...], strips_ref[HALF:]], axis=0)

    @pl.when(half == 0)
    def _():
        own = jnp.concatenate([above[:, :core], tile_ref[:, :core], below[:, :core]], axis=0)
        keep_region(jnp.concatenate([own_side, own], axis=1), section, wide, high_ref, low_ref)
        keep_region(jnp.concatenate([other_side, other], axis=1), 1 - section, wide, high_ref, low_ref)

    @pl.when(half == 1)
    def _():
        lanes = slice(width - core, width)
        own = jnp.concatenate([above[:, lanes], tile_ref[:, lanes], below[:, lanes]], axis=0)
        keep_region(jnp.concatenate([own, own_side], axis=1), section, wide, high_ref, low_ref)
        keep_region(jnp.concatenate([other, other_side], axis=1), 1 - section, wide, high_ref, low_ref)

    correlate(rows, cols, group, left_ref, right_ref, back_ref, flow_ref, high_ref, low_ref, *scratch)


def window_kernel(width, nx, own_ref, mate_ref, near_ref, far_ref, out_ref):
    _, _, x, place = where_am_i()
    half = place == 1
    own, other, close, beyond = own_ref[...], mate_ref[...], near_ref[...], far_ref[...]
    lane = lax.broadcasted_iota(jnp.int32, own.shape, 1)
    begin = jnp.where(x == 0, 0.0, jnp.where(half, beyond, close))
    left = jnp.where(half, other, own)
    right = jnp.where(half, own, other)
    end = jnp.where(x == nx - 1, 0.0, jnp.where(half, close, beyond))
    begin, left = pltpu.roll(begin, PATCH + 2 - width, 1), pltpu.roll(left, 2, 1)
    right, end = pltpu.roll(right, 2 + width, 1), pltpu.roll(end, 2 + 2 * width, 1)
    value = jnp.where(lane < 2, begin, jnp.where(lane < 2 + width, left, right))
    value = jnp.where(lane < 2 + 2 * width, value, jnp.where(lane < 4 + 2 * width, end, 0.0))
    out_ref[...] = value


def relax_kernel(rows, cols, ny, nx, own_ref, above_ref, below_ref, mesh_ref, earlier_ref):
    section, y, x, _ = where_am_i()
    tall = rows + 4
    shape = (tall, PATCH)
    row = lax.broadcasted_iota(jnp.int32, shape, 0) - 2 + y * rows
    col = lax.broadcasted_iota(jnp.int32, shape, 1) - 2 + x * cols
    inside = (row >= 0) & (row < ny * rows) & (col >= 0) & (col < nx * cols)

    def step(mesh, flow):
        around = (
            pltpu.roll(mesh, 1, 0) + pltpu.roll(mesh, tall - 1, 0)
            + pltpu.roll(mesh, 1, 1) + pltpu.roll(mesh, PATCH - 1, 1)
        )
        lap = around - 4.0 * mesh
        return jnp.where(inside, mesh + rate * (stiffness * lap + flow - mesh), 0.0)

    for c in range(2):
        flow = jnp.concatenate(
            [above_ref[(c + 1) * rows - 2:(c + 1) * rows], own_ref[c * rows:(c + 1) * rows],
             below_ref[c * rows:c * rows + 2]], axis=0)
        flow = jnp.where(inside, flow, 0.0)
        mesh = step(step(flow, flow), flow)
        mesh = pltpu.roll(pltpu.roll(mesh, tall - 2, 0), PATCH - 2, 1)[:rows, :cols]
        mesh_ref[0, c] = jnp.where(section == 0, mesh, 0.0)
        earlier_ref[0, c] = jnp.where(section == 0, 0.0, mesh)


def shared_section(images):
    tile = images[0]
    ny, nx = lax.axis_size("ty"), lax.axis_size("tx")
    rows, cols = tile.shape[0] // STRIDE, tile.shape[1] // STRIDE
    half = cols // 2
    core = half * STRIDE + HALF
    tall = tile.shape[0] + 2 * HALF

    payload = kernel_call(functools.partial(cut_kernel, core), floats(tile.shape[0], core), tile, name="cut")
    other = along(payload, mate)
    strip = floats(HALF, tile.shape[1])
    first, last = kernel_call(strips_kernel, (strip, strip), tile, name="strips")
    above, below = ring(last, "ty", 1), ring(first, "ty", -1)
    edge = floats(tall // 4, 4 * HALF)
    strips, edge_near, edge_past = kernel_call(
        functools.partial(borders_kernel, core, ny), (floats(2 * HALF, core), edge, edge),
        tile, above, below, name="borders",
    )
    strips, side, other_side = along(strips, mate), along(edge_near, near), along(edge_past, past)
    flow = kernel_call(
        functools.partial(shared_kernel, rows, half, 4, ny, nx), floats(2 * rows, PATCH),
        tile, above, below, side, other, strips, other_side, *tables(),
        scratch=flow_scratch(rows, half), name="flow",
    )
    window = kernel_call(
        functools.partial(window_kernel, half, nx), floats(*flow.shape),
        flow, along(flow, mate), along(flow, near), along(flow, far), name="window",
    )
    out = floats(1, 2, rows, cols)
    return kernel_call(
        functools.partial(relax_kernel, rows, cols, ny, nx), (out, out),
        window, ring(window, "ty", 1), ring(window, "ty", -1), name="relax", last=True,
    )


def solution(mesh):
    in_specs = (P("sec", "ty", "tx"),)
    out_specs = (P("sec", None, "ty", "tx"), P("sec", None, "ty", "tx"))
    shared = mesh.shape["sec"] == 2
    return jax.shard_map(
        shared_section if shared else whole_sections,
        mesh=mesh, in_specs=in_specs, out_specs=out_specs, check_vma=False,
    )
```

```python
import functools

import jax
import jax.numpy as jnp
import numpy as np
from jax import lax
from jax.experimental import pallas as pl
from jax.experimental.pallas import tpu as pltpu
from jax.sharding import PartitionSpec as P

PATCH = 128
STRIDE = 64
HALF = STRIDE // 2
FREQ = -(-(PATCH // 2 + 1) // 8) * 8

stiffness = 1.0
rate = 0.25


def two_parts(table):
    high = table.astype(jnp.bfloat16)
    low = (table - high.astype(np.float64)).astype(jnp.bfloat16)
    return high, low


def tables():
    angle = 2.0 * np.pi * (np.outer(np.arange(PATCH), np.arange(PATCH)) % PATCH) / PATCH
    cosine, sine = np.cos(angle), np.sin(angle)
    kept = np.arange(FREQ)[:, None] <= PATCH // 2
    left = np.concatenate([cosine[:FREQ] * kept, -sine[:FREQ] * kept])
    right = np.block([[cosine, -sine], [sine, cosine]])
    share = np.where((np.arange(FREQ) == 0) | (np.arange(FREQ) == PATCH // 2), 1.0, 2.0)
    scaled = (share * kept[:, 0])[None, :] / float(PATCH) ** 3
    back = np.concatenate([cosine[:, :FREQ] * scaled, sine[:, :FREQ] * scaled], axis=1)
    left_hi, left_lo = two_parts(left)
    back_hi, back_lo = two_parts(back)
    right_hi, right_lo = two_parts(right)
    return (
        np.concatenate([left_hi, left_hi, left_lo], axis=1),
        np.stack([right_hi, right_lo]),
        np.concatenate([back_hi, back_hi, back_lo], axis=1),
    )


def split(values):
    high = values.astype(jnp.bfloat16)
    return high, (values - high.astype(jnp.float32)).astype(jnp.bfloat16)


def mul(a, b):
    return jnp.dot(a, b, preferred_element_type=jnp.float32)


def right_dft(values, right_ref):
    high, low = split(values)
    return mul(high, right_ref[0]) + mul(low, right_ref[0]) + mul(high, right_ref[1])


def keep_region(region, z, wide, high_ref, low_ref):
    even, odd = region[:, :wide], region[:, STRIDE:STRIDE + wide]
    for part, values in enumerate((even, odd)):
        high, low = split(values)
        high_ref[z, :, part * wide:(part + 1) * wide] = high
        low_ref[z, :, part * wide:(part + 1) * wide] = low


def flow_kernel(rows, cols, group, region_ref, left_ref, right_ref, back_ref, flow_ref,
                high_ref, low_ref, *scratch):
    for z in range(2):
        keep_region(region_ref[z], z, cols * STRIDE, high_ref, low_ref)

    def put(c, i, row):
        flow_ref[c * rows + i:c * rows + i + 1, :] = row

    correlate(rows, cols, group, left_ref, right_ref, back_ref, put, high_ref, low_ref, *scratch)


def correlate(rows, cols, group, left_ref, right_ref, back_ref, put,
              high_ref, low_ref, half_ref, peak_ref, mass_ref, tilt_ref):
    order = [2 * t for t in range(cols // 2)] + [2 * t + 1 for t in range(cols // 2)]
    for z in range(2):
        for i in range(rows):
            band = pl.ds(i * STRIDE, PATCH)
            high = high_ref[z, band, :]
            stacked = jnp.concatenate([high, low_ref[z, band, :], high], axis=0)
            out = mul(left_ref[...], stacked)
            for t, j in enumerate(order):
                lanes = slice(t * PATCH, (t + 1) * PATCH)
                half_ref[z, i * cols + j, :, :PATCH] = out[:FREQ, lanes]
                half_ref[z, i * cols + j, :, PATCH:] = out[FREQ:, lanes]
    row = lax.broadcasted_iota(jnp.int32, (group, FREQ, PATCH), 1)
    lane = lax.broadcasted_iota(jnp.int32, (group, FREQ, PATCH), 2)
    varies = ((row + lane) > 0).astype(jnp.float32).reshape(group * FREQ, PATCH)
    lag = lax.broadcasted_iota(jnp.int32, (PATCH, 1), 0)
    lag = jnp.where(lag < PATCH // 2, lag, lag - PATCH).astype(jnp.float32)
    for n in range(0, rows * cols, group):
        both = half_ref[:, n:n + group].reshape(2 * group * FREQ, 2 * PATCH)
        freq = right_dft(both, right_ref)
        first, second = freq[:group * FREQ], freq[group * FREQ:]
        re1, im1 = first[:, :PATCH] * varies, first[:, PATCH:] * varies
        re2, im2 = second[:, :PATCH] * varies, second[:, PATCH:] * varies
        cross = jnp.concatenate([re1 * re2 + im1 * im2, im1 * re2 - re1 * im2], axis=1)
        mixed = right_dft(cross, right_ref)
        columns = []
        for m in range(group):
            part = mixed[m * FREQ:(m + 1) * FREQ]
            columns.append(jnp.concatenate([part[:, :PATCH], part[:, PATCH:]], axis=0))
        high, low = split(jnp.concatenate(columns, axis=1))
        scores = mul(back_ref[...], jnp.concatenate([high, low, high], axis=0))
        peak = jnp.max(scores, axis=0, keepdims=True)
        weight = jnp.exp(scores - peak)
        mass = jnp.sum(weight, axis=0, keepdims=True)
        tilt = jnp.sum(weight * lag, axis=0, keepdims=True)
        for m in range(group):
            lanes = slice(m * PATCH, (m + 1) * PATCH)
            peak_ref[n + m:n + m + 1, :] = peak[:, lanes]
            mass_ref[n + m:n + m + 1, :] = mass[:, lanes]
            tilt_ref[n + m:n + m + 1, :] = tilt[:, lanes]
    peak = peak_ref[...]
    share = jnp.exp(peak - jnp.max(peak, axis=1, keepdims=True))
    mass = mass_ref[...] * share
    lag = lax.broadcasted_iota(jnp.int32, mass.shape, 1)
    place = lax.broadcasted_iota(jnp.int32, mass.shape, 0) % cols
    here = lag == place
    lag = jnp.where(lag < PATCH // 2, lag, lag - PATCH).astype(jnp.float32)
    total = jnp.sum(mass, axis=1, keepdims=True)
    flow_y = jnp.sum(tilt_ref[...] * share, axis=1, keepdims=True) / total
    flow_x = jnp.sum(mass * lag, axis=1, keepdims=True) / total
    for c, value in enumerate((flow_y, flow_x)):
        spread = jnp.where(here, value, 0.0)
        for i in range(rows):
            put(c, i, jnp.sum(spread[i * cols:(i + 1) * cols], axis=0, keepdims=True))


def flow_scratch(rows, cols):
    tall, count = (rows + 1) * STRIDE, rows * cols
    return [
        pltpu.VMEM((2, tall, 2 * cols * STRIDE), jnp.bfloat16),
        pltpu.VMEM((2, tall, 2 * cols * STRIDE), jnp.bfloat16),
        pltpu.VMEM((2, count, FREQ, 2 * PATCH), jnp.float32),
        pltpu.VMEM((count, PATCH), jnp.float32),
        pltpu.VMEM((count, PATCH), jnp.float32),
        pltpu.VMEM((count, PATCH), jnp.float32),
    ]


IN_VMEM = pl.BlockSpec(memory_space=pltpu.VMEM)


def kernel_call(body, outs, *args, scratch=(), name=None, last=False):
    args = [pltpu.with_memory_space_constraint(a, pltpu.VMEM) if isinstance(a, jax.Array) else a for a in args]
    shapes = outs if last else jax.tree.map(lambda out: pltpu.VMEM(out.shape, out.dtype), outs)
    return pl.pallas_call(
        body,
        out_shape=shapes,
        in_specs=[IN_VMEM] * len(args),
        out_specs=jax.tree.map(lambda _: IN_VMEM, outs),
        scratch_shapes=scratch,
        compiler_params=pltpu.CompilerParams(vmem_limit_bytes=24 << 20),
        name=name,
    )(*args)


def floats(*shape):
    return jax.ShapeDtypeStruct(shape, jnp.float32)


def flow_of(region, rows, cols, group=4):
    return kernel_call(
        functools.partial(flow_kernel, rows, cols, group),
        floats(2 * rows, PATCH), region, *tables(),
        scratch=flow_scratch(rows, cols), name="flow",
    )


def shifted(value, axis, by):
    length = lax.axis_size(axis)
    pairs = [(i, i + by) for i in range(length) if 0 <= i + by < length]
    return lax.ppermute(value, axis, pairs)


def padded_2(value, sides, width):
    for axis, dim in sides:
        size, length = (lax.axis_size(axis), value.shape[dim])
        up = [(i, (i + 1) % size) for i in range(size - 1)]
        down = [(j, i) for i, j in up]
        last = lax.slice_in_dim(value, length - width, length, axis=dim)
        first = lax.slice_in_dim(value, 0, width, axis=dim)
        before = lax.ppermute(last, axis, up)
        after = lax.ppermute(first, axis, down)
        value = jnp.concatenate([before, value, after], axis=dim)
    return value


def lap_of(padded, center):
    return (
        padded[:, :-2, 1:-1]
        + padded[:, 2:, 1:-1]
        + padded[:, 1:-1, :-2]
        + padded[:, 1:-1, 2:]
        - 4.0 * center
    )


def whole_sections(images):
    tile = images[0]
    rows, cols = tile.shape[0] // STRIDE, tile.shape[1] // STRIDE
    region = padded_2(jnp.stack([tile, shifted(tile, "sec", -1)]), (("ty", 1), ("tx", 2)), HALF)
    flow = flow_of(region, rows, cols)[:, :cols].reshape(2, rows, cols)
    keep = (lax.axis_index("sec") < lax.axis_size("sec") - 1).astype(jnp.float32)
    flow = flow * keep
    padded = padded_2(flow, (("ty", 1), ("tx", 2)), 2)
    inner = padded[:, 1:-1, 1:-1]
    first = inner + rate * (stiffness * lap_of(padded, inner) + inner - inner)
    row_ids = lax.axis_index("ty") * rows + jnp.arange(-1, rows + 1, dtype=jnp.int32)
    col_ids = lax.axis_index("tx") * cols + jnp.arange(-1, cols + 1, dtype=jnp.int32)
    row_ok = (row_ids >= 0) & (row_ids < rows * lax.axis_size("ty"))
    col_ok = (col_ids >= 0) & (col_ids < cols * lax.axis_size("tx"))
    first = first * (row_ok[:, None] & col_ok[None, :]).astype(jnp.float32)[None]
    center = first[:, 1:-1, 1:-1]
    mesh = center + rate * (stiffness * lap_of(first, center) + flow - center)
    everything = lax.all_gather(mesh, "sec")
    earlier = jnp.arange(lax.axis_size("sec")) < lax.axis_index("sec")
    before = jnp.sum(jnp.where(earlier[:, None, None, None], everything, 0.0), axis=0)
    return (mesh[None], before[None])


AXES = ("sec", "ty", "tx")


def placed(half, y, x):
    ny, nx = lax.axis_size("ty"), lax.axis_size("tx")
    return (((half + x) % 2) * ny + y) * nx + x


def along(value, step):
    ny, nx = lax.axis_size("ty"), lax.axis_size("tx")
    pairs = []
    for y in range(ny):
        for g in range(2 * nx):
            to = step(g) % (2 * nx)
            pairs.append((placed(g % 2, y, g // 2), placed(to % 2, y, to // 2)))
    return lax.ppermute(value, AXES, pairs)


def mate(g):
    return g ^ 1


def near(g):
    return g - 1 if g % 2 == 0 else g + 1


def past(g):
    return g + 2 if g % 2 == 0 else g - 2


def pairs_even(value):
    size = lax.axis_size("ty")
    return lax.ppermute(value, "ty", [(i, i ^ 1) for i in range(size)])


def pairs_odd(value):
    size = lax.axis_size("ty")
    return lax.ppermute(value, "ty", [(i, (i - 1 if i % 2 == 0 else i + 1) % size) for i in range(size)])


def around(y, ny, even, odd):
    lower = y % 2 == 1
    above = jnp.where(y == 0, 0.0, jnp.where(lower, even, odd))
    below = jnp.where(y == ny - 1, 0.0, jnp.where(lower, odd, even))
    return above, below


def where_am_i():
    section, y, x = lax.axis_index("sec"), lax.axis_index("ty"), lax.axis_index("tx")
    return section, y, x, (section + x) % 2


def stack_rows(parts, start, stop):
    taken, base = [], 0
    for height, rows in parts:
        low, high = max(start - base, 0), min(stop - base, height)
        if low < high:
            taken.append(rows(low, high))
        base += height
    return taken[0] if len(taken) == 1 else jnp.concatenate(taken, axis=0)


def cut_kernel(core, upper, tile_ref, out_ref, even_ref, odd_ref):
    _, y, _, half = where_am_i()
    tall, width = tile_ref.shape

    @pl.when(half == 0)
    def _():
        out_ref[...] = tile_ref[:upper, width - core:]

    @pl.when(half == 1)
    def _():
        out_ref[...] = tile_ref[:upper, :core]

    first, last = tile_ref[:HALF], tile_ref[tall - HALF:]
    lower = y % 2 == 1
    even_ref[...] = jnp.where(lower, first, last)
    odd_ref[...] = jnp.where(lower, last, first)


def packed(column):
    quarter = column.shape[0] // 4
    return jnp.concatenate([column[q * quarter:(q + 1) * quarter] for q in range(4)], axis=1)


def unpacked(block):
    return jnp.concatenate([block[:, q * HALF:(q + 1) * HALF] for q in range(4)], axis=0)


def borders_kernel(core, upper, ny, tile_ref, even_ref, odd_ref, above_ref, rest_ref, near_ref, past_ref):
    _, y, _, half = where_am_i()
    width = tile_ref.shape[1]
    above, below = around(y, ny, even_ref[...], odd_ref[...])

    def column(lanes):
        return packed(jnp.concatenate([above[:, lanes], tile_ref[:, lanes], below[:, lanes]], axis=0))

    start, end = slice(0, HALF), slice(width - HALF, width)
    first, last = column(start), column(end)

    def send(lanes):
        above_ref[...] = above[:, lanes]
        rest_ref[...] = jnp.concatenate([tile_ref[upper:, lanes], below[:, lanes]], axis=0)

    @pl.when(half == 0)
    def _():
        send(slice(width - core, width))
        near_ref[...], past_ref[...] = first, last

    @pl.when(half == 1)
    def _():
        send(slice(0, core))
        near_ref[...], past_ref[...] = last, first


def shared_kernel(first_row, rows, all_rows, cols, group, ny, nx, tile_ref, even_ref, odd_ref, side_ref,
                  other_refs, other_side_ref, before_ref, left_ref, right_ref, back_ref, flow_ref,
                  high_ref, low_ref, *scratch):
    section, y, x, half = where_am_i()
    core, (tall, width) = other_refs[0].shape[1], tile_ref.shape
    wide = cols * STRIDE
    start, stop = first_row * STRIDE, (first_row + rows + 1) * STRIDE
    at_end = jnp.where(half == 0, x == 0, x == nx - 1)
    own_side = jnp.where(at_end, 0.0, unpacked(side_ref[...])[start:stop])
    other_side = jnp.where(at_end, 0.0, unpacked(other_side_ref[...])[start:stop])
    above, below = around(y, ny, even_ref[...], odd_ref[...])
    parts = [(ref.shape[0], lambda low, high, ref=ref: ref[low:high]) for ref in other_refs]
    other = stack_rows(parts, start, stop)

    def own(lanes):
        parts = [(HALF, lambda low, high: above[low:high, lanes]),
                 (tall, lambda low, high: tile_ref[low:high, lanes]),
                 (HALF, lambda low, high: below[low:high, lanes])]
        return stack_rows(parts, start, stop)

    @pl.when(half == 0)
    def _():
        value = jnp.concatenate([own_side, own(slice(0, core))], axis=1)
        keep_region(value, section, wide, high_ref, low_ref)
        keep_region(jnp.concatenate([other_side, other], axis=1), 1 - section, wide, high_ref, low_ref)

    @pl.when(half == 1)
    def _():
        value = jnp.concatenate([own(slice(width - core, width)), own_side], axis=1)
        keep_region(value, section, wide, high_ref, low_ref)
        keep_region(jnp.concatenate([other, other_side], axis=1), 1 - section, wide, high_ref, low_ref)

    flow_ref[...] = jnp.zeros_like(flow_ref) if before_ref is None else before_ref[...]

    def put(c, i, row):
        at = c * all_rows + first_row + i
        flow_ref[at:at + 1, :] = row

    correlate(rows, cols, group, left_ref, right_ref, back_ref, put, high_ref, low_ref, *scratch)


def upper_kernel(dims, tile, even, odd, side, above, other, other_side, left, right, back, *rest):
    shared_kernel(0, *dims, tile, even, odd, side, [above, other], other_side, None, left, right, back, *rest)


def lower_kernel(first_row, dims, tile, even, odd, side, above, other, more, other_side, before,
                 left, right, back, *rest):
    shared_kernel(first_row, *dims, tile, even, odd, side, [above, other, more], other_side, before,
                  left, right, back, *rest)


def close_kernel(width, nx, own_ref, near_ref, out_ref):
    _, _, x, half = where_am_i()
    own, lane = own_ref[...], lax.broadcasted_iota(jnp.int32, own_ref.shape, 1)
    close = jnp.where(jnp.where(half == 0, x == 0, x == nx - 1), 0.0, near_ref[...])
    begin = jnp.where(lane < 2, pltpu.roll(close, PATCH + 2 - width, 1), pltpu.roll(own, 2, 1))
    end = jnp.where(lane < width, own, pltpu.roll(close, width, 1))
    out_ref[...] = jnp.where(lane < width + 2, jnp.where(half == 0, begin, end), 0.0)


def window_kernel(width, own_ref, mate_ref, out_ref):
    _, _, _, half = where_am_i()
    own, other = own_ref[...], mate_ref[...]
    left, right = jnp.where(half == 0, own, other), jnp.where(half == 0, other, own)
    out_ref[...] = left + pltpu.roll(right, width + 2, 1)


def relax_kernel(rows, cols, ny, nx, own_ref, even_ref, odd_ref, mesh_ref, earlier_ref):
    section, y, x, _ = where_am_i()
    above, below = around(y, ny, even_ref[...], odd_ref[...])
    own = own_ref[...]
    tall = rows + 4
    shape = (tall, PATCH)
    row = lax.broadcasted_iota(jnp.int32, shape, 0) - 2 + y * rows
    col = lax.broadcasted_iota(jnp.int32, shape, 1) - 2 + x * cols
    inside = (row >= 0) & (row < ny * rows) & (col >= 0) & (col < nx * cols)

    def step(mesh, flow):
        nearby = (
            pltpu.roll(mesh, 1, 0) + pltpu.roll(mesh, tall - 1, 0)
            + pltpu.roll(mesh, 1, 1) + pltpu.roll(mesh, PATCH - 1, 1)
        )
        lap = nearby - 4.0 * mesh
        return jnp.where(inside, mesh + rate * (stiffness * lap + flow - mesh), 0.0)

    for c in range(2):
        flow = jnp.concatenate(
            [above[(c + 1) * rows - 2:(c + 1) * rows], own[c * rows:(c + 1) * rows],
             below[c * rows:c * rows + 2]], axis=0)
        flow = jnp.where(inside, flow, 0.0)
        mesh = step(step(flow, flow), flow)
        mesh = pltpu.roll(pltpu.roll(mesh, tall - 2, 0), PATCH - 2, 1)[:rows, :cols]
        mesh_ref[0, c] = jnp.where(section == 0, mesh, 0.0)
        earlier_ref[0, c] = jnp.where(section == 0, 0.0, mesh)


def shared_section(images):
    tile = images[0]
    ny, nx = lax.axis_size("ty"), lax.axis_size("tx")
    rows, cols = tile.shape[0] // STRIDE, tile.shape[1] // STRIDE
    half, early = cols // 2, rows // 2
    core, upper = half * STRIDE + HALF, early * STRIDE + HALF
    tall = tile.shape[0] + 2 * HALF

    strip = floats(HALF, tile.shape[1])
    payload, even, odd = kernel_call(
        functools.partial(cut_kernel, core, upper), (floats(upper, core), strip, strip), tile, name="cut",
    )
    other = along(payload, mate)
    even, odd = pairs_even(even), pairs_odd(odd)
    edge = floats(tall // 4, 4 * HALF)
    above, rest, edge_near, edge_past = kernel_call(
        functools.partial(borders_kernel, core, upper, ny),
        (floats(HALF, core), floats(tile.shape[0] - upper + HALF, core), edge, edge),
        tile, even, odd, name="borders",
    )
    above, side, other_side = along(above, mate), along(edge_near, near), along(edge_past, past)
    more = along(rest, mate)
    constants = tables()
    flow = kernel_call(
        functools.partial(upper_kernel, (early, rows, half, 4, ny, nx)), floats(2 * rows, PATCH),
        tile, even, odd, side, above, other, other_side, *constants,
        scratch=flow_scratch(early, half), name="upper",
    )
    flow = kernel_call(
        functools.partial(lower_kernel, early, (rows - early, rows, half, 4, ny, nx)), floats(2 * rows, PATCH),
        tile, even, odd, side, above, other, more, other_side, flow, *constants,
        scratch=flow_scratch(rows - early, half), name="lower",
    )
    close = kernel_call(
        functools.partial(close_kernel, half, nx), floats(*flow.shape), flow, along(flow, near), name="close",
    )
    window = kernel_call(
        functools.partial(window_kernel, half), floats(*flow.shape), close, along(close, mate), name="window",
    )
    out = floats(1, 2, rows, cols)
    return kernel_call(
        functools.partial(relax_kernel, rows, cols, ny, nx), (out, out),
        window, pairs_even(window), pairs_odd(window), name="relax", last=True,
    )


def solution(mesh):
    in_specs = (P("sec", "ty", "tx"),)
    out_specs = (P("sec", None, "ty", "tx"), P("sec", None, "ty", "tx"))
    even = mesh.shape["ty"] % 2 == 0 and mesh.shape["tx"] % 2 == 0
    shared = mesh.shape["sec"] == 2 and even
    return jax.shard_map(
        shared_section if shared else whole_sections,
        mesh=mesh, in_specs=in_specs, out_specs=out_specs, check_vma=False,
    )
```

```python
import functools

import jax
import jax.numpy as jnp
import numpy as np
from jax import lax
from jax.experimental import pallas as pl
from jax.experimental.pallas import tpu as pltpu
from jax.sharding import PartitionSpec as P


PATCH = 128
STRIDE = 64
HALF = STRIDE // 2
FREQ = -(-(PATCH // 2 + 1) // 8) * 8

stiffness = 1.0
rate = 0.25


def two_parts(table):
    high = table.astype(jnp.bfloat16)
    low = (table - high.astype(np.float64)).astype(jnp.bfloat16)
    return high, low


def tables():
    angle = 2.0 * np.pi * (np.outer(np.arange(PATCH), np.arange(PATCH)) % PATCH) / PATCH
    cosine, sine = np.cos(angle), np.sin(angle)
    kept = np.arange(FREQ)[:, None] <= PATCH // 2
    left = np.concatenate([cosine[:FREQ] * kept, -sine[:FREQ] * kept])
    right = np.block([[cosine, -sine], [sine, cosine]])
    share = np.where((np.arange(FREQ) == 0) | (np.arange(FREQ) == PATCH // 2), 1.0, 2.0)
    scaled = (share * kept[:, 0])[None, :] / float(PATCH) ** 3
    back = np.concatenate([cosine[:, :FREQ] * scaled, sine[:, :FREQ] * scaled], axis=1)
    left_hi, left_lo = two_parts(left)
    back_hi, back_lo = two_parts(back)
    right_hi, right_lo = two_parts(right)
    return (
        np.concatenate([left_hi, left_hi, left_lo], axis=1),
        np.stack([right_hi, right_lo]),
        np.concatenate([back_hi, back_hi, back_lo], axis=1),
    )


def split(values):
    high = values.astype(jnp.bfloat16)
    return high, (values - high.astype(jnp.float32)).astype(jnp.bfloat16)


def mul(a, b):
    return jnp.dot(a, b, preferred_element_type=jnp.float32)


def right_dft(values, right_ref):
    high, low = split(values)
    return mul(high, right_ref[0]) + mul(low, right_ref[0]) + mul(high, right_ref[1])


def node_order(cols):
    return [2 * t for t in range(cols // 2)] + [2 * t + 1 for t in range(cols // 2)]


def keep_region(region, wide, high_ref, low_ref):
    even, odd = region[:, :wide], region[:, STRIDE:STRIDE + wide]
    for part, values in enumerate((even, odd)):
        high, low = split(values)
        high_ref[:, part * wide:(part + 1) * wide] = high
        low_ref[:, part * wide:(part + 1) * wide] = low


def left_dft(cols, bands, high_ref, low_ref, left_ref, half_ref):
    for k, i in enumerate(bands):
        band = pl.ds(i * STRIDE, PATCH)
        high = high_ref[band, :]
        stacked = jnp.concatenate([high, low_ref[band, :], high], axis=0)
        out = mul(left_ref[...], stacked)
        for t, j in enumerate(node_order(cols)):
            lanes = slice(t * PATCH, (t + 1) * PATCH)
            half_ref[k * cols + j, :, :PATCH] = out[:FREQ, lanes]
            half_ref[k * cols + j, :, PATCH:] = out[FREQ:, lanes]


def correlate(rows, cols, group, sign, own_ref, other_ref, right_ref, back_ref, put,
              peak_ref, mass_ref, tilt_ref):
    row = lax.broadcasted_iota(jnp.int32, (group, FREQ, PATCH), 1)
    lane = lax.broadcasted_iota(jnp.int32, (group, FREQ, PATCH), 2)
    varies = ((row + lane) > 0).astype(jnp.float32).reshape(group * FREQ, PATCH)
    lag = lax.broadcasted_iota(jnp.int32, (PATCH, 1), 0)
    lag = jnp.where(lag < PATCH // 2, lag, lag - PATCH).astype(jnp.float32)
    for n in range(0, rows * cols, group):
        both = jnp.concatenate([ref[n:n + group].reshape(group * FREQ, 2 * PATCH) for ref in (own_ref, other_ref)])
        freq = right_dft(both, right_ref)
        first, second = freq[:group * FREQ], freq[group * FREQ:]
        re1, im1 = first[:, :PATCH] * varies, first[:, PATCH:] * varies
        re2, im2 = second[:, :PATCH] * varies, second[:, PATCH:] * varies
        cross = jnp.concatenate([re1 * re2 + im1 * im2, (im1 * re2 - re1 * im2) * sign], axis=1)
        mixed = right_dft(cross, right_ref)
        columns = []
        for m in range(group):
            part = mixed[m * FREQ:(m + 1) * FREQ]
            columns.append(jnp.concatenate([part[:, :PATCH], part[:, PATCH:]], axis=0))
        high, low = split(jnp.concatenate(columns, axis=1))
        scores = mul(back_ref[...], jnp.concatenate([high, low, high], axis=0))
        peak = jnp.max(scores, axis=0, keepdims=True)
        weight = jnp.exp(scores - peak)
        mass = jnp.sum(weight, axis=0, keepdims=True)
        tilt = jnp.sum(weight * lag, axis=0, keepdims=True)
        for m in range(group):
            lanes = slice(m * PATCH, (m + 1) * PATCH)
            peak_ref[n + m:n + m + 1, :] = peak[:, lanes]
            mass_ref[n + m:n + m + 1, :] = mass[:, lanes]
            tilt_ref[n + m:n + m + 1, :] = tilt[:, lanes]
    peak = peak_ref[...]
    share = jnp.exp(peak - jnp.max(peak, axis=1, keepdims=True))
    mass = mass_ref[...] * share
    lag = lax.broadcasted_iota(jnp.int32, mass.shape, 1)
    place = lax.broadcasted_iota(jnp.int32, mass.shape, 0) % cols
    here = lag == place
    lag = jnp.where(lag < PATCH // 2, lag, lag - PATCH).astype(jnp.float32)
    total = jnp.sum(mass, axis=1, keepdims=True)
    flow_y = jnp.sum(tilt_ref[...] * share, axis=1, keepdims=True) / total
    flow_x = jnp.sum(mass * lag, axis=1, keepdims=True) / total
    for c, value in enumerate((flow_y, flow_x)):
        spread = jnp.where(here, value, 0.0)
        for i in range(rows):
            put(c, i, jnp.sum(spread[i * cols:(i + 1) * cols], axis=0, keepdims=True))


def flow_kernel(rows, cols, group, region_ref, left_ref, right_ref, back_ref, flow_ref,
                high_ref, low_ref, own_ref, other_ref, *stats):
    for z, half_ref in enumerate((own_ref, other_ref)):
        keep_region(region_ref[z], cols * STRIDE, high_ref, low_ref)
        left_dft(cols, range(rows), high_ref, low_ref, left_ref, half_ref)

    def put(c, i, row):
        flow_ref[c * rows + i:c * rows + i + 1, :] = row

    correlate(rows, cols, group, 1.0, own_ref, other_ref, right_ref, back_ref, put, *stats)


def region_scratch(rows, cols):
    return [pltpu.VMEM(((rows + 1) * STRIDE, 2 * cols * STRIDE), jnp.bfloat16)] * 2


def half_shape(rows, cols):
    return (rows * cols, FREQ, 2 * PATCH)


def stats_scratch(rows, cols):
    return [pltpu.VMEM((rows * cols, PATCH), jnp.float32)] * 3


IN_VMEM = pl.BlockSpec(memory_space=pltpu.VMEM)


def kernel_call(body, outs, *args, scratch=(), last=False):
    args = [pltpu.with_memory_space_constraint(a, pltpu.VMEM) if isinstance(a, jax.Array) else a for a in args]
    shapes = outs if last else jax.tree.map(lambda out: pltpu.VMEM(out.shape, out.dtype), outs)
    return pl.pallas_call(
        body,
        out_shape=shapes,
        in_specs=[IN_VMEM] * len(args),
        out_specs=jax.tree.map(lambda _: IN_VMEM, outs),
        scratch_shapes=scratch,
        compiler_params=pltpu.CompilerParams(vmem_limit_bytes=24 << 20),
    )(*args)


def floats(*shape):
    return jax.ShapeDtypeStruct(shape, jnp.float32)


def flow_of(region, rows, cols, group=4):
    return kernel_call(
        functools.partial(flow_kernel, rows, cols, group),
        floats(2 * rows, PATCH), region, *tables(),
        scratch=region_scratch(rows, cols) + [pltpu.VMEM(half_shape(rows, cols), jnp.float32)] * 2
        + stats_scratch(rows, cols),
    )


def shifted(value, axis, by):
    length = lax.axis_size(axis)
    pairs = [(i, i + by) for i in range(length) if 0 <= i + by < length]
    return lax.ppermute(value, axis, pairs)


def padded_2(value, sides, width):
    for axis, dim in sides:
        size, length = (lax.axis_size(axis), value.shape[dim])
        up = [(i, (i + 1) % size) for i in range(size - 1)]
        down = [(j, i) for i, j in up]
        last = lax.slice_in_dim(value, length - width, length, axis=dim)
        first = lax.slice_in_dim(value, 0, width, axis=dim)
        before = lax.ppermute(last, axis, up)
        after = lax.ppermute(first, axis, down)
        value = jnp.concatenate([before, value, after], axis=dim)
    return value


def lap_of(padded, center):
    return (
        padded[:, :-2, 1:-1]
        + padded[:, 2:, 1:-1]
        + padded[:, 1:-1, :-2]
        + padded[:, 1:-1, 2:]
        - 4.0 * center
    )


def whole_sections(images):
    tile = images[0]
    rows, cols = tile.shape[0] // STRIDE, tile.shape[1] // STRIDE
    region = padded_2(jnp.stack([tile, shifted(tile, "sec", -1)]), (("ty", 1), ("tx", 2)), HALF)
    flow = flow_of(region, rows, cols)[:, :cols].reshape(2, rows, cols)
    keep = (lax.axis_index("sec") < lax.axis_size("sec") - 1).astype(jnp.float32)
    flow = flow * keep
    padded = padded_2(flow, (("ty", 1), ("tx", 2)), 2)
    inner = padded[:, 1:-1, 1:-1]
    first = inner + rate * (stiffness * lap_of(padded, inner) + inner - inner)
    row_ids = lax.axis_index("ty") * rows + jnp.arange(-1, rows + 1, dtype=jnp.int32)
    col_ids = lax.axis_index("tx") * cols + jnp.arange(-1, cols + 1, dtype=jnp.int32)
    row_ok = (row_ids >= 0) & (row_ids < rows * lax.axis_size("ty"))
    col_ok = (col_ids >= 0) & (col_ids < cols * lax.axis_size("tx"))
    first = first * (row_ok[:, None] & col_ok[None, :]).astype(jnp.float32)[None]
    center = first[:, 1:-1, 1:-1]
    mesh = center + rate * (stiffness * lap_of(first, center) + flow - center)
    everything = lax.all_gather(mesh, "sec")
    earlier = jnp.arange(lax.axis_size("sec")) < lax.axis_index("sec")
    before = jnp.sum(jnp.where(earlier[:, None, None, None], everything, 0.0), axis=0)
    return (mesh[None], before[None])


AXES = ("sec", "ty", "tx")


def placed(half, y, x):
    ny, nx = lax.axis_size("ty"), lax.axis_size("tx")
    return (((half + x) % 2) * ny + y) * nx + x


def along(value, step):
    ny, nx = lax.axis_size("ty"), lax.axis_size("tx")
    pairs = []
    for y in range(ny):
        for g in range(2 * nx):
            to = step(g) % (2 * nx)
            pairs.append((placed(g % 2, y, g // 2), placed(to % 2, y, to // 2)))
    return lax.ppermute(value, AXES, pairs)


def mate(g):
    return g ^ 1


def near(g):
    return g - 1 if g % 2 == 0 else g + 1


def far(g):
    return g - 2 if g % 2 == 0 else g + 2


def past(g):
    return g + 2 if g % 2 == 0 else g - 2


def pairs_even(value):
    size = lax.axis_size("ty")
    return lax.ppermute(value, "ty", [(i, i ^ 1) for i in range(size)])


def pairs_odd(value):
    size = lax.axis_size("ty")
    return lax.ppermute(value, "ty", [(i, (i - 1 if i % 2 == 0 else i + 1) % size) for i in range(size)])


def around(y, ny, even, odd):
    lower = y % 2 == 1
    above = jnp.where(y == 0, 0.0, jnp.where(lower, even, odd))
    below = jnp.where(y == ny - 1, 0.0, jnp.where(lower, odd, even))
    return above, below


def where_am_i():
    section, y, x = lax.axis_index("sec"), lax.axis_index("ty"), lax.axis_index("tx")
    return section, y, x, (section + x) % 2


def stack_rows(parts, start, stop):
    taken, base = [], 0
    for height, rows in parts:
        low, high = max(start - base, 0), min(stop - base, height)
        if low < high:
            taken.append(rows(low, high))
        base += height
    return taken[0] if len(taken) == 1 else jnp.concatenate(taken, axis=0)


def cut_kernel(core, upper, tile_ref, out_ref, even_ref, odd_ref):
    _, y, _, half = where_am_i()
    tall, width = tile_ref.shape

    @pl.when(half == 0)
    def _():
        out_ref[...] = tile_ref[:upper, width - core:]

    @pl.when(half == 1)
    def _():
        out_ref[...] = tile_ref[:upper, :core]

    first, last = tile_ref[:HALF], tile_ref[tall - HALF:]
    lower = y % 2 == 1
    even_ref[...] = jnp.where(lower, first, last)
    odd_ref[...] = jnp.where(lower, last, first)


def packed(column):
    quarter = column.shape[0] // 4
    return jnp.concatenate([column[q * quarter:(q + 1) * quarter] for q in range(4)], axis=1)


def unpacked(block):
    return jnp.concatenate([block[:, q * HALF:(q + 1) * HALF] for q in range(4)], axis=0)


def borders_kernel(core, upper, ny, tile_ref, even_ref, odd_ref, above_ref, rest_ref, near_ref, past_ref):
    _, y, _, half = where_am_i()
    width = tile_ref.shape[1]
    above, below = around(y, ny, even_ref[...], odd_ref[...])

    def column(lanes):
        return packed(jnp.concatenate([above[:, lanes], tile_ref[:, lanes], below[:, lanes]], axis=0))

    start, end = slice(0, HALF), slice(width - HALF, width)
    first, last = column(start), column(end)

    def send(lanes):
        above_ref[...] = above[:, lanes]
        rest_ref[...] = jnp.concatenate([tile_ref[upper:, lanes], below[:, lanes]], axis=0)

    @pl.when(half == 0)
    def _():
        send(slice(width - core, width))
        near_ref[...], past_ref[...] = first, last

    @pl.when(half == 1)
    def _():
        send(slice(0, core))
        near_ref[...], past_ref[...] = last, first


def fill_region(values, side, first_row, rows, cols, half, high_ref, low_ref):
    start, stop = first_row * STRIDE, (first_row + rows + 1) * STRIDE

    @pl.when(half == 0)
    def _():
        value = jnp.concatenate([side[start:stop], values(0, start, stop)], axis=1)
        keep_region(value, cols * STRIDE, high_ref, low_ref)

    @pl.when(half == 1)
    def _():
        value = jnp.concatenate([values(1, start, stop), side[start:stop]], axis=1)
        keep_region(value, cols * STRIDE, high_ref, low_ref)


def own_values(core, tile_ref, above, below):
    tall, width = tile_ref.shape

    def values(h, start, stop):
        lanes = slice(0, core) if h == 0 else slice(width - core, width)
        parts = [(HALF, lambda low, high: above[low:high, lanes]),
                 (tall, lambda low, high: tile_ref[low:high, lanes]),
                 (HALF, lambda low, high: below[low:high, lanes])]
        return stack_rows(parts, start, stop)

    return values


def other_values(refs):
    parts = [(ref.shape[0], lambda low, high, ref=ref: ref[low:high]) for ref in refs]
    return lambda h, start, stop: stack_rows(parts, start, stop)


def upper_kernel(early, rows, cols, group, ny, nx, tile_ref, even_ref, odd_ref, side_ref,
                 above_ref, other_ref, cross_ref, left_ref, right_ref, back_ref, flow_ref, later_ref,
                 own_high, own_low, high_ref, low_ref, own_half, other_half, *stats):
    section, y, x, half = where_am_i()
    at_end = jnp.where(half == 0, x == 0, x == nx - 1)
    above, below = around(y, ny, even_ref[...], odd_ref[...])
    side = jnp.where(at_end, 0.0, unpacked(side_ref[...]))
    fill_region(own_values(other_ref.shape[1], tile_ref, above, below), side, 0, rows, cols, half, own_high, own_low)
    left_dft(cols, range(early), own_high, own_low, left_ref, own_half)
    left_dft(cols, range(early, rows), own_high, own_low, left_ref, later_ref)
    side = jnp.where(at_end, 0.0, unpacked(cross_ref[...]))
    fill_region(other_values([above_ref, other_ref]), side, 0, early, cols, half, high_ref, low_ref)
    left_dft(cols, range(early), high_ref, low_ref, left_ref, other_half)
    flow_ref[...] = jnp.zeros_like(flow_ref)

    def put(c, i, row):
        flow_ref[c * rows + i:c * rows + i + 1, :] = row

    sign = jnp.where(section == 0, 1.0, -1.0)
    correlate(early, cols, group, sign, own_half, other_half, right_ref, back_ref, put, *stats)


def lower_kernel(early, rows, cols, group, nx, later_ref, above_ref, other_ref, rest_ref, cross_ref,
                 before_ref, left_ref, right_ref, back_ref, flow_ref, high_ref, low_ref, other_half, *stats):
    section, _, x, half = where_am_i()
    at_end = jnp.where(half == 0, x == 0, x == nx - 1)
    side = jnp.where(at_end, 0.0, unpacked(cross_ref[...]))
    others = other_values([above_ref, other_ref, rest_ref])
    fill_region(others, side, early, rows - early, cols, half, high_ref, low_ref)
    left_dft(cols, range(rows - early), high_ref, low_ref, left_ref, other_half)
    flow_ref[...] = before_ref[...]

    def put(c, i, row):
        at = c * rows + early + i
        flow_ref[at:at + 1, :] = row

    sign = jnp.where(section == 0, 1.0, -1.0)
    correlate(rows - early, cols, group, sign, later_ref, other_half, right_ref, back_ref, put, *stats)


def window_kernel(width, nx, own_ref, mate_ref, near_ref, far_ref, out_ref):
    _, _, x, place = where_am_i()
    half = place == 1
    own, other, close, beyond = own_ref[...], mate_ref[...], near_ref[...], far_ref[...]
    lane = lax.broadcasted_iota(jnp.int32, own.shape, 1)
    begin = jnp.where(x == 0, 0.0, jnp.where(half, beyond, close))
    left = jnp.where(half, other, own)
    right = jnp.where(half, own, other)
    end = jnp.where(x == nx - 1, 0.0, jnp.where(half, close, beyond))
    begin, left = pltpu.roll(begin, PATCH + 2 - width, 1), pltpu.roll(left, 2, 1)
    right, end = pltpu.roll(right, 2 + width, 1), pltpu.roll(end, 2 + 2 * width, 1)
    value = jnp.where(lane < 2, begin, jnp.where(lane < 2 + width, left, right))
    value = jnp.where(lane < 2 + 2 * width, value, jnp.where(lane < 4 + 2 * width, end, 0.0))
    out_ref[...] = value


def relax_kernel(rows, cols, ny, nx, own_ref, even_ref, odd_ref, mesh_ref, earlier_ref):
    section, y, x, _ = where_am_i()
    above, below = around(y, ny, even_ref[...], odd_ref[...])
    own = own_ref[...]
    tall = rows + 4
    shape = (tall, PATCH)
    row = lax.broadcasted_iota(jnp.int32, shape, 0) - 2 + y * rows
    col = lax.broadcasted_iota(jnp.int32, shape, 1) - 2 + x * cols
    inside = (row >= 0) & (row < ny * rows) & (col >= 0) & (col < nx * cols)

    def step(mesh, flow):
        nearby = (
            pltpu.roll(mesh, 1, 0) + pltpu.roll(mesh, tall - 1, 0)
            + pltpu.roll(mesh, 1, 1) + pltpu.roll(mesh, PATCH - 1, 1)
        )
        lap = nearby - 4.0 * mesh
        return jnp.where(inside, mesh + rate * (stiffness * lap + flow - mesh), 0.0)

    for c in range(2):
        flow = jnp.concatenate(
            [above[(c + 1) * rows - 2:(c + 1) * rows], own[c * rows:(c + 1) * rows],
             below[c * rows:c * rows + 2]], axis=0)
        flow = jnp.where(inside, flow, 0.0)
        mesh = step(step(flow, flow), flow)
        mesh = pltpu.roll(pltpu.roll(mesh, tall - 2, 0), PATCH - 2, 1)[:rows, :cols]
        mesh_ref[0, c] = jnp.where(section == 0, mesh, 0.0)
        earlier_ref[0, c] = jnp.where(section == 0, 0.0, mesh)


def shared_section(images):
    tile = images[0]
    ny, nx = lax.axis_size("ty"), lax.axis_size("tx")
    rows, cols = tile.shape[0] // STRIDE, tile.shape[1] // STRIDE
    half, early = cols // 2, rows // 2
    core, upper = half * STRIDE + HALF, early * STRIDE + HALF
    tall = tile.shape[0] + 2 * HALF

    strip = floats(HALF, tile.shape[1])
    payload, even, odd = kernel_call(
        functools.partial(cut_kernel, core, upper), (floats(upper, core), strip, strip), tile,
    )
    other = along(payload, mate)
    even, odd = pairs_even(even), pairs_odd(odd)
    edge = floats(tall // 4, 4 * HALF)
    above, rest, edge_near, edge_past = kernel_call(
        functools.partial(borders_kernel, core, upper, ny),
        (floats(HALF, core), floats(tile.shape[0] - upper + HALF, core), edge, edge),
        tile, even, odd,
    )
    above, side = along(above, mate), along(edge_near, near)
    cross, rest = along(edge_past, past), along(rest, mate)
    constants = tables()
    half_of = lambda count: pltpu.VMEM(half_shape(count, half), jnp.float32)
    late = rows - early
    flow, later = kernel_call(
        functools.partial(upper_kernel, early, rows, half, 4, ny, nx),
        (floats(2 * rows, PATCH), floats(*half_shape(late, half))),
        tile, even, odd, side, above, other, cross, *constants,
        scratch=region_scratch(rows, half) + region_scratch(early, half) + [half_of(early)] * 2
        + stats_scratch(early, half),
    )
    flow = kernel_call(
        functools.partial(lower_kernel, early, rows, half, 4, nx), floats(2 * rows, PATCH),
        later, above, other, rest, cross, flow, *constants,
        scratch=region_scratch(late, half) + [half_of(late)] + stats_scratch(late, half),
    )
    window = kernel_call(
        functools.partial(window_kernel, half, nx), floats(*flow.shape),
        flow, along(flow, mate), along(flow, near), along(flow, far),
    )
    out = floats(1, 2, rows, cols)
    return kernel_call(
        functools.partial(relax_kernel, rows, cols, ny, nx), (out, out),
        window, pairs_even(window), pairs_odd(window), last=True,
    )


def solution(mesh):
    in_specs = (P("sec", "ty", "tx"),)
    out_specs = (P("sec", None, "ty", "tx"), P("sec", None, "ty", "tx"))
    even = mesh.shape["ty"] % 2 == 0 and mesh.shape["tx"] % 2 == 0
    shared = mesh.shape["sec"] == 2 and even

    def body(images):
        return (shared_section if shared else whole_sections)(images)

    return jax.shard_map(body, mesh=mesh, in_specs=in_specs, out_specs=out_specs, check_vma=False)
```

```python
import functools

import jax
import jax.numpy as jnp
import numpy as np
from jax import lax
from jax.experimental import pallas as pl
from jax.experimental.pallas import tpu as pltpu
from jax.sharding import PartitionSpec as P


PATCH = 128
STRIDE = 64
HALF = STRIDE // 2
FREQ = -(-(PATCH // 2 + 1) // 8) * 8

stiffness = 1.0
rate = 0.25


def two_parts(table):
    high = table.astype(jnp.bfloat16)
    low = (table - high.astype(np.float64)).astype(jnp.bfloat16)
    return high, low


def tables():
    angle = 2.0 * np.pi * (np.outer(np.arange(PATCH), np.arange(PATCH)) % PATCH) / PATCH
    cosine, sine = np.cos(angle), np.sin(angle)
    kept = np.arange(FREQ)[:, None] <= PATCH // 2
    left = np.concatenate([cosine[:FREQ] * kept, -sine[:FREQ] * kept])
    right = np.block([[cosine, -sine], [sine, cosine]])
    share = np.where((np.arange(FREQ) == 0) | (np.arange(FREQ) == PATCH // 2), 1.0, 2.0)
    scaled = (share * kept[:, 0])[None, :] / float(PATCH) ** 3
    back = np.concatenate([cosine[:, :FREQ] * scaled, sine[:, :FREQ] * scaled], axis=1)
    left_hi, left_lo = two_parts(left)
    back_hi, back_lo = two_parts(back)
    right_hi, right_lo = two_parts(right)
    return (
        np.concatenate([left_hi, left_hi, left_lo], axis=1),
        np.stack([right_hi, right_lo]),
        np.concatenate([back_hi, back_hi, back_lo], axis=1),
    )


def split(values):
    high = values.astype(jnp.bfloat16)
    return high, (values - high.astype(jnp.float32)).astype(jnp.bfloat16)


def mul(a, b):
    return jnp.dot(a, b, preferred_element_type=jnp.float32)


def right_dft(values, right_ref):
    high, low = split(values)
    return mul(high, right_ref[0]) + mul(low, right_ref[0]) + mul(high, right_ref[1])


def node_order(cols):
    return [2 * t for t in range(cols // 2)] + [2 * t + 1 for t in range(cols // 2)]


def keep_region(region, wide, high_ref, low_ref):
    even, odd = region[:, :wide], region[:, STRIDE:STRIDE + wide]
    for part, values in enumerate((even, odd)):
        high, low = split(values)
        high_ref[:, part * wide:(part + 1) * wide] = high
        low_ref[:, part * wide:(part + 1) * wide] = low


def left_dft(cols, bands, high_ref, low_ref, left_ref, half_ref):
    for k, i in enumerate(bands):
        band = pl.ds(i * STRIDE, PATCH)
        high = high_ref[band, :]
        stacked = jnp.concatenate([high, low_ref[band, :], high], axis=0)
        out = mul(left_ref[...], stacked)
        for t, j in enumerate(node_order(cols)):
            lanes = slice(t * PATCH, (t + 1) * PATCH)
            half_ref[k * cols + j, :, :PATCH] = out[:FREQ, lanes]
            half_ref[k * cols + j, :, PATCH:] = out[FREQ:, lanes]


def correlate(rows, cols, group, sign, own_ref, other_ref, right_ref, back_ref, put,
              peak_ref, mass_ref, tilt_ref):
    row = lax.broadcasted_iota(jnp.int32, (group, FREQ, PATCH), 1)
    lane = lax.broadcasted_iota(jnp.int32, (group, FREQ, PATCH), 2)
    varies = ((row + lane) > 0).astype(jnp.float32).reshape(group * FREQ, PATCH)
    lag = lax.broadcasted_iota(jnp.int32, (PATCH, 1), 0)
    lag = jnp.where(lag < PATCH // 2, lag, lag - PATCH).astype(jnp.float32)
    for n in range(0, rows * cols, group):
        both = jnp.concatenate([ref[n:n + group].reshape(group * FREQ, 2 * PATCH) for ref in (own_ref, other_ref)])
        freq = right_dft(both, right_ref)
        first, second = freq[:group * FREQ], freq[group * FREQ:]
        re1, im1 = first[:, :PATCH] * varies, first[:, PATCH:] * varies
        re2, im2 = second[:, :PATCH] * varies, second[:, PATCH:] * varies
        cross = jnp.concatenate([re1 * re2 + im1 * im2, (im1 * re2 - re1 * im2) * sign], axis=1)
        mixed = right_dft(cross, right_ref)
        columns = []
        for m in range(group):
            part = mixed[m * FREQ:(m + 1) * FREQ]
            columns.append(jnp.concatenate([part[:, :PATCH], part[:, PATCH:]], axis=0))
        high, low = split(jnp.concatenate(columns, axis=1))
        scores = mul(back_ref[...], jnp.concatenate([high, low, high], axis=0))
        peak = jnp.max(scores, axis=0, keepdims=True)
        weight = jnp.exp(scores - peak)
        mass = jnp.sum(weight, axis=0, keepdims=True)
        tilt = jnp.sum(weight * lag, axis=0, keepdims=True)
        for m in range(group):
            lanes = slice(m * PATCH, (m + 1) * PATCH)
            peak_ref[n + m:n + m + 1, :] = peak[:, lanes]
            mass_ref[n + m:n + m + 1, :] = mass[:, lanes]
            tilt_ref[n + m:n + m + 1, :] = tilt[:, lanes]
    peak = peak_ref[...]
    share = jnp.exp(peak - jnp.max(peak, axis=1, keepdims=True))
    mass = mass_ref[...] * share
    lag = lax.broadcasted_iota(jnp.int32, mass.shape, 1)
    place = lax.broadcasted_iota(jnp.int32, mass.shape, 0) % cols
    here = lag == place
    lag = jnp.where(lag < PATCH // 2, lag, lag - PATCH).astype(jnp.float32)
    total = jnp.sum(mass, axis=1, keepdims=True)
    flow_y = jnp.sum(tilt_ref[...] * share, axis=1, keepdims=True) / total
    flow_x = jnp.sum(mass * lag, axis=1, keepdims=True) / total
    for c, value in enumerate((flow_y, flow_x)):
        spread = jnp.where(here, value, 0.0)
        for i in range(rows):
            put(c, i, jnp.sum(spread[i * cols:(i + 1) * cols], axis=0, keepdims=True))


def flow_kernel(rows, cols, group, region_ref, left_ref, right_ref, back_ref, flow_ref,
                high_ref, low_ref, own_ref, other_ref, *stats):
    for z, half_ref in enumerate((own_ref, other_ref)):
        keep_region(region_ref[z], cols * STRIDE, high_ref, low_ref)
        left_dft(cols, range(rows), high_ref, low_ref, left_ref, half_ref)

    def put(c, i, row):
        flow_ref[c * rows + i:c * rows + i + 1, :] = row

    correlate(rows, cols, group, 1.0, own_ref, other_ref, right_ref, back_ref, put, *stats)


def region_scratch(rows, cols):
    return [pltpu.VMEM(((rows + 1) * STRIDE, 2 * cols * STRIDE), jnp.bfloat16)] * 2


def half_shape(rows, cols):
    return (rows * cols, FREQ, 2 * PATCH)


def stats_scratch(rows, cols):
    return [pltpu.VMEM((rows * cols, PATCH), jnp.float32)] * 3


IN_VMEM = pl.BlockSpec(memory_space=pltpu.VMEM)


def kernel_call(body, outs, *args, scratch=(), last=False):
    args = [pltpu.with_memory_space_constraint(a, pltpu.VMEM) if isinstance(a, jax.Array) else a for a in args]
    shapes = outs if last else jax.tree.map(lambda out: pltpu.VMEM(out.shape, out.dtype), outs)
    return pl.pallas_call(
        body,
        out_shape=shapes,
        in_specs=[IN_VMEM] * len(args),
        out_specs=jax.tree.map(lambda _: IN_VMEM, outs),
        scratch_shapes=scratch,
        compiler_params=pltpu.CompilerParams(vmem_limit_bytes=24 << 20),
    )(*args)


def floats(*shape):
    return jax.ShapeDtypeStruct(shape, jnp.float32)


def flow_of(region, rows, cols, group=4):
    return kernel_call(
        functools.partial(flow_kernel, rows, cols, group),
        floats(2 * rows, PATCH), region, *tables(),
        scratch=region_scratch(rows, cols) + [pltpu.VMEM(half_shape(rows, cols), jnp.float32)] * 2
        + stats_scratch(rows, cols),
    )


def shifted(value, axis, by):
    length = lax.axis_size(axis)
    pairs = [(i, i + by) for i in range(length) if 0 <= i + by < length]
    return lax.ppermute(value, axis, pairs)


def padded_2(value, sides, width):
    for axis, dim in sides:
        size, length = (lax.axis_size(axis), value.shape[dim])
        up = [(i, (i + 1) % size) for i in range(size - 1)]
        down = [(j, i) for i, j in up]
        last = lax.slice_in_dim(value, length - width, length, axis=dim)
        first = lax.slice_in_dim(value, 0, width, axis=dim)
        before = lax.ppermute(last, axis, up)
        after = lax.ppermute(first, axis, down)
        value = jnp.concatenate([before, value, after], axis=dim)
    return value


def lap_of(padded, center):
    return (
        padded[:, :-2, 1:-1]
        + padded[:, 2:, 1:-1]
        + padded[:, 1:-1, :-2]
        + padded[:, 1:-1, 2:]
        - 4.0 * center
    )


def whole_sections(images):
    tile = images[0]
    rows, cols = tile.shape[0] // STRIDE, tile.shape[1] // STRIDE
    region = padded_2(jnp.stack([tile, shifted(tile, "sec", -1)]), (("ty", 1), ("tx", 2)), HALF)
    flow = flow_of(region, rows, cols)[:, :cols].reshape(2, rows, cols)
    keep = (lax.axis_index("sec") < lax.axis_size("sec") - 1).astype(jnp.float32)
    flow = flow * keep
    padded = padded_2(flow, (("ty", 1), ("tx", 2)), 2)
    inner = padded[:, 1:-1, 1:-1]
    first = inner + rate * (stiffness * lap_of(padded, inner) + inner - inner)
    row_ids = lax.axis_index("ty") * rows + jnp.arange(-1, rows + 1, dtype=jnp.int32)
    col_ids = lax.axis_index("tx") * cols + jnp.arange(-1, cols + 1, dtype=jnp.int32)
    row_ok = (row_ids >= 0) & (row_ids < rows * lax.axis_size("ty"))
    col_ok = (col_ids >= 0) & (col_ids < cols * lax.axis_size("tx"))
    first = first * (row_ok[:, None] & col_ok[None, :]).astype(jnp.float32)[None]
    center = first[:, 1:-1, 1:-1]
    mesh = center + rate * (stiffness * lap_of(first, center) + flow - center)
    everything = lax.all_gather(mesh, "sec")
    earlier = jnp.arange(lax.axis_size("sec")) < lax.axis_index("sec")
    before = jnp.sum(jnp.where(earlier[:, None, None, None], everything, 0.0), axis=0)
    return (mesh[None], before[None])


AXES = ("sec", "ty", "tx")


def placed(half, y, x):
    ny, nx = lax.axis_size("ty"), lax.axis_size("tx")
    return (((half + x) % 2) * ny + y) * nx + x


def along(value, step):
    ny, nx = lax.axis_size("ty"), lax.axis_size("tx")
    pairs = []
    for y in range(ny):
        for g in range(2 * nx):
            to = step(g) % (2 * nx)
            pairs.append((placed(g % 2, y, g // 2), placed(to % 2, y, to // 2)))
    return lax.ppermute(value, AXES, pairs)


def mate(g):
    return g ^ 1


def near(g):
    return g - 1 if g % 2 == 0 else g + 1


def far(g):
    return g - 2 if g % 2 == 0 else g + 2


def pairs_even(value):
    size = lax.axis_size("ty")
    return lax.ppermute(value, "ty", [(i, i ^ 1) for i in range(size)])


def pairs_odd(value):
    size = lax.axis_size("ty")
    return lax.ppermute(value, "ty", [(i, (i - 1 if i % 2 == 0 else i + 1) % size) for i in range(size)])


def around(y, ny, even, odd):
    lower = y % 2 == 1
    above = jnp.where(y == 0, 0.0, jnp.where(lower, even, odd))
    below = jnp.where(y == ny - 1, 0.0, jnp.where(lower, odd, even))
    return above, below


def where_am_i():
    section, y, x = lax.axis_index("sec"), lax.axis_index("ty"), lax.axis_index("tx")
    return section, y, x, (section + x) % 2


def packed(column):
    quarter = column.shape[0] // 4
    return jnp.concatenate([column[q * quarter:(q + 1) * quarter] for q in range(4)], axis=1)


def unpacked(block):
    return jnp.concatenate([block[:, q * HALF:(q + 1) * HALF] for q in range(4)], axis=0)


def packed_wide(value):
    full = value.shape[1] // PATCH
    tiles = [value[:, t * PATCH:(t + 1) * PATCH] for t in range(full)]
    return jnp.concatenate(tiles + [packed(value[:, full * PATCH:])], axis=0)


def unpacked_wide(block, tall, width):
    full = width // PATCH
    tiles = [block[t * tall:(t + 1) * tall] for t in range(full)]
    return jnp.concatenate(tiles + [unpacked(block[full * tall:full * tall + tall // 4])], axis=1)


def own_lanes(half, core, width):
    return slice(0, core) if half == 0 else slice(width - core, width)


def edge_of(half, value):
    return value[:, :HALF] if half == 0 else value[:, value.shape[1] - HALF:]


def body_of(half, value):
    return value[:, HALF:] if half == 0 else value[:, :value.shape[1] - HALF]


def by_half(half, branch):
    for h in range(2):
        pl.when(half == h)(functools.partial(branch, h))


def cut_kernel(core, tile_ref, frame_ref, rest_ref):
    _, _, _, half = where_am_i()
    tall, width = tile_ref.shape

    def branch(h):
        value = tile_ref[:, own_lanes(1 - h, core, width)]
        middle = value[HALF:tall - HALF]
        ends = jnp.concatenate([value[:HALF], value[tall - HALF:]], axis=0)
        frame_ref[...] = jnp.concatenate([packed_wide(ends), packed(edge_of(1 - h, middle))], axis=0)
        rest_ref[...] = body_of(1 - h, middle)

    by_half(half, branch)


def ends_of(core, frame):
    return unpacked_wide(frame, 2 * HALF, core)


def side_of(tall, frame):
    return unpacked(frame[frame.shape[0] - (tall - 2 * HALF) // 4:])


def strips_kernel(core, tile_ref, frame_ref, even_ref, odd_ref):
    _, y, _, half = where_am_i()
    tall, width = tile_ref.shape
    lower = y % 2 == 1
    ends = ends_of(core, frame_ref[...])

    def branch(h):
        lanes = own_lanes(h, core, width)
        first = packed_wide(jnp.concatenate([tile_ref[:HALF, lanes], ends[:HALF]], axis=0))
        last = packed_wide(jnp.concatenate([tile_ref[tall - HALF:, lanes], ends[HALF:]], axis=0))
        even_ref[...] = jnp.where(lower, first, last)
        odd_ref[...] = jnp.where(lower, last, first)

    by_half(half, branch)


def strips_of(core, y, ny, even_ref, odd_ref):
    above, below = around(y, ny, even_ref[...], odd_ref[...])
    return unpacked_wide(above, 2 * HALF, core), unpacked_wide(below, 2 * HALF, core)


def sides_kernel(core, ny, tile_ref, frame_ref, even_ref, odd_ref, side_ref):
    _, y, _, half = where_am_i()
    tall, width = tile_ref.shape
    above, below = strips_of(core, y, ny, even_ref, odd_ref)
    ends, side = ends_of(core, frame_ref[...]), side_of(tall, frame_ref[...])

    def branch(h):
        own = edge_of(h, tile_ref[:, own_lanes(h, core, width)])
        over, under = edge_of(h, above), edge_of(h, below)
        limits = edge_of(h, ends)
        side_ref[...] = jnp.concatenate(
            [packed(jnp.concatenate([over[:HALF], own, under[:HALF]], axis=0)),
             packed(jnp.concatenate([over[HALF:], limits[:HALF], side, limits[HALF:], under[HALF:]], axis=0))],
            axis=0)

    by_half(half, branch)


def shared_kernel(rows, cols, group, ny, nx, tile_ref, frame_ref, rest_ref, even_ref, odd_ref, sides_ref,
                  left_ref, right_ref, back_ref, flow_ref, high_ref, low_ref, own_half, other_half, *stats):
    section, y, x, half = where_am_i()
    tall, width = tile_ref.shape
    core = cols * STRIDE + HALF
    above, below = strips_of(core, y, ny, even_ref, odd_ref)
    ends, side = ends_of(core, frame_ref[...]), side_of(tall, frame_ref[...])
    at_end = jnp.where(half == 0, x == 0, x == nx - 1)
    sides = jnp.where(at_end, 0.0, sides_ref[...])
    quarter = sides.shape[0] // 2
    own_side, other_side = unpacked(sides[:quarter]), unpacked(sides[quarter:])

    def joined(h, outer, value):
        return jnp.concatenate([outer, value] if h == 0 else [value, outer], axis=1)

    def own_branch(h):
        middle = tile_ref[:, own_lanes(h, core, width)]
        value = jnp.concatenate([above[:HALF], middle, below[:HALF]], axis=0)
        keep_region(joined(h, own_side, value), cols * STRIDE, high_ref, low_ref)

    def other_branch(h):
        middle = joined(h, side, rest_ref[...])
        value = jnp.concatenate([above[HALF:], ends[:HALF], middle, ends[HALF:], below[HALF:]], axis=0)
        keep_region(joined(h, other_side, value), cols * STRIDE, high_ref, low_ref)

    for branch, half_ref in ((own_branch, own_half), (other_branch, other_half)):
        by_half(half, branch)
        left_dft(cols, range(rows), high_ref, low_ref, left_ref, half_ref)

    def put(c, i, row):
        flow_ref[c * rows + i:c * rows + i + 1, :] = row

    sign = jnp.where(section == 0, 1.0, -1.0)
    correlate(rows, cols, group, sign, own_half, other_half, right_ref, back_ref, put, *stats)


def window_kernel(width, nx, own_ref, mate_ref, near_ref, far_ref, out_ref):
    _, _, x, place = where_am_i()
    half = place == 1
    own, other, close, beyond = own_ref[...], mate_ref[...], near_ref[...], far_ref[...]
    lane = lax.broadcasted_iota(jnp.int32, own.shape, 1)
    begin = jnp.where(x == 0, 0.0, jnp.where(half, beyond, close))
    left = jnp.where(half, other, own)
    right = jnp.where(half, own, other)
    end = jnp.where(x == nx - 1, 0.0, jnp.where(half, close, beyond))
    begin, left = pltpu.roll(begin, PATCH + 2 - width, 1), pltpu.roll(left, 2, 1)
    right, end = pltpu.roll(right, 2 + width, 1), pltpu.roll(end, 2 + 2 * width, 1)
    value = jnp.where(lane < 2, begin, jnp.where(lane < 2 + width, left, right))
    value = jnp.where(lane < 2 + 2 * width, value, jnp.where(lane < 4 + 2 * width, end, 0.0))
    out_ref[...] = value


def relax_kernel(rows, cols, ny, nx, own_ref, even_ref, odd_ref, mesh_ref, earlier_ref):
    section, y, x, _ = where_am_i()
    above, below = around(y, ny, even_ref[...], odd_ref[...])
    own = own_ref[...]
    tall = rows + 4
    shape = (tall, PATCH)
    row = lax.broadcasted_iota(jnp.int32, shape, 0) - 2 + y * rows
    col = lax.broadcasted_iota(jnp.int32, shape, 1) - 2 + x * cols
    inside = (row >= 0) & (row < ny * rows) & (col >= 0) & (col < nx * cols)

    def step(mesh, flow):
        nearby = (
            pltpu.roll(mesh, 1, 0) + pltpu.roll(mesh, tall - 1, 0)
            + pltpu.roll(mesh, 1, 1) + pltpu.roll(mesh, PATCH - 1, 1)
        )
        lap = nearby - 4.0 * mesh
        return jnp.where(inside, mesh + rate * (stiffness * lap + flow - mesh), 0.0)

    for c in range(2):
        flow = jnp.concatenate(
            [above[(c + 1) * rows - 2:(c + 1) * rows], own[c * rows:(c + 1) * rows],
             below[c * rows:c * rows + 2]], axis=0)
        flow = jnp.where(inside, flow, 0.0)
        mesh = step(step(flow, flow), flow)
        mesh = pltpu.roll(pltpu.roll(mesh, tall - 2, 0), PATCH - 2, 1)[:rows, :cols]
        mesh_ref[0, c] = jnp.where(section == 0, mesh, 0.0)
        earlier_ref[0, c] = jnp.where(section == 0, 0.0, mesh)


def shared_section(images):
    tile = images[0]
    ny, nx = lax.axis_size("ty"), lax.axis_size("tx")
    rows, cols = tile.shape[0] // STRIDE, tile.shape[1] // STRIDE
    half = cols // 2
    core, tall = half * STRIDE + HALF, tile.shape[0]

    wide = 2 * HALF * core // PATCH
    strip = floats(wide, PATCH)
    frame, rest = kernel_call(
        functools.partial(cut_kernel, core),
        (floats(wide + (tall - 2 * HALF) // 4, PATCH), floats(tall - 2 * HALF, core - HALF)), tile,
    )
    frame, rest = along(frame, mate), along(rest, mate)
    even, odd = kernel_call(functools.partial(strips_kernel, core), (strip, strip), tile, frame)
    even, odd = pairs_even(even), pairs_odd(odd)
    sides = kernel_call(
        functools.partial(sides_kernel, core, ny), floats((tall + 2 * HALF) // 2, PATCH),
        tile, frame, even, odd,
    )
    sides = along(sides, near)
    flow = kernel_call(
        functools.partial(shared_kernel, rows, half, 4, ny, nx), floats(2 * rows, PATCH),
        tile, frame, rest, even, odd, sides, *tables(),
        scratch=region_scratch(rows, half) + [pltpu.VMEM(half_shape(rows, half), jnp.float32)] * 2
        + stats_scratch(rows, half),
    )
    window = kernel_call(
        functools.partial(window_kernel, half, nx), floats(*flow.shape),
        flow, along(flow, mate), along(flow, near), along(flow, far),
    )
    out = floats(1, 2, rows, cols)
    return kernel_call(
        functools.partial(relax_kernel, rows, cols, ny, nx), (out, out),
        window, pairs_even(window), pairs_odd(window), last=True,
    )


def solution(mesh):
    in_specs = (P("sec", "ty", "tx"),)
    out_specs = (P("sec", None, "ty", "tx"), P("sec", None, "ty", "tx"))
    even = mesh.shape["ty"] % 2 == 0 and mesh.shape["tx"] % 2 == 0
    shared = mesh.shape["sec"] == 2 and even

    def body(images):
        return (shared_section if shared else whole_sections)(images)

    return jax.shard_map(body, mesh=mesh, in_specs=in_specs, out_specs=out_specs, check_vma=False)
```

```python
import functools

import jax
import jax.numpy as jnp
import numpy as np
from jax import lax
from jax.experimental import pallas as pl
from jax.experimental.pallas import tpu as pltpu
from jax.sharding import PartitionSpec as P


PATCH = 128
STRIDE = 64
HALF = STRIDE // 2
FREQ = -(-(PATCH // 2 + 1) // 8) * 8

stiffness = 1.0
rate = 0.25


def two_parts(table):
    high = table.astype(jnp.bfloat16)
    low = (table - high.astype(np.float64)).astype(jnp.bfloat16)
    return high, low


def tables():
    angle = 2.0 * np.pi * (np.outer(np.arange(PATCH), np.arange(PATCH)) % PATCH) / PATCH
    cosine, sine = np.cos(angle), np.sin(angle)
    kept = np.arange(FREQ)[:, None] <= PATCH // 2
    left = np.concatenate([cosine[:FREQ] * kept, -sine[:FREQ] * kept])
    right = np.block([[cosine, -sine], [sine, cosine]])
    share = np.where((np.arange(FREQ) == 0) | (np.arange(FREQ) == PATCH // 2), 1.0, 2.0)
    scaled = (share * kept[:, 0])[None, :] / float(PATCH) ** 3
    back = np.concatenate([cosine[:, :FREQ] * scaled, sine[:, :FREQ] * scaled], axis=1)
    left_hi, left_lo = two_parts(left)
    back_hi, back_lo = two_parts(back)
    right_hi, right_lo = two_parts(right)
    return (
        np.concatenate([left_hi, left_hi, left_lo], axis=1),
        np.stack([right_hi, right_lo]),
        np.concatenate([back_hi, back_hi, back_lo], axis=1),
    )


def split(values):
    high = values.astype(jnp.bfloat16)
    return high, (values - high.astype(jnp.float32)).astype(jnp.bfloat16)


def mul(a, b):
    return jnp.dot(a, b, preferred_element_type=jnp.float32)


def right_dft(values, right_ref):
    high, low = split(values)
    return mul(high, right_ref[0]) + mul(low, right_ref[0]) + mul(high, right_ref[1])


def node_order(cols):
    return [2 * t for t in range(cols // 2)] + [2 * t + 1 for t in range(cols // 2)]


def keep_region(region, wide, high_ref, low_ref):
    even, odd = region[:, :wide], region[:, STRIDE:STRIDE + wide]
    for part, values in enumerate((even, odd)):
        high, low = split(values)
        high_ref[:, part * wide:(part + 1) * wide] = high
        low_ref[:, part * wide:(part + 1) * wide] = low


def left_dft(cols, bands, high_ref, low_ref, left_ref, half_ref):
    for k, i in enumerate(bands):
        band = pl.ds(i * STRIDE, PATCH)
        high = high_ref[band, :]
        stacked = jnp.concatenate([high, low_ref[band, :], high], axis=0)
        out = mul(left_ref[...], stacked)
        for t, j in enumerate(node_order(cols)):
            lanes = slice(t * PATCH, (t + 1) * PATCH)
            half_ref[k * cols + j, :, :PATCH] = out[:FREQ, lanes]
            half_ref[k * cols + j, :, PATCH:] = out[FREQ:, lanes]


def correlate(rows, cols, group, sign, own_ref, other_ref, right_ref, back_ref, put,
              peak_ref, mass_ref, tilt_ref):
    row = lax.broadcasted_iota(jnp.int32, (group, FREQ, PATCH), 1)
    lane = lax.broadcasted_iota(jnp.int32, (group, FREQ, PATCH), 2)
    varies = ((row + lane) > 0).astype(jnp.float32).reshape(group * FREQ, PATCH)
    lag = lax.broadcasted_iota(jnp.int32, (PATCH, 1), 0)
    lag = jnp.where(lag < PATCH // 2, lag, lag - PATCH).astype(jnp.float32)
    for n in range(0, rows * cols, group):
        both = jnp.concatenate([ref[n:n + group].reshape(group * FREQ, 2 * PATCH) for ref in (own_ref, other_ref)])
        freq = right_dft(both, right_ref)
        first, second = freq[:group * FREQ], freq[group * FREQ:]
        re1, im1 = first[:, :PATCH] * varies, first[:, PATCH:] * varies
        re2, im2 = second[:, :PATCH] * varies, second[:, PATCH:] * varies
        cross = jnp.concatenate([re1 * re2 + im1 * im2, (im1 * re2 - re1 * im2) * sign], axis=1)
        mixed = right_dft(cross, right_ref)
        columns = []
        for m in range(group):
            part = mixed[m * FREQ:(m + 1) * FREQ]
            columns.append(jnp.concatenate([part[:, :PATCH], part[:, PATCH:]], axis=0))
        high, low = split(jnp.concatenate(columns, axis=1))
        scores = mul(back_ref[...], jnp.concatenate([high, low, high], axis=0))
        peak = jnp.max(scores, axis=0, keepdims=True)
        weight = jnp.exp(scores - peak)
        mass = jnp.sum(weight, axis=0, keepdims=True)
        tilt = jnp.sum(weight * lag, axis=0, keepdims=True)
        for m in range(group):
            lanes = slice(m * PATCH, (m + 1) * PATCH)
            peak_ref[n + m:n + m + 1, :] = peak[:, lanes]
            mass_ref[n + m:n + m + 1, :] = mass[:, lanes]
            tilt_ref[n + m:n + m + 1, :] = tilt[:, lanes]
    peak = peak_ref[...]
    share = jnp.exp(peak - jnp.max(peak, axis=1, keepdims=True))
    mass = mass_ref[...] * share
    lag = lax.broadcasted_iota(jnp.int32, mass.shape, 1)
    place = lax.broadcasted_iota(jnp.int32, mass.shape, 0) % cols
    here = lag == place
    lag = jnp.where(lag < PATCH // 2, lag, lag - PATCH).astype(jnp.float32)
    total = jnp.sum(mass, axis=1, keepdims=True)
    flow_y = jnp.sum(tilt_ref[...] * share, axis=1, keepdims=True) / total
    flow_x = jnp.sum(mass * lag, axis=1, keepdims=True) / total
    for c, value in enumerate((flow_y, flow_x)):
        spread = jnp.where(here, value, 0.0)
        for i in range(rows):
            put(c, i, jnp.sum(spread[i * cols:(i + 1) * cols], axis=0, keepdims=True))


def flow_kernel(rows, cols, group, region_ref, left_ref, right_ref, back_ref, flow_ref,
                high_ref, low_ref, own_ref, other_ref, *stats):
    for z, half_ref in enumerate((own_ref, other_ref)):
        keep_region(region_ref[z], cols * STRIDE, high_ref, low_ref)
        left_dft(cols, range(rows), high_ref, low_ref, left_ref, half_ref)

    def put(c, i, row):
        flow_ref[c * rows + i:c * rows + i + 1, :] = row

    correlate(rows, cols, group, 1.0, own_ref, other_ref, right_ref, back_ref, put, *stats)


def region_scratch(rows, cols):
    return [pltpu.VMEM(((rows + 1) * STRIDE, 2 * cols * STRIDE), jnp.bfloat16)] * 2


def half_shape(rows, cols):
    return (rows * cols, FREQ, 2 * PATCH)


def stats_scratch(rows, cols):
    return [pltpu.VMEM((rows * cols, PATCH), jnp.float32)] * 3


IN_VMEM = pl.BlockSpec(memory_space=pltpu.VMEM)


def kernel_call(body, outs, *args, scratch=(), last=False):
    args = [pltpu.with_memory_space_constraint(a, pltpu.VMEM) if isinstance(a, jax.Array) else a for a in args]
    shapes = outs if last else jax.tree.map(lambda out: pltpu.VMEM(out.shape, out.dtype), outs)
    return pl.pallas_call(
        body,
        out_shape=shapes,
        in_specs=[IN_VMEM] * len(args),
        out_specs=jax.tree.map(lambda _: IN_VMEM, outs),
        scratch_shapes=scratch,
        compiler_params=pltpu.CompilerParams(vmem_limit_bytes=24 << 20),
    )(*args)


def floats(*shape):
    return jax.ShapeDtypeStruct(shape, jnp.float32)


def flow_of(region, rows, cols, group=4):
    return kernel_call(
        functools.partial(flow_kernel, rows, cols, group),
        floats(2 * rows, PATCH), region, *tables(),
        scratch=region_scratch(rows, cols) + [pltpu.VMEM(half_shape(rows, cols), jnp.float32)] * 2
        + stats_scratch(rows, cols),
    )


def shifted(value, axis, by):
    length = lax.axis_size(axis)
    pairs = [(i, i + by) for i in range(length) if 0 <= i + by < length]
    return lax.ppermute(value, axis, pairs)


def padded_2(value, sides, width):
    for axis, dim in sides:
        size, length = (lax.axis_size(axis), value.shape[dim])
        up = [(i, (i + 1) % size) for i in range(size - 1)]
        down = [(j, i) for i, j in up]
        last = lax.slice_in_dim(value, length - width, length, axis=dim)
        first = lax.slice_in_dim(value, 0, width, axis=dim)
        before = lax.ppermute(last, axis, up)
        after = lax.ppermute(first, axis, down)
        value = jnp.concatenate([before, value, after], axis=dim)
    return value


def lap_of(padded, center):
    return (
        padded[:, :-2, 1:-1]
        + padded[:, 2:, 1:-1]
        + padded[:, 1:-1, :-2]
        + padded[:, 1:-1, 2:]
        - 4.0 * center
    )


def whole_sections(images):
    tile = images[0]
    rows, cols = tile.shape[0] // STRIDE, tile.shape[1] // STRIDE
    region = padded_2(jnp.stack([tile, shifted(tile, "sec", -1)]), (("ty", 1), ("tx", 2)), HALF)
    flow = flow_of(region, rows, cols)[:, :cols].reshape(2, rows, cols)
    keep = (lax.axis_index("sec") < lax.axis_size("sec") - 1).astype(jnp.float32)
    flow = flow * keep
    padded = padded_2(flow, (("ty", 1), ("tx", 2)), 2)
    inner = padded[:, 1:-1, 1:-1]
    first = inner + rate * (stiffness * lap_of(padded, inner) + inner - inner)
    row_ids = lax.axis_index("ty") * rows + jnp.arange(-1, rows + 1, dtype=jnp.int32)
    col_ids = lax.axis_index("tx") * cols + jnp.arange(-1, cols + 1, dtype=jnp.int32)
    row_ok = (row_ids >= 0) & (row_ids < rows * lax.axis_size("ty"))
    col_ok = (col_ids >= 0) & (col_ids < cols * lax.axis_size("tx"))
    first = first * (row_ok[:, None] & col_ok[None, :]).astype(jnp.float32)[None]
    center = first[:, 1:-1, 1:-1]
    mesh = center + rate * (stiffness * lap_of(first, center) + flow - center)
    everything = lax.all_gather(mesh, "sec")
    earlier = jnp.arange(lax.axis_size("sec")) < lax.axis_index("sec")
    before = jnp.sum(jnp.where(earlier[:, None, None, None], everything, 0.0), axis=0)
    return (mesh[None], before[None])


AXES = ("sec", "ty", "tx")


def placed(half, y, x):
    ny, nx = lax.axis_size("ty"), lax.axis_size("tx")
    return (((half + x) % 2) * ny + y) * nx + x


def along(value, step):
    ny, nx = lax.axis_size("ty"), lax.axis_size("tx")
    pairs = []
    for y in range(ny):
        for g in range(2 * nx):
            to = step(g) % (2 * nx)
            pairs.append((placed(g % 2, y, g // 2), placed(to % 2, y, to // 2)))
    return lax.ppermute(value, AXES, pairs)


def mate(g):
    return g ^ 1


def near(g):
    return g - 1 if g % 2 == 0 else g + 1


def far(g):
    return g - 2 if g % 2 == 0 else g + 2


def past(g):
    return g + 2 if g % 2 == 0 else g - 2


def pairs_even(value):
    size = lax.axis_size("ty")
    return lax.ppermute(value, "ty", [(i, i ^ 1) for i in range(size)])


def pairs_odd(value):
    size = lax.axis_size("ty")
    return lax.ppermute(value, "ty", [(i, (i - 1 if i % 2 == 0 else i + 1) % size) for i in range(size)])


def around(y, ny, even, odd):
    lower = y % 2 == 1
    above = jnp.where(y == 0, 0.0, jnp.where(lower, even, odd))
    below = jnp.where(y == ny - 1, 0.0, jnp.where(lower, odd, even))
    return above, below


def where_am_i():
    section, y, x = lax.axis_index("sec"), lax.axis_index("ty"), lax.axis_index("tx")
    return section, y, x, (section + x) % 2


def packed(column):
    quarter = column.shape[0] // 4
    return jnp.concatenate([column[q * quarter:(q + 1) * quarter] for q in range(4)], axis=1)


def unpacked(block):
    return jnp.concatenate([block[:, q * HALF:(q + 1) * HALF] for q in range(4)], axis=0)


def packed_wide(value):
    full = value.shape[1] // PATCH
    tiles = [value[:, t * PATCH:(t + 1) * PATCH] for t in range(full)]
    return jnp.concatenate(tiles + [packed(value[:, full * PATCH:])], axis=0)


def unpacked_wide(block, tall, width):
    full = width // PATCH
    tiles = [block[t * tall:(t + 1) * tall] for t in range(full)]
    return jnp.concatenate(tiles + [unpacked(block[full * tall:full * tall + tall // 4])], axis=1)


def own_lanes(half, core, width):
    return slice(0, core) if half == 0 else slice(width - core, width)


def by_half(half, branch):
    for h in range(2):
        pl.when(half == h)(functools.partial(branch, h))


def cut_kernel(core, tile_ref, other_ref, even_ref, odd_ref):
    _, y, _, half = where_am_i()
    tall, width = tile_ref.shape
    lower = y % 2 == 1
    first, last = tile_ref[:HALF], tile_ref[tall - HALF:]
    even_ref[...] = jnp.where(lower, first, last)
    odd_ref[...] = jnp.where(lower, last, first)

    def branch(h):
        other_ref[...] = packed_wide(tile_ref[:, own_lanes(1 - h, core, width)])

    by_half(half, branch)


def borders_kernel(core, ny, tile_ref, even_ref, odd_ref, strips_ref, near_ref, past_ref):
    _, y, _, half = where_am_i()
    width = tile_ref.shape[1]
    above, below = around(y, ny, even_ref[...], odd_ref[...])

    def column(lanes):
        return packed(jnp.concatenate([above[:, lanes], tile_ref[:, lanes], below[:, lanes]], axis=0))

    first, last = column(slice(0, HALF)), column(slice(width - HALF, width))

    def branch(h):
        lanes = own_lanes(1 - h, core, width)
        strips_ref[...] = packed_wide(jnp.concatenate([above[:, lanes], below[:, lanes]], axis=0))
        near_ref[...], past_ref[...] = (first, last) if h == 0 else (last, first)

    by_half(half, branch)


def keep_half(half, x, nx, cols, side_ref, values, high_ref, low_ref):
    at_end = jnp.where(half == 0, x == 0, x == nx - 1)
    side = jnp.where(at_end, 0.0, unpacked(side_ref[...]))

    def branch(h):
        value = jnp.concatenate([side, values(h)] if h == 0 else [values(h), side], axis=1)
        keep_region(value, cols * STRIDE, high_ref, low_ref)

    by_half(half, branch)


def own_kernel(rows, cols, ny, nx, tile_ref, even_ref, odd_ref, side_ref, left_ref, half_ref, high_ref, low_ref):
    _, y, x, half = where_am_i()
    width, core = tile_ref.shape[1], cols * STRIDE + HALF
    above, below = around(y, ny, even_ref[...], odd_ref[...])

    def values(h):
        lanes = own_lanes(h, core, width)
        return jnp.concatenate([above[:, lanes], tile_ref[:, lanes], below[:, lanes]], axis=0)

    keep_half(half, x, nx, cols, side_ref, values, high_ref, low_ref)
    left_dft(cols, range(rows), high_ref, low_ref, left_ref, half_ref)


def pair_kernel(rows, cols, group, nx, own_ref, other_ref, strips_ref, cross_ref,
                left_ref, right_ref, back_ref, flow_ref, high_ref, low_ref, half_ref, *stats):
    section, _, x, half = where_am_i()
    core = cols * STRIDE + HALF
    strips = unpacked_wide(strips_ref[...], 2 * HALF, core)
    middle = unpacked_wide(other_ref[...], rows * STRIDE, core)
    value = jnp.concatenate([strips[:HALF], middle, strips[HALF:]], axis=0)
    keep_half(half, x, nx, cols, cross_ref, lambda h: value, high_ref, low_ref)
    left_dft(cols, range(rows), high_ref, low_ref, left_ref, half_ref)

    def put(c, i, row):
        flow_ref[c * rows + i:c * rows + i + 1, :] = row

    sign = jnp.where(section == 0, 1.0, -1.0)
    correlate(rows, cols, group, sign, own_ref, half_ref, right_ref, back_ref, put, *stats)


def window_kernel(width, nx, own_ref, mate_ref, near_ref, far_ref, out_ref):
    _, _, x, place = where_am_i()
    half = place == 1
    own, other, close, beyond = own_ref[...], mate_ref[...], near_ref[...], far_ref[...]
    lane = lax.broadcasted_iota(jnp.int32, own.shape, 1)
    begin = jnp.where(x == 0, 0.0, jnp.where(half, beyond, close))
    left = jnp.where(half, other, own)
    right = jnp.where(half, own, other)
    end = jnp.where(x == nx - 1, 0.0, jnp.where(half, close, beyond))
    begin, left = pltpu.roll(begin, PATCH + 2 - width, 1), pltpu.roll(left, 2, 1)
    right, end = pltpu.roll(right, 2 + width, 1), pltpu.roll(end, 2 + 2 * width, 1)
    value = jnp.where(lane < 2, begin, jnp.where(lane < 2 + width, left, right))
    value = jnp.where(lane < 2 + 2 * width, value, jnp.where(lane < 4 + 2 * width, end, 0.0))
    out_ref[...] = value


def relax_kernel(rows, cols, ny, nx, own_ref, even_ref, odd_ref, mesh_ref, earlier_ref):
    section, y, x, _ = where_am_i()
    above, below = around(y, ny, even_ref[...], odd_ref[...])
    own = own_ref[...]
    tall = rows + 4
    shape = (tall, PATCH)
    row = lax.broadcasted_iota(jnp.int32, shape, 0) - 2 + y * rows
    col = lax.broadcasted_iota(jnp.int32, shape, 1) - 2 + x * cols
    inside = (row >= 0) & (row < ny * rows) & (col >= 0) & (col < nx * cols)

    def step(mesh, flow):
        nearby = (
            pltpu.roll(mesh, 1, 0) + pltpu.roll(mesh, tall - 1, 0)
            + pltpu.roll(mesh, 1, 1) + pltpu.roll(mesh, PATCH - 1, 1)
        )
        lap = nearby - 4.0 * mesh
        return jnp.where(inside, mesh + rate * (stiffness * lap + flow - mesh), 0.0)

    for c in range(2):
        flow = jnp.concatenate(
            [above[(c + 1) * rows - 2:(c + 1) * rows], own[c * rows:(c + 1) * rows],
             below[c * rows:c * rows + 2]], axis=0)
        flow = jnp.where(inside, flow, 0.0)
        mesh = step(step(flow, flow), flow)
        mesh = pltpu.roll(pltpu.roll(mesh, tall - 2, 0), PATCH - 2, 1)[:rows, :cols]
        mesh_ref[0, c] = jnp.where(section == 0, mesh, 0.0)
        earlier_ref[0, c] = jnp.where(section == 0, 0.0, mesh)


def shared_section(images):
    tile = images[0]
    ny, nx = lax.axis_size("ty"), lax.axis_size("tx")
    rows, cols = tile.shape[0] // STRIDE, tile.shape[1] // STRIDE
    half = cols // 2
    core, tall = half * STRIDE + HALF, tile.shape[0]

    strip = floats(HALF, tile.shape[1])
    other, even, odd = kernel_call(
        functools.partial(cut_kernel, core), (floats(tall * core // PATCH, PATCH), strip, strip), tile,
    )
    other = along(other, mate)
    even, odd = pairs_even(even), pairs_odd(odd)
    edge = floats((tall + 2 * HALF) // 4, PATCH)
    strips, side, cross = kernel_call(
        functools.partial(borders_kernel, core, ny), (floats(2 * HALF * core // PATCH, PATCH), edge, edge),
        tile, even, odd,
    )
    side, cross = along(side, near), along(cross, past)
    strips = along(strips, mate)
    left, right, back = tables()
    spectra = half_shape(rows, half)
    own = kernel_call(
        functools.partial(own_kernel, rows, half, ny, nx), floats(*spectra), tile, even, odd, side, left,
        scratch=region_scratch(rows, half),
    )
    flow = kernel_call(
        functools.partial(pair_kernel, rows, half, 4, nx), floats(2 * rows, PATCH),
        own, other, strips, cross, left, right, back,
        scratch=region_scratch(rows, half) + [pltpu.VMEM(spectra, jnp.float32)] + stats_scratch(rows, half),
    )
    window = kernel_call(
        functools.partial(window_kernel, half, nx), floats(*flow.shape),
        flow, along(flow, mate), along(flow, near), along(flow, far),
    )
    out = floats(1, 2, rows, cols)
    return kernel_call(
        functools.partial(relax_kernel, rows, cols, ny, nx), (out, out),
        window, pairs_even(window), pairs_odd(window), last=True,
    )


def solution(mesh):
    in_specs = (P("sec", "ty", "tx"),)
    out_specs = (P("sec", None, "ty", "tx"), P("sec", None, "ty", "tx"))
    even = mesh.shape["ty"] % 2 == 0 and mesh.shape["tx"] % 2 == 0
    shared = mesh.shape["sec"] == 2 and even

    def body(images):
        return (shared_section if shared else whole_sections)(images)

    return jax.shard_map(body, mesh=mesh, in_specs=in_specs, out_specs=out_specs, check_vma=False)
```

```python
import functools

import jax
import jax.numpy as jnp
import numpy as np
from jax import lax
from jax.experimental import pallas as pl
from jax.experimental.pallas import tpu as pltpu
from jax.sharding import PartitionSpec as P


PATCH = 128
STRIDE = 64
HALF = STRIDE // 2
FREQ = -(-(PATCH // 2 + 1) // 8) * 8

stiffness = 1.0
rate = 0.25


def two_parts(table):
    high = table.astype(jnp.bfloat16)
    low = (table - high.astype(np.float64)).astype(jnp.bfloat16)
    return high, low


def tables():
    angle = 2.0 * np.pi * (np.outer(np.arange(PATCH), np.arange(PATCH)) % PATCH) / PATCH
    cosine, sine = np.cos(angle), np.sin(angle)
    kept = np.arange(FREQ)[:, None] <= PATCH // 2
    left = np.concatenate([cosine[:FREQ] * kept, -sine[:FREQ] * kept])
    right = np.block([[cosine, -sine], [sine, cosine]])
    share = np.where((np.arange(FREQ) == 0) | (np.arange(FREQ) == PATCH // 2), 1.0, 2.0)
    scaled = (share * kept[:, 0])[None, :] / float(PATCH) ** 3
    back = np.concatenate([cosine[:, :FREQ] * scaled, sine[:, :FREQ] * scaled], axis=1)
    left_hi, left_lo = two_parts(left)
    back_hi, back_lo = two_parts(back)
    right_hi, right_lo = two_parts(right)
    return (
        np.concatenate([left_hi, left_hi, left_lo], axis=1),
        np.stack([right_hi, right_lo]),
        np.concatenate([back_hi, back_hi, back_lo], axis=1),
    )


def split(values):
    high = values.astype(jnp.bfloat16)
    return high, (values - high.astype(jnp.float32)).astype(jnp.bfloat16)


def mul(a, b):
    return jnp.dot(a, b, preferred_element_type=jnp.float32)


def right_dft(values, right_ref):
    high, low = split(values)
    return mul(high, right_ref[0]) + mul(low, right_ref[0]) + mul(high, right_ref[1])


def node_order(cols):
    return [2 * t for t in range(cols // 2)] + [2 * t + 1 for t in range(cols // 2)]


def keep_region(region, wide, high_ref, low_ref):
    even, odd = region[:, :wide], region[:, STRIDE:STRIDE + wide]
    for part, values in enumerate((even, odd)):
        high, low = split(values)
        high_ref[:, part * wide:(part + 1) * wide] = high
        low_ref[:, part * wide:(part + 1) * wide] = low


def left_dft(cols, bands, high_ref, low_ref, left_ref, half_ref):
    for k, i in enumerate(bands):
        band = pl.ds(i * STRIDE, PATCH)
        high = high_ref[band, :]
        stacked = jnp.concatenate([high, low_ref[band, :], high], axis=0)
        out = mul(left_ref[...], stacked)
        for t, j in enumerate(node_order(cols)):
            lanes = slice(t * PATCH, (t + 1) * PATCH)
            half_ref[k * cols + j, :, :PATCH] = out[:FREQ, lanes]
            half_ref[k * cols + j, :, PATCH:] = out[FREQ:, lanes]


def correlate(rows, cols, group, sign, own_ref, other_ref, right_ref, back_ref, put,
              peak_ref, mass_ref, tilt_ref):
    row = lax.broadcasted_iota(jnp.int32, (group, FREQ, PATCH), 1)
    lane = lax.broadcasted_iota(jnp.int32, (group, FREQ, PATCH), 2)
    varies = ((row + lane) > 0).astype(jnp.float32).reshape(group * FREQ, PATCH)
    lag = lax.broadcasted_iota(jnp.int32, (PATCH, 1), 0)
    lag = jnp.where(lag < PATCH // 2, lag, lag - PATCH).astype(jnp.float32)
    for n in range(0, rows * cols, group):
        both = jnp.concatenate([ref[n:n + group].reshape(group * FREQ, 2 * PATCH) for ref in (own_ref, other_ref)])
        freq = right_dft(both, right_ref)
        first, second = freq[:group * FREQ], freq[group * FREQ:]
        re1, im1 = first[:, :PATCH] * varies, first[:, PATCH:] * varies
        re2, im2 = second[:, :PATCH] * varies, second[:, PATCH:] * varies
        cross = jnp.concatenate([re1 * re2 + im1 * im2, (im1 * re2 - re1 * im2) * sign], axis=1)
        mixed = right_dft(cross, right_ref)
        columns = []
        for m in range(group):
            part = mixed[m * FREQ:(m + 1) * FREQ]
            columns.append(jnp.concatenate([part[:, :PATCH], part[:, PATCH:]], axis=0))
        high, low = split(jnp.concatenate(columns, axis=1))
        scores = mul(back_ref[...], jnp.concatenate([high, low, high], axis=0))
        peak = jnp.max(scores, axis=0, keepdims=True)
        weight = jnp.exp(scores - peak)
        mass = jnp.sum(weight, axis=0, keepdims=True)
        tilt = jnp.sum(weight * lag, axis=0, keepdims=True)
        for m in range(group):
            lanes = slice(m * PATCH, (m + 1) * PATCH)
            peak_ref[n + m:n + m + 1, :] = peak[:, lanes]
            mass_ref[n + m:n + m + 1, :] = mass[:, lanes]
            tilt_ref[n + m:n + m + 1, :] = tilt[:, lanes]
    peak = peak_ref[...]
    share = jnp.exp(peak - jnp.max(peak, axis=1, keepdims=True))
    mass = mass_ref[...] * share
    lag = lax.broadcasted_iota(jnp.int32, mass.shape, 1)
    place = lax.broadcasted_iota(jnp.int32, mass.shape, 0) % cols
    here = lag == place
    lag = jnp.where(lag < PATCH // 2, lag, lag - PATCH).astype(jnp.float32)
    total = jnp.sum(mass, axis=1, keepdims=True)
    flow_y = jnp.sum(tilt_ref[...] * share, axis=1, keepdims=True) / total
    flow_x = jnp.sum(mass * lag, axis=1, keepdims=True) / total
    for c, value in enumerate((flow_y, flow_x)):
        spread = jnp.where(here, value, 0.0)
        for i in range(rows):
            put(c, i, jnp.sum(spread[i * cols:(i + 1) * cols], axis=0, keepdims=True))


def flow_kernel(rows, cols, group, region_ref, left_ref, right_ref, back_ref, flow_ref,
                high_ref, low_ref, own_ref, other_ref, *stats):
    for z, half_ref in enumerate((own_ref, other_ref)):
        keep_region(region_ref[z], cols * STRIDE, high_ref, low_ref)
        left_dft(cols, range(rows), high_ref, low_ref, left_ref, half_ref)

    def put(c, i, row):
        flow_ref[c * rows + i:c * rows + i + 1, :] = row

    correlate(rows, cols, group, 1.0, own_ref, other_ref, right_ref, back_ref, put, *stats)


def region_scratch(rows, cols):
    return [pltpu.VMEM(((rows + 1) * STRIDE, 2 * cols * STRIDE), jnp.bfloat16)] * 2


def half_shape(rows, cols):
    return (rows * cols, FREQ, 2 * PATCH)


def stats_scratch(rows, cols):
    return [pltpu.VMEM((rows * cols, PATCH), jnp.float32)] * 3


IN_VMEM = pl.BlockSpec(memory_space=pltpu.VMEM)


def kernel_call(body, outs, *args, scratch=(), first=False, last=False):
    place = pltpu.HBM if first else pltpu.VMEM
    args = [pltpu.with_memory_space_constraint(a, place) if isinstance(a, jax.Array) else a for a in args]
    shapes = outs if last else jax.tree.map(lambda out: pltpu.VMEM(out.shape, out.dtype), outs)
    return pl.pallas_call(
        body,
        out_shape=shapes,
        in_specs=[pl.BlockSpec(memory_space=place)] * len(args),
        out_specs=jax.tree.map(lambda _: IN_VMEM, outs),
        scratch_shapes=scratch,
        compiler_params=pltpu.CompilerParams(vmem_limit_bytes=24 << 20),
    )(*args)


def floats(*shape):
    return jax.ShapeDtypeStruct(shape, jnp.float32)


def flow_of(region, rows, cols, group=16):
    return kernel_call(
        functools.partial(flow_kernel, rows, cols, group),
        floats(2 * rows, PATCH), region, *tables(),
        scratch=region_scratch(rows, cols) + [pltpu.VMEM(half_shape(rows, cols), jnp.float32)] * 2
        + stats_scratch(rows, cols),
    )


def shifted(value, axis, by):
    length = lax.axis_size(axis)
    pairs = [(i, i + by) for i in range(length) if 0 <= i + by < length]
    return lax.ppermute(value, axis, pairs)


def padded_2(value, sides, width):
    for axis, dim in sides:
        size, length = (lax.axis_size(axis), value.shape[dim])
        up = [(i, (i + 1) % size) for i in range(size - 1)]
        down = [(j, i) for i, j in up]
        last = lax.slice_in_dim(value, length - width, length, axis=dim)
        first = lax.slice_in_dim(value, 0, width, axis=dim)
        before = lax.ppermute(last, axis, up)
        after = lax.ppermute(first, axis, down)
        value = jnp.concatenate([before, value, after], axis=dim)
    return value


def lap_of(padded, center):
    return (
        padded[:, :-2, 1:-1]
        + padded[:, 2:, 1:-1]
        + padded[:, 1:-1, :-2]
        + padded[:, 1:-1, 2:]
        - 4.0 * center
    )


def whole_sections(images):
    tile = images[0]
    rows, cols = tile.shape[0] // STRIDE, tile.shape[1] // STRIDE
    region = padded_2(jnp.stack([tile, shifted(tile, "sec", -1)]), (("ty", 1), ("tx", 2)), HALF)
    flow = flow_of(region, rows, cols)[:, :cols].reshape(2, rows, cols)
    keep = (lax.axis_index("sec") < lax.axis_size("sec") - 1).astype(jnp.float32)
    flow = flow * keep
    padded = padded_2(flow, (("ty", 1), ("tx", 2)), 2)
    inner = padded[:, 1:-1, 1:-1]
    first = inner + rate * (stiffness * lap_of(padded, inner) + inner - inner)
    row_ids = lax.axis_index("ty") * rows + jnp.arange(-1, rows + 1, dtype=jnp.int32)
    col_ids = lax.axis_index("tx") * cols + jnp.arange(-1, cols + 1, dtype=jnp.int32)
    row_ok = (row_ids >= 0) & (row_ids < rows * lax.axis_size("ty"))
    col_ok = (col_ids >= 0) & (col_ids < cols * lax.axis_size("tx"))
    first = first * (row_ok[:, None] & col_ok[None, :]).astype(jnp.float32)[None]
    center = first[:, 1:-1, 1:-1]
    mesh = center + rate * (stiffness * lap_of(first, center) + flow - center)
    everything = lax.all_gather(mesh, "sec")
    earlier = jnp.arange(lax.axis_size("sec")) < lax.axis_index("sec")
    before = jnp.sum(jnp.where(earlier[:, None, None, None], everything, 0.0), axis=0)
    return (mesh[None], before[None])


AXES = ("sec", "ty", "tx")


def placed(half, y, x):
    ny, nx = lax.axis_size("ty"), lax.axis_size("tx")
    return (((half + x) % 2) * ny + y) * nx + x


def along(value, step):
    ny, nx = lax.axis_size("ty"), lax.axis_size("tx")
    pairs = []
    for y in range(ny):
        for g in range(2 * nx):
            to = step(g) % (2 * nx)
            pairs.append((placed(g % 2, y, g // 2), placed(to % 2, y, to // 2)))
    return lax.ppermute(value, AXES, pairs)


def mate(g):
    return g ^ 1


def near(g):
    return g - 1 if g % 2 == 0 else g + 1


def far(g):
    return g - 2 if g % 2 == 0 else g + 2


def past(g):
    return g + 2 if g % 2 == 0 else g - 2


def pairs_even(value):
    size = lax.axis_size("ty")
    return lax.ppermute(value, "ty", [(i, i ^ 1) for i in range(size)])


def pairs_odd(value):
    size = lax.axis_size("ty")
    return lax.ppermute(value, "ty", [(i, (i - 1 if i % 2 == 0 else i + 1) % size) for i in range(size)])


def around(y, ny, even, odd):
    lower = y % 2 == 1
    above = jnp.where(y == 0, 0.0, jnp.where(lower, even, odd))
    below = jnp.where(y == ny - 1, 0.0, jnp.where(lower, odd, even))
    return above, below


def where_am_i():
    section, y, x = lax.axis_index("sec"), lax.axis_index("ty"), lax.axis_index("tx")
    return section, y, x, (section + x) % 2


def packed(column):
    quarter = column.shape[0] // 4
    return jnp.concatenate([column[q * quarter:(q + 1) * quarter] for q in range(4)], axis=1)


def unpacked(block):
    return jnp.concatenate([block[:, q * HALF:(q + 1) * HALF] for q in range(4)], axis=0)


def packed_wide(value):
    full = value.shape[1] // PATCH
    tiles = [value[:, t * PATCH:(t + 1) * PATCH] for t in range(full)]
    return jnp.concatenate(tiles + [packed(value[:, full * PATCH:])], axis=0)


def unpacked_wide(block, tall, width):
    full = width // PATCH
    tiles = [block[t * tall:(t + 1) * tall] for t in range(full)]
    return jnp.concatenate(tiles + [unpacked(block[full * tall:full * tall + tall // 4])], axis=1)


def own_lanes(half, core, width):
    return slice(0, core) if half == 0 else slice(width - core, width)


def by_half(half, branch):
    for h in range(2):
        pl.when(half == h)(functools.partial(branch, h))


def cut_kernel(core, image_ref, tile_ref, other_ref, even_ref, odd_ref, sems):
    _, y, _, half = where_am_i()
    tall, width = tile_ref.shape
    copies = []
    for k in range(tall // HALF):
        rows = pl.ds(k * HALF, HALF)
        copies.append(pltpu.make_async_copy(image_ref.at[rows], tile_ref.at[rows], sems.at[k]))
    for copy in copies:
        copy.start()
    for copy in copies:
        copy.wait()
    lower = y % 2 == 1
    first, last = tile_ref[:HALF], tile_ref[tall - HALF:]
    even_ref[...] = jnp.where(lower, first, last)
    odd_ref[...] = jnp.where(lower, last, first)

    def branch(h):
        other_ref[...] = packed_wide(tile_ref[:, own_lanes(1 - h, core, width)])

    by_half(half, branch)


def borders_kernel(core, ny, tile_ref, even_ref, odd_ref, strips_ref, near_ref, past_ref):
    _, y, _, half = where_am_i()
    width = tile_ref.shape[1]
    above, below = around(y, ny, even_ref[...], odd_ref[...])

    def column(lanes):
        return packed(jnp.concatenate([above[:, lanes], tile_ref[:, lanes], below[:, lanes]], axis=0))

    first, last = column(slice(0, HALF)), column(slice(width - HALF, width))

    def branch(h):
        lanes = own_lanes(1 - h, core, width)
        strips_ref[...] = packed_wide(jnp.concatenate([above[:, lanes], below[:, lanes]], axis=0))
        near_ref[...], past_ref[...] = (first, last) if h == 0 else (last, first)

    by_half(half, branch)


def keep_half(half, x, nx, cols, side_ref, values, high_ref, low_ref):
    at_end = jnp.where(half == 0, x == 0, x == nx - 1)
    side = jnp.where(at_end, 0.0, unpacked(side_ref[...]))

    def branch(h):
        value = jnp.concatenate([side, values(h)] if h == 0 else [values(h), side], axis=1)
        keep_region(value, cols * STRIDE, high_ref, low_ref)

    by_half(half, branch)


def own_kernel(rows, cols, ny, nx, tile_ref, even_ref, odd_ref, side_ref, left_ref, half_ref, high_ref, low_ref):
    _, y, x, half = where_am_i()
    width, core = tile_ref.shape[1], cols * STRIDE + HALF
    above, below = around(y, ny, even_ref[...], odd_ref[...])

    def values(h):
        lanes = own_lanes(h, core, width)
        return jnp.concatenate([above[:, lanes], tile_ref[:, lanes], below[:, lanes]], axis=0)

    keep_half(half, x, nx, cols, side_ref, values, high_ref, low_ref)
    left_dft(cols, range(rows), high_ref, low_ref, left_ref, half_ref)


def pair_kernel(rows, cols, group, nx, own_ref, other_ref, strips_ref, cross_ref,
                left_ref, right_ref, back_ref, flow_ref, high_ref, low_ref, half_ref, *stats):
    section, _, x, half = where_am_i()
    core = cols * STRIDE + HALF
    strips = unpacked_wide(strips_ref[...], 2 * HALF, core)
    middle = unpacked_wide(other_ref[...], rows * STRIDE, core)
    value = jnp.concatenate([strips[:HALF], middle, strips[HALF:]], axis=0)
    keep_half(half, x, nx, cols, cross_ref, lambda h: value, high_ref, low_ref)
    left_dft(cols, range(rows), high_ref, low_ref, left_ref, half_ref)

    def put(c, i, row):
        flow_ref[c * rows + i:c * rows + i + 1, :] = row

    sign = jnp.where(section == 0, 1.0, -1.0)
    correlate(rows, cols, group, sign, own_ref, half_ref, right_ref, back_ref, put, *stats)


def window_kernel(width, nx, own_ref, mate_ref, near_ref, far_ref, out_ref):
    _, _, x, place = where_am_i()
    half = place == 1
    own, other, close, beyond = own_ref[...], mate_ref[...], near_ref[...], far_ref[...]
    lane = lax.broadcasted_iota(jnp.int32, own.shape, 1)
    begin = jnp.where(x == 0, 0.0, jnp.where(half, beyond, close))
    left = jnp.where(half, other, own)
    right = jnp.where(half, own, other)
    end = jnp.where(x == nx - 1, 0.0, jnp.where(half, close, beyond))
    begin, left = pltpu.roll(begin, PATCH + 2 - width, 1), pltpu.roll(left, 2, 1)
    right, end = pltpu.roll(right, 2 + width, 1), pltpu.roll(end, 2 + 2 * width, 1)
    value = jnp.where(lane < 2, begin, jnp.where(lane < 2 + width, left, right))
    value = jnp.where(lane < 2 + 2 * width, value, jnp.where(lane < 4 + 2 * width, end, 0.0))
    out_ref[...] = value


def relax_kernel(rows, cols, ny, nx, own_ref, even_ref, odd_ref, mesh_ref, earlier_ref):
    section, y, x, _ = where_am_i()
    above, below = around(y, ny, even_ref[...], odd_ref[...])
    own = own_ref[...]
    tall = rows + 4
    shape = (tall, PATCH)
    row = lax.broadcasted_iota(jnp.int32, shape, 0) - 2 + y * rows
    col = lax.broadcasted_iota(jnp.int32, shape, 1) - 2 + x * cols
    inside = (row >= 0) & (row < ny * rows) & (col >= 0) & (col < nx * cols)

    def step(mesh, flow):
        nearby = (
            pltpu.roll(mesh, 1, 0) + pltpu.roll(mesh, tall - 1, 0)
            + pltpu.roll(mesh, 1, 1) + pltpu.roll(mesh, PATCH - 1, 1)
        )
        lap = nearby - 4.0 * mesh
        return jnp.where(inside, mesh + rate * (stiffness * lap + flow - mesh), 0.0)

    for c in range(2):
        flow = jnp.concatenate(
            [above[(c + 1) * rows - 2:(c + 1) * rows], own[c * rows:(c + 1) * rows],
             below[c * rows:c * rows + 2]], axis=0)
        flow = jnp.where(inside, flow, 0.0)
        mesh = step(step(flow, flow), flow)
        mesh = pltpu.roll(pltpu.roll(mesh, tall - 2, 0), PATCH - 2, 1)[:rows, :cols]
        mesh_ref[0, c] = jnp.where(section == 0, mesh, 0.0)
        earlier_ref[0, c] = jnp.where(section == 0, 0.0, mesh)


def shared_section(images):
    tile = images[0]
    ny, nx = lax.axis_size("ty"), lax.axis_size("tx")
    rows, cols = tile.shape[0] // STRIDE, tile.shape[1] // STRIDE
    half = cols // 2
    core, tall = half * STRIDE + HALF, tile.shape[0]

    strip = floats(HALF, tile.shape[1])
    tile, other, even, odd = kernel_call(
        functools.partial(cut_kernel, core),
        (floats(*tile.shape), floats(tall * core // PATCH, PATCH), strip, strip), tile,
        scratch=[pltpu.SemaphoreType.DMA((tall // HALF,))], first=True,
    )
    other = along(other, mate)
    even, odd = pairs_even(even), pairs_odd(odd)
    edge = floats((tall + 2 * HALF) // 4, PATCH)
    strips, side, cross = kernel_call(
        functools.partial(borders_kernel, core, ny), (floats(2 * HALF * core // PATCH, PATCH), edge, edge),
        tile, even, odd,
    )
    side, cross = along(side, near), along(cross, past)
    strips = along(strips, mate)
    left, right, back = tables()
    spectra = half_shape(rows, half)
    own = kernel_call(
        functools.partial(own_kernel, rows, half, ny, nx), floats(*spectra), tile, even, odd, side, left,
        scratch=region_scratch(rows, half),
    )
    flow = kernel_call(
        functools.partial(pair_kernel, rows, half, rows * half, nx), floats(2 * rows, PATCH),
        own, other, strips, cross, left, right, back,
        scratch=region_scratch(rows, half) + [pltpu.VMEM(spectra, jnp.float32)] + stats_scratch(rows, half),
    )
    window = kernel_call(
        functools.partial(window_kernel, half, nx), floats(*flow.shape),
        flow, along(flow, mate), along(flow, near), along(flow, far),
    )
    out = floats(1, 2, rows, cols)
    return kernel_call(
        functools.partial(relax_kernel, rows, cols, ny, nx), (out, out),
        window, pairs_even(window), pairs_odd(window), last=True,
    )


def solution(mesh):
    in_specs = (P("sec", "ty", "tx"),)
    out_specs = (P("sec", None, "ty", "tx"), P("sec", None, "ty", "tx"))
    even = mesh.shape["ty"] % 2 == 0 and mesh.shape["tx"] % 2 == 0
    shared = mesh.shape["sec"] == 2 and even

    def body(images):
        return (shared_section if shared else whole_sections)(images)

    return jax.shard_map(body, mesh=mesh, in_specs=in_specs, out_specs=out_specs, check_vma=False)
```

```python
import functools

import jax
import jax.numpy as jnp
import numpy as np
from jax import lax
from jax.experimental import pallas as pl
from jax.experimental.pallas import tpu as pltpu
from jax.sharding import PartitionSpec as P


PATCH = 128
STRIDE = 64
HALF = STRIDE // 2
FREQ = -(-(PATCH // 2 + 1) // 8) * 8

stiffness = 1.0
rate = 0.25


def two_parts(table):
    high = table.astype(jnp.bfloat16)
    low = (table - high.astype(np.float64)).astype(jnp.bfloat16)
    return high, low


def tables():
    angle = 2.0 * np.pi * (np.outer(np.arange(PATCH), np.arange(PATCH)) % PATCH) / PATCH
    cosine, sine = np.cos(angle), np.sin(angle)
    kept = np.arange(FREQ)[:, None] <= PATCH // 2
    left = np.concatenate([cosine[:FREQ] * kept, -sine[:FREQ] * kept])
    right = np.block([[cosine, -sine], [sine, cosine]])
    share = np.where((np.arange(FREQ) == 0) | (np.arange(FREQ) == PATCH // 2), 1.0, 2.0)
    scaled = (share * kept[:, 0])[None, :] / float(PATCH) ** 3
    back = np.concatenate([cosine[:, :FREQ] * scaled, sine[:, :FREQ] * scaled], axis=1)
    left_hi, left_lo = two_parts(left)
    back_hi, back_lo = two_parts(back)
    right_hi, right_lo = two_parts(right)
    return (
        np.concatenate([left_hi, left_hi, left_lo], axis=1),
        np.stack([right_hi, right_lo]),
        np.concatenate([back_hi, back_hi, back_lo], axis=1),
    )


def split(values):
    high = values.astype(jnp.bfloat16)
    return high, (values - high.astype(jnp.float32)).astype(jnp.bfloat16)


def mul(a, b):
    return jnp.dot(a, b, preferred_element_type=jnp.float32)


def right_dft(values, right_ref):
    high, low = split(values)
    return mul(high, right_ref[0]) + mul(low, right_ref[0]) + mul(high, right_ref[1])


def node_order(cols):
    return [2 * t for t in range(cols // 2)] + [2 * t + 1 for t in range(cols // 2)]


def keep_region(region, wide, high_ref, low_ref):
    even, odd = region[:, :wide], region[:, STRIDE:STRIDE + wide]
    for part, values in enumerate((even, odd)):
        high, low = split(values)
        high_ref[:, part * wide:(part + 1) * wide] = high
        low_ref[:, part * wide:(part + 1) * wide] = low


def left_dft(cols, bands, high_ref, low_ref, left_ref, half_ref):
    for k, i in enumerate(bands):
        band = pl.ds(i * STRIDE, PATCH)
        high = high_ref[band, :]
        stacked = jnp.concatenate([high, low_ref[band, :], high], axis=0)
        out = mul(left_ref[...], stacked)
        for t, j in enumerate(node_order(cols)):
            lanes = slice(t * PATCH, (t + 1) * PATCH)
            half_ref[k * cols + j, :, :PATCH] = out[:FREQ, lanes]
            half_ref[k * cols + j, :, PATCH:] = out[FREQ:, lanes]


def correlate(rows, cols, group, sign, own_ref, other_ref, right_ref, back_ref, put,
              peak_ref, mass_ref, tilt_ref):
    row = lax.broadcasted_iota(jnp.int32, (group, FREQ, PATCH), 1)
    lane = lax.broadcasted_iota(jnp.int32, (group, FREQ, PATCH), 2)
    varies = ((row + lane) > 0).astype(jnp.float32).reshape(group * FREQ, PATCH)
    lag = lax.broadcasted_iota(jnp.int32, (PATCH, 1), 0)
    lag = jnp.where(lag < PATCH // 2, lag, lag - PATCH).astype(jnp.float32)
    for n in range(0, rows * cols, group):
        both = jnp.concatenate([ref[n:n + group].reshape(group * FREQ, 2 * PATCH) for ref in (own_ref, other_ref)])
        freq = right_dft(both, right_ref)
        first, second = freq[:group * FREQ], freq[group * FREQ:]
        re1, im1 = first[:, :PATCH] * varies, first[:, PATCH:] * varies
        re2, im2 = second[:, :PATCH] * varies, second[:, PATCH:] * varies
        cross = jnp.concatenate([re1 * re2 + im1 * im2, (im1 * re2 - re1 * im2) * sign], axis=1)
        mixed = right_dft(cross, right_ref)
        columns = []
        for m in range(group):
            part = mixed[m * FREQ:(m + 1) * FREQ]
            columns.append(jnp.concatenate([part[:, :PATCH], part[:, PATCH:]], axis=0))
        high, low = split(jnp.concatenate(columns, axis=1))
        scores = mul(back_ref[...], jnp.concatenate([high, low, high], axis=0))
        peak = jnp.max(scores, axis=0, keepdims=True)
        weight = jnp.exp(scores - peak)
        mass = jnp.sum(weight, axis=0, keepdims=True)
        tilt = jnp.sum(weight * lag, axis=0, keepdims=True)
        for m in range(group):
            lanes = slice(m * PATCH, (m + 1) * PATCH)
            peak_ref[n + m:n + m + 1, :] = peak[:, lanes]
            mass_ref[n + m:n + m + 1, :] = mass[:, lanes]
            tilt_ref[n + m:n + m + 1, :] = tilt[:, lanes]
    peak = peak_ref[...]
    share = jnp.exp(peak - jnp.max(peak, axis=1, keepdims=True))
    mass = mass_ref[...] * share
    lag = lax.broadcasted_iota(jnp.int32, mass.shape, 1)
    place = lax.broadcasted_iota(jnp.int32, mass.shape, 0) % cols
    here = lag == place
    lag = jnp.where(lag < PATCH // 2, lag, lag - PATCH).astype(jnp.float32)
    total = jnp.sum(mass, axis=1, keepdims=True)
    flow_y = jnp.sum(tilt_ref[...] * share, axis=1, keepdims=True) / total
    flow_x = jnp.sum(mass * lag, axis=1, keepdims=True) / total
    for c, value in enumerate((flow_y, flow_x)):
        spread = jnp.where(here, value, 0.0)
        for i in range(rows):
            put(c, i, jnp.sum(spread[i * cols:(i + 1) * cols], axis=0, keepdims=True))


def flow_kernel(rows, cols, group, region_ref, left_ref, right_ref, back_ref, flow_ref,
                high_ref, low_ref, own_ref, other_ref, *stats):
    for z, half_ref in enumerate((own_ref, other_ref)):
        keep_region(region_ref[z], cols * STRIDE, high_ref, low_ref)
        left_dft(cols, range(rows), high_ref, low_ref, left_ref, half_ref)

    def put(c, i, row):
        flow_ref[c * rows + i:c * rows + i + 1, :] = row

    correlate(rows, cols, group, 1.0, own_ref, other_ref, right_ref, back_ref, put, *stats)


def region_scratch(rows, cols):
    return [pltpu.VMEM(((rows + 1) * STRIDE, 2 * cols * STRIDE), jnp.bfloat16)] * 2


def half_shape(rows, cols):
    return (rows * cols, FREQ, 2 * PATCH)


def stats_scratch(rows, cols):
    return [pltpu.VMEM((rows * cols, PATCH), jnp.float32)] * 3


IN_VMEM = pl.BlockSpec(memory_space=pltpu.VMEM)


def kernel_call(body, outs, *args, scratch=(), last=False):
    args = [pltpu.with_memory_space_constraint(a, pltpu.VMEM) if isinstance(a, jax.Array) else a for a in args]
    shapes = outs if last else jax.tree.map(lambda out: pltpu.VMEM(out.shape, out.dtype), outs)
    return pl.pallas_call(
        body,
        out_shape=shapes,
        in_specs=[IN_VMEM] * len(args),
        out_specs=jax.tree.map(lambda _: IN_VMEM, outs),
        scratch_shapes=scratch,
        compiler_params=pltpu.CompilerParams(vmem_limit_bytes=24 << 20),
    )(*args)


def floats(*shape):
    return jax.ShapeDtypeStruct(shape, jnp.float32)


def flow_of(region, rows, cols, group=16):
    return kernel_call(
        functools.partial(flow_kernel, rows, cols, group),
        floats(2 * rows, PATCH), region, *tables(),
        scratch=region_scratch(rows, cols) + [pltpu.VMEM(half_shape(rows, cols), jnp.float32)] * 2
        + stats_scratch(rows, cols),
    )


def shifted(value, axis, by):
    length = lax.axis_size(axis)
    pairs = [(i, i + by) for i in range(length) if 0 <= i + by < length]
    return lax.ppermute(value, axis, pairs)


def padded_2(value, sides, width):
    for axis, dim in sides:
        size, length = (lax.axis_size(axis), value.shape[dim])
        up = [(i, (i + 1) % size) for i in range(size - 1)]
        down = [(j, i) for i, j in up]
        last = lax.slice_in_dim(value, length - width, length, axis=dim)
        first = lax.slice_in_dim(value, 0, width, axis=dim)
        before = lax.ppermute(last, axis, up)
        after = lax.ppermute(first, axis, down)
        value = jnp.concatenate([before, value, after], axis=dim)
    return value


def lap_of(padded, center):
    return (
        padded[:, :-2, 1:-1]
        + padded[:, 2:, 1:-1]
        + padded[:, 1:-1, :-2]
        + padded[:, 1:-1, 2:]
        - 4.0 * center
    )


def whole_sections(images):
    tile = images[0]
    rows, cols = tile.shape[0] // STRIDE, tile.shape[1] // STRIDE
    region = padded_2(jnp.stack([tile, shifted(tile, "sec", -1)]), (("ty", 1), ("tx", 2)), HALF)
    flow = flow_of(region, rows, cols)[:, :cols].reshape(2, rows, cols)
    keep = (lax.axis_index("sec") < lax.axis_size("sec") - 1).astype(jnp.float32)
    flow = flow * keep
    padded = padded_2(flow, (("ty", 1), ("tx", 2)), 2)
    inner = padded[:, 1:-1, 1:-1]
    first = inner + rate * (stiffness * lap_of(padded, inner) + inner - inner)
    row_ids = lax.axis_index("ty") * rows + jnp.arange(-1, rows + 1, dtype=jnp.int32)
    col_ids = lax.axis_index("tx") * cols + jnp.arange(-1, cols + 1, dtype=jnp.int32)
    row_ok = (row_ids >= 0) & (row_ids < rows * lax.axis_size("ty"))
    col_ok = (col_ids >= 0) & (col_ids < cols * lax.axis_size("tx"))
    first = first * (row_ok[:, None] & col_ok[None, :]).astype(jnp.float32)[None]
    center = first[:, 1:-1, 1:-1]
    mesh = center + rate * (stiffness * lap_of(first, center) + flow - center)
    everything = lax.all_gather(mesh, "sec")
    earlier = jnp.arange(lax.axis_size("sec")) < lax.axis_index("sec")
    before = jnp.sum(jnp.where(earlier[:, None, None, None], everything, 0.0), axis=0)
    return (mesh[None], before[None])


AXES = ("sec", "ty", "tx")


def placed(half, y, x):
    ny, nx = lax.axis_size("ty"), lax.axis_size("tx")
    return (((half + x) % 2) * ny + y) * nx + x


def along(value, step):
    ny, nx = lax.axis_size("ty"), lax.axis_size("tx")
    pairs = []
    for y in range(ny):
        for g in range(2 * nx):
            to = step(g, 2 * nx)
            pairs.append((placed(g % 2, y, g // 2), placed(to % 2, y, to // 2)))
    return lax.ppermute(value, AXES, pairs)


def mate(g, count):
    return g ^ 1


def near(g, count):
    to = g - 1 if g % 2 == 0 else g + 1
    return to if 0 <= to < count else g


def far(g, count):
    to = g - 2 if g % 2 == 0 else g + 2
    return to if 0 <= to < count else g ^ 1


def past(g, count):
    to = g + 2 if g % 2 == 0 else g - 2
    return to if 0 <= to < count else g ^ 1


def pairs_even(value):
    size = lax.axis_size("ty")
    return lax.ppermute(value, "ty", [(i, i ^ 1) for i in range(size)])


def pairs_odd(value):
    size = lax.axis_size("ty")
    to = [i - 1 if i % 2 == 0 else i + 1 for i in range(size)]
    return lax.ppermute(value, "ty", [(i, t if 0 <= t < size else i) for i, t in enumerate(to)])


def around(y, ny, even, odd):
    lower = y % 2 == 1
    above = jnp.where(y == 0, 0.0, jnp.where(lower, even, odd))
    below = jnp.where(y == ny - 1, 0.0, jnp.where(lower, odd, even))
    return above, below


def where_am_i():
    section, y, x = lax.axis_index("sec"), lax.axis_index("ty"), lax.axis_index("tx")
    return section, y, x, (section + x) % 2


def packed(column):
    quarter = column.shape[0] // 4
    return jnp.concatenate([column[q * quarter:(q + 1) * quarter] for q in range(4)], axis=1)


def unpacked(block):
    return jnp.concatenate([block[:, q * HALF:(q + 1) * HALF] for q in range(4)], axis=0)


def packed_wide(value):
    full = value.shape[1] // PATCH
    tiles = [value[:, t * PATCH:(t + 1) * PATCH] for t in range(full)]
    return jnp.concatenate(tiles + [packed(value[:, full * PATCH:])], axis=0)


def unpacked_wide(block, tall, width):
    full = width // PATCH
    tiles = [block[t * tall:(t + 1) * tall] for t in range(full)]
    return jnp.concatenate(tiles + [unpacked(block[full * tall:full * tall + tall // 4])], axis=1)


def own_lanes(half, core, width):
    return slice(0, core) if half == 0 else slice(width - core, width)


def by_half(half, branch):
    for h in range(2):
        pl.when(half == h)(functools.partial(branch, h))


def cut_kernel(core, tile_ref, other_ref, even_ref, odd_ref):
    _, y, _, half = where_am_i()
    tall, width = tile_ref.shape
    lower = y % 2 == 1
    first, last = tile_ref[:HALF], tile_ref[tall - HALF:]
    even_ref[...] = jnp.where(lower, first, last)
    odd_ref[...] = jnp.where(lower, last, first)

    def branch(h):
        other_ref[...] = packed_wide(tile_ref[:, own_lanes(1 - h, core, width)])

    by_half(half, branch)


def borders_kernel(core, ny, tile_ref, even_ref, odd_ref, strips_ref, near_ref, past_ref):
    _, y, _, half = where_am_i()
    width = tile_ref.shape[1]
    above, below = around(y, ny, even_ref[...], odd_ref[...])

    def column(lanes):
        return packed(jnp.concatenate([above[:, lanes], tile_ref[:, lanes], below[:, lanes]], axis=0))

    first, last = column(slice(0, HALF)), column(slice(width - HALF, width))

    def branch(h):
        lanes = own_lanes(1 - h, core, width)
        strips_ref[...] = packed_wide(jnp.concatenate([above[:, lanes], below[:, lanes]], axis=0))
        near_ref[...], past_ref[...] = (first, last) if h == 0 else (last, first)

    by_half(half, branch)


def keep_half(half, x, nx, cols, side_ref, values, high_ref, low_ref):
    at_end = jnp.where(half == 0, x == 0, x == nx - 1)
    side = jnp.where(at_end, 0.0, unpacked(side_ref[...]))

    def branch(h):
        value = jnp.concatenate([side, values(h)] if h == 0 else [values(h), side], axis=1)
        keep_region(value, cols * STRIDE, high_ref, low_ref)

    by_half(half, branch)


def own_kernel(rows, cols, ny, nx, tile_ref, even_ref, odd_ref, side_ref, left_ref, half_ref, high_ref, low_ref):
    _, y, x, half = where_am_i()
    width, core = tile_ref.shape[1], cols * STRIDE + HALF
    above, below = around(y, ny, even_ref[...], odd_ref[...])

    def values(h):
        lanes = own_lanes(h, core, width)
        return jnp.concatenate([above[:, lanes], tile_ref[:, lanes], below[:, lanes]], axis=0)

    keep_half(half, x, nx, cols, side_ref, values, high_ref, low_ref)
    left_dft(cols, range(rows), high_ref, low_ref, left_ref, half_ref)


def pair_kernel(rows, cols, group, nx, own_ref, other_ref, strips_ref, cross_ref,
                left_ref, right_ref, back_ref, flow_ref, high_ref, low_ref, half_ref, *stats):
    section, _, x, half = where_am_i()
    core = cols * STRIDE + HALF
    strips = unpacked_wide(strips_ref[...], 2 * HALF, core)
    middle = unpacked_wide(other_ref[...], rows * STRIDE, core)
    value = jnp.concatenate([strips[:HALF], middle, strips[HALF:]], axis=0)
    keep_half(half, x, nx, cols, cross_ref, lambda h: value, high_ref, low_ref)
    left_dft(cols, range(rows), high_ref, low_ref, left_ref, half_ref)

    def put(c, i, row):
        flow_ref[c * rows + i:c * rows + i + 1, :] = row

    sign = jnp.where(section == 0, 1.0, -1.0)
    correlate(rows, cols, group, sign, own_ref, half_ref, right_ref, back_ref, put, *stats)


def window_kernel(width, nx, own_ref, mate_ref, near_ref, far_ref, out_ref):
    _, _, x, place = where_am_i()
    half = place == 1
    own, other, close, beyond = own_ref[...], mate_ref[...], near_ref[...], far_ref[...]
    lane = lax.broadcasted_iota(jnp.int32, own.shape, 1)
    begin = jnp.where(x == 0, 0.0, jnp.where(half, beyond, close))
    left = jnp.where(half, other, own)
    right = jnp.where(half, own, other)
    end = jnp.where(x == nx - 1, 0.0, jnp.where(half, close, beyond))
    begin, left = pltpu.roll(begin, PATCH + 2 - width, 1), pltpu.roll(left, 2, 1)
    right, end = pltpu.roll(right, 2 + width, 1), pltpu.roll(end, 2 + 2 * width, 1)
    value = jnp.where(lane < 2, begin, jnp.where(lane < 2 + width, left, right))
    value = jnp.where(lane < 2 + 2 * width, value, jnp.where(lane < 4 + 2 * width, end, 0.0))
    out_ref[...] = value


def relax_kernel(rows, cols, ny, nx, own_ref, even_ref, odd_ref, mesh_ref, earlier_ref):
    section, y, x, _ = where_am_i()
    above, below = around(y, ny, even_ref[...], odd_ref[...])
    own = own_ref[...]
    tall = rows + 4
    shape = (tall, PATCH)
    row = lax.broadcasted_iota(jnp.int32, shape, 0) - 2 + y * rows
    col = lax.broadcasted_iota(jnp.int32, shape, 1) - 2 + x * cols
    inside = (row >= 0) & (row < ny * rows) & (col >= 0) & (col < nx * cols)

    def step(mesh, flow):
        nearby = (
            pltpu.roll(mesh, 1, 0) + pltpu.roll(mesh, tall - 1, 0)
            + pltpu.roll(mesh, 1, 1) + pltpu.roll(mesh, PATCH - 1, 1)
        )
        lap = nearby - 4.0 * mesh
        return jnp.where(inside, mesh + rate * (stiffness * lap + flow - mesh), 0.0)

    for c in range(2):
        flow = jnp.concatenate(
            [above[(c + 1) * rows - 2:(c + 1) * rows], own[c * rows:(c + 1) * rows],
             below[c * rows:c * rows + 2]], axis=0)
        flow = jnp.where(inside, flow, 0.0)
        mesh = step(step(flow, flow), flow)
        mesh = pltpu.roll(pltpu.roll(mesh, tall - 2, 0), PATCH - 2, 1)[:rows, :cols]
        mesh_ref[0, c] = jnp.where(section == 0, mesh, 0.0)
        earlier_ref[0, c] = jnp.where(section == 0, 0.0, mesh)


def shared_section(images):
    tile = images[0]
    ny, nx = lax.axis_size("ty"), lax.axis_size("tx")
    rows, cols = tile.shape[0] // STRIDE, tile.shape[1] // STRIDE
    half = cols // 2
    core, tall = half * STRIDE + HALF, tile.shape[0]

    strip = floats(HALF, tile.shape[1])
    other, even, odd = kernel_call(
        functools.partial(cut_kernel, core), (floats(tall * core // PATCH, PATCH), strip, strip), tile,
    )
    other = along(other, mate)
    even, odd = pairs_even(even), pairs_odd(odd)
    edge = floats((tall + 2 * HALF) // 4, PATCH)
    strips, side, cross = kernel_call(
        functools.partial(borders_kernel, core, ny), (floats(2 * HALF * core // PATCH, PATCH), edge, edge),
        tile, even, odd,
    )
    side, cross = along(side, near), along(cross, past)
    strips = along(strips, mate)
    left, right, back = tables()
    spectra = half_shape(rows, half)
    own = kernel_call(
        functools.partial(own_kernel, rows, half, ny, nx), floats(*spectra), tile, even, odd, side, left,
        scratch=region_scratch(rows, half),
    )
    flow = kernel_call(
        functools.partial(pair_kernel, rows, half, rows * half, nx), floats(2 * rows, PATCH),
        own, other, strips, cross, left, right, back,
        scratch=region_scratch(rows, half) + [pltpu.VMEM(spectra, jnp.float32)] + stats_scratch(rows, half),
    )
    window = kernel_call(
        functools.partial(window_kernel, half, nx), floats(*flow.shape),
        flow, along(flow, mate), along(flow, near), along(flow, far),
    )
    out = floats(1, 2, rows, cols)
    return kernel_call(
        functools.partial(relax_kernel, rows, cols, ny, nx), (out, out),
        window, pairs_even(window), pairs_odd(window), last=True,
    )


def solution(mesh):
    in_specs = (P("sec", "ty", "tx"),)
    out_specs = (P("sec", None, "ty", "tx"), P("sec", None, "ty", "tx"))
    even = mesh.shape["ty"] % 2 == 0 and mesh.shape["tx"] % 2 == 0
    shared = mesh.shape["sec"] == 2 and even

    def body(images):
        return (shared_section if shared else whole_sections)(images)

    return jax.shard_map(body, mesh=mesh, in_specs=in_specs, out_specs=out_specs, check_vma=False)
```

```python
import functools

import jax
import jax.numpy as jnp
import numpy as np
from jax import lax
from jax.experimental import pallas as pl
from jax.experimental.pallas import tpu as pltpu
from jax.sharding import PartitionSpec as P


PATCH = 128
STRIDE = 64
HALF = STRIDE // 2
FREQ = -(-(PATCH // 2 + 1) // 8) * 8

stiffness = 1.0
rate = 0.25


def two_parts(table):
    high = table.astype(jnp.bfloat16)
    low = (table - high.astype(np.float64)).astype(jnp.bfloat16)
    return high, low


def tables():
    angle = 2.0 * np.pi * (np.outer(np.arange(PATCH), np.arange(PATCH)) % PATCH) / PATCH
    cosine, sine = np.cos(angle), np.sin(angle)
    kept = np.arange(FREQ)[:, None] <= PATCH // 2
    left = np.concatenate([cosine[:FREQ] * kept, -sine[:FREQ] * kept])
    right = np.block([[cosine, -sine], [sine, cosine]])
    share = np.where((np.arange(FREQ) == 0) | (np.arange(FREQ) == PATCH // 2), 1.0, 2.0)
    scaled = (share * kept[:, 0])[None, :] / float(PATCH) ** 3
    back = np.concatenate([cosine[:, :FREQ] * scaled, sine[:, :FREQ] * scaled], axis=1)
    left_hi, left_lo = two_parts(left)
    back_hi, back_lo = two_parts(back)
    right_hi, right_lo = two_parts(right)
    return (
        np.concatenate([left_hi, left_hi, left_lo], axis=1),
        np.stack([right_hi, right_lo]),
        np.concatenate([back_hi, back_hi, back_lo], axis=1),
    )


def split(values):
    high = values.astype(jnp.bfloat16)
    return high, (values - high.astype(jnp.float32)).astype(jnp.bfloat16)


def mul(a, b):
    return jnp.dot(a, b, preferred_element_type=jnp.float32)


def right_dft(values, right_ref):
    high, low = split(values)
    return mul(high, right_ref[0]) + mul(low, right_ref[0]) + mul(high, right_ref[1])


def node_order(cols):
    return [2 * t for t in range((cols + 1) // 2)] + [2 * t + 1 for t in range(cols // 2)]


def keep_region(region, cols, high_ref, low_ref):
    even = PATCH * ((cols + 1) // 2)
    high_ref[:, :even], low_ref[:, :even] = split(region[:, :even])
    if cols > 1:
        high_ref[:, even:], low_ref[:, even:] = split(region[:, STRIDE:STRIDE + PATCH * (cols // 2)])


def left_dft(cols, bands, high_ref, low_ref, left_ref, half_ref):
    for k, i in enumerate(bands):
        band = pl.ds(i * STRIDE, PATCH)
        high = high_ref[band, :]
        stacked = jnp.concatenate([high, low_ref[band, :], high], axis=0)
        out = mul(left_ref[...], stacked)
        for t, j in enumerate(node_order(cols)):
            lanes = slice(t * PATCH, (t + 1) * PATCH)
            half_ref[k * cols + j, :, :PATCH] = out[:FREQ, lanes]
            half_ref[k * cols + j, :, PATCH:] = out[FREQ:, lanes]


def correlate(rows, cols, group, sign, own_ref, other_ref, right_ref, back_ref, lane0, put,
              peak_ref, mass_ref, tilt_ref):
    row = lax.broadcasted_iota(jnp.int32, (group, FREQ, PATCH), 1)
    lane = lax.broadcasted_iota(jnp.int32, (group, FREQ, PATCH), 2)
    varies = ((row + lane) > 0).astype(jnp.float32).reshape(group * FREQ, PATCH)
    lag = lax.broadcasted_iota(jnp.int32, (PATCH, 1), 0)
    lag = jnp.where(lag < PATCH // 2, lag, lag - PATCH).astype(jnp.float32)
    for n in range(0, rows * cols, group):
        both = jnp.concatenate([ref[n:n + group].reshape(group * FREQ, 2 * PATCH) for ref in (own_ref, other_ref)])
        freq = right_dft(both, right_ref)
        first, second = freq[:group * FREQ], freq[group * FREQ:]
        re1, im1 = first[:, :PATCH] * varies, first[:, PATCH:] * varies
        re2, im2 = second[:, :PATCH] * varies, second[:, PATCH:] * varies
        cross = jnp.concatenate([re1 * re2 + im1 * im2, (im1 * re2 - re1 * im2) * sign], axis=1)
        mixed = right_dft(cross, right_ref)
        columns = []
        for m in range(group):
            part = mixed[m * FREQ:(m + 1) * FREQ]
            columns.append(jnp.concatenate([part[:, :PATCH], part[:, PATCH:]], axis=0))
        high, low = split(jnp.concatenate(columns, axis=1))
        scores = mul(back_ref[...], jnp.concatenate([high, low, high], axis=0))
        peak = jnp.max(scores, axis=0, keepdims=True)
        weight = jnp.exp(scores - peak)
        mass = jnp.sum(weight, axis=0, keepdims=True)
        tilt = jnp.sum(weight * lag, axis=0, keepdims=True)
        for m in range(group):
            lanes = slice(m * PATCH, (m + 1) * PATCH)
            peak_ref[n + m:n + m + 1, :] = peak[:, lanes]
            mass_ref[n + m:n + m + 1, :] = mass[:, lanes]
            tilt_ref[n + m:n + m + 1, :] = tilt[:, lanes]
    peak = peak_ref[...]
    share = jnp.exp(peak - jnp.max(peak, axis=1, keepdims=True))
    mass = mass_ref[...] * share
    lag = lax.broadcasted_iota(jnp.int32, mass.shape, 1)
    place = lax.broadcasted_iota(jnp.int32, mass.shape, 0) % cols + lane0
    here = lag == place
    lag = jnp.where(lag < PATCH // 2, lag, lag - PATCH).astype(jnp.float32)
    total = jnp.sum(mass, axis=1, keepdims=True)
    flow_y = jnp.sum(tilt_ref[...] * share, axis=1, keepdims=True) / total
    flow_x = jnp.sum(mass * lag, axis=1, keepdims=True) / total
    for c, value in enumerate((flow_y, flow_x)):
        spread = jnp.where(here, value, 0.0)
        for i in range(rows):
            put(c, i, jnp.sum(spread[i * cols:(i + 1) * cols], axis=0, keepdims=True))


def flow_kernel(rows, cols, group, region_ref, left_ref, right_ref, back_ref, flow_ref,
                high_ref, low_ref, own_ref, other_ref, *stats):
    for z, half_ref in enumerate((own_ref, other_ref)):
        keep_region(region_ref[z], cols, high_ref, low_ref)
        left_dft(cols, range(rows), high_ref, low_ref, left_ref, half_ref)

    def put(c, i, row):
        flow_ref[c * rows + i:c * rows + i + 1, :] = row

    correlate(rows, cols, group, 1.0, own_ref, other_ref, right_ref, back_ref, 0, put, *stats)


def region_scratch(rows, cols):
    return [pltpu.VMEM(((rows + 1) * STRIDE, cols * PATCH), jnp.bfloat16)] * 2


def half_shape(rows, cols):
    return (rows * cols, FREQ, 2 * PATCH)


def stats_scratch(rows, cols):
    return [pltpu.VMEM((rows * cols, PATCH), jnp.float32)] * 3


IN_VMEM = pl.BlockSpec(memory_space=pltpu.VMEM)


def kernel_call(body, outs, *args, scratch=(), last=False):
    args = [pltpu.with_memory_space_constraint(a, pltpu.VMEM) if isinstance(a, jax.Array) else a for a in args]
    shapes = outs if last else jax.tree.map(lambda out: pltpu.VMEM(out.shape, out.dtype), outs)
    return pl.pallas_call(
        body,
        out_shape=shapes,
        in_specs=[IN_VMEM] * len(args),
        out_specs=jax.tree.map(lambda _: IN_VMEM, outs),
        scratch_shapes=scratch,
        compiler_params=pltpu.CompilerParams(vmem_limit_bytes=24 << 20),
    )(*args)


def floats(*shape):
    return jax.ShapeDtypeStruct(shape, jnp.float32)


def flow_of(region, rows, cols, group=16):
    return kernel_call(
        functools.partial(flow_kernel, rows, cols, group),
        floats(2 * rows, PATCH), region, *tables(),
        scratch=region_scratch(rows, cols) + [pltpu.VMEM(half_shape(rows, cols), jnp.float32)] * 2
        + stats_scratch(rows, cols),
    )


def shifted(value, axis, by):
    length = lax.axis_size(axis)
    pairs = [(i, i + by) for i in range(length) if 0 <= i + by < length]
    return lax.ppermute(value, axis, pairs)


def padded_2(value, sides, width):
    for axis, dim in sides:
        size, length = (lax.axis_size(axis), value.shape[dim])
        up = [(i, (i + 1) % size) for i in range(size - 1)]
        down = [(j, i) for i, j in up]
        last = lax.slice_in_dim(value, length - width, length, axis=dim)
        first = lax.slice_in_dim(value, 0, width, axis=dim)
        before = lax.ppermute(last, axis, up)
        after = lax.ppermute(first, axis, down)
        value = jnp.concatenate([before, value, after], axis=dim)
    return value


def lap_of(padded, center):
    return (
        padded[:, :-2, 1:-1]
        + padded[:, 2:, 1:-1]
        + padded[:, 1:-1, :-2]
        + padded[:, 1:-1, 2:]
        - 4.0 * center
    )


def whole_sections(images):
    tile = images[0]
    rows, cols = tile.shape[0] // STRIDE, tile.shape[1] // STRIDE
    region = padded_2(jnp.stack([tile, shifted(tile, "sec", -1)]), (("ty", 1), ("tx", 2)), HALF)
    flow = flow_of(region, rows, cols)[:, :cols].reshape(2, rows, cols)
    keep = (lax.axis_index("sec") < lax.axis_size("sec") - 1).astype(jnp.float32)
    flow = flow * keep
    padded = padded_2(flow, (("ty", 1), ("tx", 2)), 2)
    inner = padded[:, 1:-1, 1:-1]
    first = inner + rate * (stiffness * lap_of(padded, inner) + inner - inner)
    row_ids = lax.axis_index("ty") * rows + jnp.arange(-1, rows + 1, dtype=jnp.int32)
    col_ids = lax.axis_index("tx") * cols + jnp.arange(-1, cols + 1, dtype=jnp.int32)
    row_ok = (row_ids >= 0) & (row_ids < rows * lax.axis_size("ty"))
    col_ok = (col_ids >= 0) & (col_ids < cols * lax.axis_size("tx"))
    first = first * (row_ok[:, None] & col_ok[None, :]).astype(jnp.float32)[None]
    center = first[:, 1:-1, 1:-1]
    mesh = center + rate * (stiffness * lap_of(first, center) + flow - center)
    everything = lax.all_gather(mesh, "sec")
    earlier = jnp.arange(lax.axis_size("sec")) < lax.axis_index("sec")
    before = jnp.sum(jnp.where(earlier[:, None, None, None], everything, 0.0), axis=0)
    return (mesh[None], before[None])


AXES = ("sec", "ty", "tx")


def placed(half, y, x):
    ny, nx = lax.axis_size("ty"), lax.axis_size("tx")
    return (((half + x) % 2) * ny + y) * nx + x


def along(value, step):
    ny, nx = lax.axis_size("ty"), lax.axis_size("tx")
    pairs = []
    for y in range(ny):
        for g in range(2 * nx):
            to = step(g, 2 * nx)
            pairs.append((placed(g % 2, y, g // 2), placed(to % 2, y, to // 2)))
    return lax.ppermute(value, AXES, pairs)


def mate(g, count):
    return g ^ 1


def near(g, count):
    return (g - 1 if g % 2 == 0 else g + 1) % count


def far(g, count):
    to = g - 2 if g % 2 == 0 else g + 2
    return to if 0 <= to < count else g ^ 1


def past(g, count):
    to = g + 2 if g % 2 == 0 else g - 2
    return to if 0 <= to < count else g ^ 1


def pairs_even(value):
    size = lax.axis_size("ty")
    return lax.ppermute(value, "ty", [(i, i ^ 1) for i in range(size)])


def pairs_odd(value):
    size = lax.axis_size("ty")
    return lax.ppermute(value, "ty", [(i, (i - 1 if i % 2 == 0 else i + 1) % size) for i in range(size)])


def around(y, ny, even, odd):
    lower = y % 2 == 1
    above = jnp.where(y == 0, 0.0, jnp.where(lower, even, odd))
    below = jnp.where(y == ny - 1, 0.0, jnp.where(lower, odd, even))
    return above, below


def where_am_i():
    section, y, x = lax.axis_index("sec"), lax.axis_index("ty"), lax.axis_index("tx")
    return section, y, x, (section + x) % 2


def packed(column):
    quarter = column.shape[0] // 4
    return jnp.concatenate([column[q * quarter:(q + 1) * quarter] for q in range(4)], axis=1)


def unpacked(block):
    return jnp.concatenate([block[:, q * HALF:(q + 1) * HALF] for q in range(4)], axis=0)


def inner(half, value):
    return value[:, HALF:] if half == 0 else value[:, :value.shape[1] - HALF]


def outer(half, value):
    return value[:, :HALF] if half == 0 else value[:, value.shape[1] - HALF:]


def packed_wide(half, value):
    tiles = inner(half, value)
    blocks = [tiles[:, t * PATCH:(t + 1) * PATCH] for t in range(tiles.shape[1] // PATCH)]
    return jnp.concatenate(blocks + [packed(outer(half, value))], axis=0)


def unpacked_wide(block, tall):
    full = block.shape[0] // tall
    tiles = [block[t * tall:(t + 1) * tall] for t in range(full)]
    return jnp.concatenate(tiles, axis=1), unpacked(block[full * tall:])


def own_lanes(half, core, width):
    return slice(0, core) if half == 0 else slice(width - core, width)


def by_half(half, branch):
    for h in range(2):
        pl.when(half == h)(functools.partial(branch, h))


def cut_kernel(core, tile_ref, other_ref, even_ref, odd_ref):
    _, y, _, half = where_am_i()
    tall, width = tile_ref.shape
    lower = y % 2 == 1
    first, last = tile_ref[:HALF], tile_ref[tall - HALF:]
    even_ref[...] = jnp.where(lower, first, last)
    odd_ref[...] = jnp.where(lower, last, first)

    def branch(h):
        other_ref[...] = packed_wide(1 - h, tile_ref[:, own_lanes(1 - h, core, width)])

    by_half(half, branch)


def borders_kernel(core, ny, tile_ref, even_ref, odd_ref, strips_ref, near_ref, past_ref):
    _, y, _, half = where_am_i()
    width = tile_ref.shape[1]
    above, below = around(y, ny, even_ref[...], odd_ref[...])

    def column(lanes):
        return packed(jnp.concatenate([above[:, lanes], tile_ref[:, lanes], below[:, lanes]], axis=0))

    first, last = column(slice(0, HALF)), column(slice(width - HALF, width))

    def branch(h):
        lanes = own_lanes(1 - h, core, width)
        strips_ref[...] = packed_wide(1 - h, jnp.concatenate([above[:, lanes], below[:, lanes]], axis=0))
        near_ref[...], past_ref[...] = (first, last) if h == 0 else (last, first)

    by_half(half, branch)


def border_patches(h, side, edge, tiles):
    need = PATCH - 2 * HALF
    if h == 0:
        return jnp.concatenate([side, edge, tiles[:, :need]], axis=1)
    return jnp.concatenate([tiles[:, tiles.shape[1] - need:], edge, side], axis=1)


def masked_side(half, x, nx, side_ref):
    at_end = jnp.where(half == 0, x == 0, x == nx - 1)
    return jnp.where(at_end, 0.0, unpacked(side_ref[...]))


def own_kernel(rows, cols, ny, nx, tile_ref, even_ref, odd_ref, side_ref, left_ref, free_ref, border_ref,
               high_ref, low_ref, border_high, border_low):
    _, y, x, half = where_am_i()
    width, core = tile_ref.shape[1], cols * STRIDE + HALF
    above, below = around(y, ny, even_ref[...], odd_ref[...])
    side = masked_side(half, x, nx, side_ref)

    def branch(h):
        lanes = own_lanes(h, core, width)
        value = jnp.concatenate([above[:, lanes], tile_ref[:, lanes], below[:, lanes]], axis=0)
        tiles = inner(h, value)
        keep_region(tiles, cols - 1, high_ref, low_ref)
        keep_region(border_patches(h, side, outer(h, value), tiles), 1, border_high, border_low)

    by_half(half, branch)
    left_dft(cols - 1, range(rows), high_ref, low_ref, left_ref, free_ref)
    left_dft(1, range(rows), border_high, border_low, left_ref, border_ref)


def other_parts(rows, other_ref, strips_ref):
    tiles, edge = unpacked_wide(other_ref[...], rows * STRIDE)
    more_tiles, more_edge = unpacked_wide(strips_ref[...], 2 * HALF)
    return (jnp.concatenate([more[:HALF], middle, more[HALF:]], axis=0)
            for more, middle in ((more_tiles, tiles), (more_edge, edge)))


def free_kernel(rows, cols, own_ref, other_ref, strips_ref, left_ref, right_ref, back_ref, flow_ref,
                high_ref, low_ref, half_ref, *stats):
    section, _, _, half = where_am_i()
    tiles, _ = other_parts(rows, other_ref, strips_ref)
    keep_region(tiles, cols - 1, high_ref, low_ref)
    left_dft(cols - 1, range(rows), high_ref, low_ref, left_ref, half_ref)

    def put(c, i, row):
        flow_ref[c * rows + i:c * rows + i + 1, :] = row

    sign = jnp.where(section == 0, 1.0, -1.0)
    count = rows * (cols - 1)
    correlate(rows, cols - 1, count, sign, own_ref, half_ref, right_ref, back_ref, 1 - half, put, *stats)


def border_kernel(rows, cols, nx, own_ref, other_ref, strips_ref, cross_ref, before_ref, left_ref, right_ref,
                  back_ref, flow_ref, high_ref, low_ref, half_ref, *stats):
    section, _, x, half = where_am_i()
    tiles, edge = other_parts(rows, other_ref, strips_ref)
    side = masked_side(half, x, nx, cross_ref)
    by_half(half, lambda h: keep_region(border_patches(h, side, edge, tiles), 1, high_ref, low_ref))
    left_dft(1, range(rows), high_ref, low_ref, left_ref, half_ref)

    def put(c, i, row):
        at = slice(c * rows + i, c * rows + i + 1)
        flow_ref[at, :] = before_ref[at, :] + row

    sign = jnp.where(section == 0, 1.0, -1.0)
    lane = (cols - 1) * half
    correlate(rows, 1, rows, sign, own_ref, half_ref, right_ref, back_ref, lane, put, *stats)


def window_kernel(width, nx, own_ref, mate_ref, near_ref, far_ref, out_ref):
    _, _, x, place = where_am_i()
    half = place == 1
    own, other, close, beyond = own_ref[...], mate_ref[...], near_ref[...], far_ref[...]
    lane = lax.broadcasted_iota(jnp.int32, own.shape, 1)
    begin = jnp.where(x == 0, 0.0, jnp.where(half, beyond, close))
    left = jnp.where(half, other, own)
    right = jnp.where(half, own, other)
    end = jnp.where(x == nx - 1, 0.0, jnp.where(half, close, beyond))
    begin, left = pltpu.roll(begin, PATCH + 2 - width, 1), pltpu.roll(left, 2, 1)
    right, end = pltpu.roll(right, 2 + width, 1), pltpu.roll(end, 2 + 2 * width, 1)
    value = jnp.where(lane < 2, begin, jnp.where(lane < 2 + width, left, right))
    value = jnp.where(lane < 2 + 2 * width, value, jnp.where(lane < 4 + 2 * width, end, 0.0))
    out_ref[...] = value


def relax_kernel(rows, cols, ny, nx, own_ref, even_ref, odd_ref, mesh_ref, earlier_ref):
    section, y, x, _ = where_am_i()
    above, below = around(y, ny, even_ref[...], odd_ref[...])
    own = own_ref[...]
    tall = rows + 4
    shape = (tall, PATCH)
    row = lax.broadcasted_iota(jnp.int32, shape, 0) - 2 + y * rows
    col = lax.broadcasted_iota(jnp.int32, shape, 1) - 2 + x * cols
    inside = (row >= 0) & (row < ny * rows) & (col >= 0) & (col < nx * cols)

    def step(mesh, flow):
        nearby = (
            pltpu.roll(mesh, 1, 0) + pltpu.roll(mesh, tall - 1, 0)
            + pltpu.roll(mesh, 1, 1) + pltpu.roll(mesh, PATCH - 1, 1)
        )
        lap = nearby - 4.0 * mesh
        return jnp.where(inside, mesh + rate * (stiffness * lap + flow - mesh), 0.0)

    for c in range(2):
        flow = jnp.concatenate(
            [above[(c + 1) * rows - 2:(c + 1) * rows], own[c * rows:(c + 1) * rows],
             below[c * rows:c * rows + 2]], axis=0)
        flow = jnp.where(inside, flow, 0.0)
        mesh = step(step(flow, flow), flow)
        mesh = pltpu.roll(pltpu.roll(mesh, tall - 2, 0), PATCH - 2, 1)[:rows, :cols]
        mesh_ref[0, c] = jnp.where(section == 0, mesh, 0.0)
        earlier_ref[0, c] = jnp.where(section == 0, 0.0, mesh)


def shared_section(images):
    tile = images[0]
    ny, nx = lax.axis_size("ty"), lax.axis_size("tx")
    rows, cols = tile.shape[0] // STRIDE, tile.shape[1] // STRIDE
    half = cols // 2
    core, tall = half * STRIDE + HALF, tile.shape[0]

    strip = floats(HALF, tile.shape[1])
    other, even, odd = kernel_call(
        functools.partial(cut_kernel, core), (floats(tall * core // PATCH, PATCH), strip, strip), tile,
    )
    other = along(other, mate)
    even, odd = pairs_even(even), pairs_odd(odd)
    edge = floats((tall + 2 * HALF) // 4, PATCH)
    strips, side, cross = kernel_call(
        functools.partial(borders_kernel, core, ny), (floats(2 * HALF * core // PATCH, PATCH), edge, edge),
        tile, even, odd,
    )
    side, cross = along(side, near), along(cross, past)
    strips = along(strips, mate)
    left, right, back = tables()
    free, border = half_shape(rows, half - 1), half_shape(rows, 1)
    own_free, own_border = kernel_call(
        functools.partial(own_kernel, rows, half, ny, nx), (floats(*free), floats(*border)),
        tile, even, odd, side, left,
        scratch=region_scratch(rows, half - 1) + region_scratch(rows, 1),
    )
    flow = kernel_call(
        functools.partial(free_kernel, rows, half), floats(2 * rows, PATCH),
        own_free, other, strips, left, right, back,
        scratch=region_scratch(rows, half - 1) + [pltpu.VMEM(free, jnp.float32)] + stats_scratch(rows, half - 1),
    )
    flow = kernel_call(
        functools.partial(border_kernel, rows, half, nx), floats(2 * rows, PATCH),
        own_border, other, strips, cross, flow, left, right, back,
        scratch=region_scratch(rows, 1) + [pltpu.VMEM(border, jnp.float32)] + stats_scratch(rows, 1),
    )
    window = kernel_call(
        functools.partial(window_kernel, half, nx), floats(*flow.shape),
        flow, along(flow, mate), along(flow, near), along(flow, far),
    )
    out = floats(1, 2, rows, cols)
    return kernel_call(
        functools.partial(relax_kernel, rows, cols, ny, nx), (out, out),
        window, pairs_even(window), pairs_odd(window), last=True,
    )


def solution(mesh):
    in_specs = (P("sec", "ty", "tx"),)
    out_specs = (P("sec", None, "ty", "tx"), P("sec", None, "ty", "tx"))
    even = mesh.shape["ty"] % 2 == 0 and mesh.shape["tx"] % 2 == 0
    shared = mesh.shape["sec"] == 2 and even

    def body(images):
        return (shared_section if shared else whole_sections)(images)

    return jax.shard_map(body, mesh=mesh, in_specs=in_specs, out_specs=out_specs, check_vma=False)
```

```python
import functools

import jax
import jax.numpy as jnp
import numpy as np
from jax import lax
from jax.experimental import pallas as pl
from jax.experimental.pallas import tpu as pltpu
from jax.sharding import PartitionSpec as P


PATCH = 128
STRIDE = 64
HALF = STRIDE // 2
FREQ = -(-(PATCH // 2 + 1) // 8) * 8

stiffness = 1.0
rate = 0.25


def two_parts(table):
    high = table.astype(jnp.bfloat16)
    low = (table - high.astype(np.float64)).astype(jnp.bfloat16)
    return high, low


def tables():
    angle = 2.0 * np.pi * (np.outer(np.arange(PATCH), np.arange(PATCH)) % PATCH) / PATCH
    cosine, sine = np.cos(angle), np.sin(angle)
    kept = np.arange(FREQ)[:, None] <= PATCH // 2
    left = np.concatenate([cosine[:FREQ] * kept, -sine[:FREQ] * kept])
    right = np.block([[cosine, -sine], [sine, cosine]])
    share = np.where((np.arange(FREQ) == 0) | (np.arange(FREQ) == PATCH // 2), 1.0, 2.0)
    scaled = (share * kept[:, 0])[None, :] / float(PATCH) ** 3
    back = np.concatenate([cosine[:, :FREQ] * scaled, sine[:, :FREQ] * scaled], axis=1)
    left_hi, left_lo = two_parts(left)
    back_hi, back_lo = two_parts(back)
    right_hi, right_lo = two_parts(right)
    return (
        np.concatenate([left_hi, left_hi, left_lo], axis=1),
        np.stack([right_hi, right_lo]),
        np.concatenate([back_hi, back_hi, back_lo], axis=1),
    )


def split(values):
    high = values.astype(jnp.bfloat16)
    return high, (values - high.astype(jnp.float32)).astype(jnp.bfloat16)


def mul(a, b):
    return jnp.dot(a, b, preferred_element_type=jnp.float32)


def right_dft(values, right_ref):
    high, low = split(values)
    return mul(high, right_ref[0]) + mul(low, right_ref[0]) + mul(high, right_ref[1])


def node_order(cols):
    return [2 * t for t in range((cols + 1) // 2)] + [2 * t + 1 for t in range(cols // 2)]


def keep_region(region, cols, high_ref, low_ref):
    even = PATCH * ((cols + 1) // 2)
    high_ref[:, :even], low_ref[:, :even] = split(region[:, :even])
    if cols > 1:
        high_ref[:, even:], low_ref[:, even:] = split(region[:, STRIDE:STRIDE + PATCH * (cols // 2)])


def left_dft(cols, bands, high_ref, low_ref, left_ref, half_ref):
    for k, i in enumerate(bands):
        band = pl.ds(i * STRIDE, PATCH)
        high = high_ref[band, :]
        stacked = jnp.concatenate([high, low_ref[band, :], high], axis=0)
        out = mul(left_ref[...], stacked)
        for t, j in enumerate(node_order(cols)):
            lanes = slice(t * PATCH, (t + 1) * PATCH)
            half_ref[k * cols + j, :, :PATCH] = out[:FREQ, lanes]
            half_ref[k * cols + j, :, PATCH:] = out[FREQ:, lanes]


def correlate(rows, cols, group, sign, own_ref, other_ref, right_ref, back_ref, lane0, put,
              peak_ref, mass_ref, tilt_ref):
    row = lax.broadcasted_iota(jnp.int32, (group, FREQ, PATCH), 1)
    lane = lax.broadcasted_iota(jnp.int32, (group, FREQ, PATCH), 2)
    varies = ((row + lane) > 0).astype(jnp.float32).reshape(group * FREQ, PATCH)
    lag = lax.broadcasted_iota(jnp.int32, (PATCH, 1), 0)
    lag = jnp.where(lag < PATCH // 2, lag, lag - PATCH).astype(jnp.float32)
    for n in range(0, rows * cols, group):
        both = jnp.concatenate([ref[n:n + group].reshape(group * FREQ, 2 * PATCH) for ref in (own_ref, other_ref)])
        freq = right_dft(both, right_ref)
        first, second = freq[:group * FREQ], freq[group * FREQ:]
        re1, im1 = first[:, :PATCH] * varies, first[:, PATCH:] * varies
        re2, im2 = second[:, :PATCH] * varies, second[:, PATCH:] * varies
        cross = jnp.concatenate([re1 * re2 + im1 * im2, (im1 * re2 - re1 * im2) * sign], axis=1)
        mixed = right_dft(cross, right_ref)
        columns = []
        for m in range(group):
            part = mixed[m * FREQ:(m + 1) * FREQ]
            columns.append(jnp.concatenate([part[:, :PATCH], part[:, PATCH:]], axis=0))
        high, low = split(jnp.concatenate(columns, axis=1))
        scores = mul(back_ref[...], jnp.concatenate([high, low, high], axis=0))
        peak = jnp.max(scores, axis=0, keepdims=True)
        weight = jnp.exp(scores - peak)
        mass = jnp.sum(weight, axis=0, keepdims=True)
        tilt = jnp.sum(weight * lag, axis=0, keepdims=True)
        for m in range(group):
            lanes = slice(m * PATCH, (m + 1) * PATCH)
            peak_ref[n + m:n + m + 1, :] = peak[:, lanes]
            mass_ref[n + m:n + m + 1, :] = mass[:, lanes]
            tilt_ref[n + m:n + m + 1, :] = tilt[:, lanes]
    peak = peak_ref[...]
    share = jnp.exp(peak - jnp.max(peak, axis=1, keepdims=True))
    mass = mass_ref[...] * share
    lag = lax.broadcasted_iota(jnp.int32, mass.shape, 1)
    place = lax.broadcasted_iota(jnp.int32, mass.shape, 0) % cols + lane0
    here = lag == place
    lag = jnp.where(lag < PATCH // 2, lag, lag - PATCH).astype(jnp.float32)
    total = jnp.sum(mass, axis=1, keepdims=True)
    flow_y = jnp.sum(tilt_ref[...] * share, axis=1, keepdims=True) / total
    flow_x = jnp.sum(mass * lag, axis=1, keepdims=True) / total
    for c, value in enumerate((flow_y, flow_x)):
        spread = jnp.where(here, value, 0.0)
        for i in range(rows):
            put(c, i, jnp.sum(spread[i * cols:(i + 1) * cols], axis=0, keepdims=True))


def flow_kernel(rows, cols, group, region_ref, left_ref, right_ref, back_ref, flow_ref,
                high_ref, low_ref, own_ref, other_ref, *stats):
    for z, half_ref in enumerate((own_ref, other_ref)):
        keep_region(region_ref[z], cols, high_ref, low_ref)
        left_dft(cols, range(rows), high_ref, low_ref, left_ref, half_ref)

    def put(c, i, row):
        flow_ref[c * rows + i:c * rows + i + 1, :] = row

    correlate(rows, cols, group, 1.0, own_ref, other_ref, right_ref, back_ref, 0, put, *stats)


def region_scratch(rows, cols):
    return [pltpu.VMEM(((rows + 1) * STRIDE, cols * PATCH), jnp.bfloat16)] * 2


def half_shape(rows, cols):
    return (rows * cols, FREQ, 2 * PATCH)


def stats_scratch(rows, cols):
    return [pltpu.VMEM((rows * cols, PATCH), jnp.float32)] * 3


IN_VMEM = pl.BlockSpec(memory_space=pltpu.VMEM)


def kernel_call(body, outs, *args, scratch=(), last=False):
    args = [pltpu.with_memory_space_constraint(a, pltpu.VMEM) if isinstance(a, jax.Array) else a for a in args]
    shapes = outs if last else jax.tree.map(lambda out: pltpu.VMEM(out.shape, out.dtype), outs)
    return pl.pallas_call(
        body,
        out_shape=shapes,
        in_specs=[IN_VMEM] * len(args),
        out_specs=jax.tree.map(lambda _: IN_VMEM, outs),
        scratch_shapes=scratch,
        compiler_params=pltpu.CompilerParams(vmem_limit_bytes=24 << 20),
    )(*args)


def floats(*shape):
    return jax.ShapeDtypeStruct(shape, jnp.float32)


def flow_of(region, rows, cols, group=16):
    return kernel_call(
        functools.partial(flow_kernel, rows, cols, group),
        floats(2 * rows, PATCH), region, *tables(),
        scratch=region_scratch(rows, cols) + [pltpu.VMEM(half_shape(rows, cols), jnp.float32)] * 2
        + stats_scratch(rows, cols),
    )


def shifted(value, axis, by):
    length = lax.axis_size(axis)
    pairs = [(i, i + by) for i in range(length) if 0 <= i + by < length]
    return lax.ppermute(value, axis, pairs)


def padded_2(value, sides, width):
    for axis, dim in sides:
        size, length = (lax.axis_size(axis), value.shape[dim])
        up = [(i, (i + 1) % size) for i in range(size - 1)]
        down = [(j, i) for i, j in up]
        last = lax.slice_in_dim(value, length - width, length, axis=dim)
        first = lax.slice_in_dim(value, 0, width, axis=dim)
        before = lax.ppermute(last, axis, up)
        after = lax.ppermute(first, axis, down)
        value = jnp.concatenate([before, value, after], axis=dim)
    return value


def lap_of(padded, center):
    return (
        padded[:, :-2, 1:-1]
        + padded[:, 2:, 1:-1]
        + padded[:, 1:-1, :-2]
        + padded[:, 1:-1, 2:]
        - 4.0 * center
    )


def whole_sections(images):
    tile = images[0]
    rows, cols = tile.shape[0] // STRIDE, tile.shape[1] // STRIDE
    region = padded_2(jnp.stack([tile, shifted(tile, "sec", -1)]), (("ty", 1), ("tx", 2)), HALF)
    flow = flow_of(region, rows, cols)[:, :cols].reshape(2, rows, cols)
    keep = (lax.axis_index("sec") < lax.axis_size("sec") - 1).astype(jnp.float32)
    flow = flow * keep
    padded = padded_2(flow, (("ty", 1), ("tx", 2)), 2)
    inner = padded[:, 1:-1, 1:-1]
    first = inner + rate * (stiffness * lap_of(padded, inner) + inner - inner)
    row_ids = lax.axis_index("ty") * rows + jnp.arange(-1, rows + 1, dtype=jnp.int32)
    col_ids = lax.axis_index("tx") * cols + jnp.arange(-1, cols + 1, dtype=jnp.int32)
    row_ok = (row_ids >= 0) & (row_ids < rows * lax.axis_size("ty"))
    col_ok = (col_ids >= 0) & (col_ids < cols * lax.axis_size("tx"))
    first = first * (row_ok[:, None] & col_ok[None, :]).astype(jnp.float32)[None]
    center = first[:, 1:-1, 1:-1]
    mesh = center + rate * (stiffness * lap_of(first, center) + flow - center)
    everything = lax.all_gather(mesh, "sec")
    earlier = jnp.arange(lax.axis_size("sec")) < lax.axis_index("sec")
    before = jnp.sum(jnp.where(earlier[:, None, None, None], everything, 0.0), axis=0)
    return (mesh[None], before[None])


AXES = ("sec", "ty", "tx")


def placed(half, y, x):
    ny, nx = lax.axis_size("ty"), lax.axis_size("tx")
    return (((half + x) % 2) * ny + y) * nx + x


def along(value, step):
    ny, nx = lax.axis_size("ty"), lax.axis_size("tx")
    pairs = []
    for y in range(ny):
        for g in range(2 * nx):
            to = step(g, 2 * nx)
            pairs.append((placed(g % 2, y, g // 2), placed(to % 2, y, to // 2)))
    return lax.ppermute(value, AXES, pairs)


def mate(g, count):
    return g ^ 1


def near(g, count):
    return (g - 1 if g % 2 == 0 else g + 1) % count


def far(g, count):
    to = g - 2 if g % 2 == 0 else g + 2
    return to if 0 <= to < count else g ^ 1


def past(g, count):
    to = g + 2 if g % 2 == 0 else g - 2
    return to if 0 <= to < count else g ^ 1


def pairs_even(value):
    size = lax.axis_size("ty")
    return lax.ppermute(value, "ty", [(i, i ^ 1) for i in range(size)])


def pairs_odd(value):
    size = lax.axis_size("ty")
    return lax.ppermute(value, "ty", [(i, (i - 1 if i % 2 == 0 else i + 1) % size) for i in range(size)])


def around(y, ny, even, odd):
    lower = y % 2 == 1
    above = jnp.where(y == 0, 0.0, jnp.where(lower, even, odd))
    below = jnp.where(y == ny - 1, 0.0, jnp.where(lower, odd, even))
    return above, below


def where_am_i():
    section, y, x = lax.axis_index("sec"), lax.axis_index("ty"), lax.axis_index("tx")
    return section, y, x, (section + x) % 2


def packed(column):
    quarter = column.shape[0] // 4
    return jnp.concatenate([column[q * quarter:(q + 1) * quarter] for q in range(4)], axis=1)


def unpacked(block):
    return jnp.concatenate([block[:, q * HALF:(q + 1) * HALF] for q in range(4)], axis=0)


def inner(half, value):
    return value[:, HALF:] if half == 0 else value[:, :value.shape[1] - HALF]


def outer(half, value):
    return value[:, :HALF] if half == 0 else value[:, value.shape[1] - HALF:]


def packed_wide(half, value):
    tiles = inner(half, value)
    blocks = [tiles[:, t * PATCH:(t + 1) * PATCH] for t in range(tiles.shape[1] // PATCH)]
    return jnp.concatenate(blocks + [packed(outer(half, value))], axis=0)


def unpacked_wide(block, tall):
    full = block.shape[0] // tall
    tiles = [block[t * tall:(t + 1) * tall] for t in range(full)]
    return jnp.concatenate(tiles, axis=1), unpacked(block[full * tall:])


def own_lanes(half, core, width):
    return slice(0, core) if half == 0 else slice(width - core, width)


def by_half(half, branch):
    for h in range(2):
        pl.when(half == h)(functools.partial(branch, h))


def cut_kernel(core, tile_ref, other_ref, even_ref, odd_ref):
    _, y, _, half = where_am_i()
    tall, width = tile_ref.shape
    lower = y % 2 == 1
    first, last = tile_ref[:HALF], tile_ref[tall - HALF:]
    even_ref[...] = jnp.where(lower, first, last)
    odd_ref[...] = jnp.where(lower, last, first)

    def branch(h):
        other_ref[...] = packed_wide(1 - h, tile_ref[:, own_lanes(1 - h, core, width)])

    by_half(half, branch)


def borders_kernel(core, ny, tile_ref, even_ref, odd_ref, strips_ref, near_ref, past_ref):
    _, y, _, half = where_am_i()
    width = tile_ref.shape[1]
    above, below = around(y, ny, even_ref[...], odd_ref[...])

    def column(lanes):
        return packed(jnp.concatenate([above[:, lanes], tile_ref[:, lanes], below[:, lanes]], axis=0))

    first, last = column(slice(0, HALF)), column(slice(width - HALF, width))

    def branch(h):
        lanes = own_lanes(1 - h, core, width)
        strips_ref[...] = packed_wide(1 - h, jnp.concatenate([above[:, lanes], below[:, lanes]], axis=0))
        near_ref[...], past_ref[...] = (first, last) if h == 0 else (last, first)

    by_half(half, branch)


def border_patches(h, side, edge, tiles):
    need = PATCH - 2 * HALF
    if h == 0:
        return jnp.concatenate([side, edge, tiles[:, :need]], axis=1)
    return jnp.concatenate([tiles[:, tiles.shape[1] - need:], edge, side], axis=1)


def masked_side(half, x, nx, side_ref):
    at_end = jnp.where(half == 0, x == 0, x == nx - 1)
    return jnp.where(at_end, 0.0, unpacked(side_ref[...]))


def own_value(h, core, tile_ref, above, below):
    lanes = own_lanes(h, core, tile_ref.shape[1])
    return jnp.concatenate([above[:, lanes], tile_ref[:, lanes], below[:, lanes]], axis=0)


def own_kernel(rows, cols, ny, tile_ref, even_ref, odd_ref, left_ref, free_ref, high_ref, low_ref):
    _, y, _, half = where_am_i()
    core = cols * STRIDE + HALF
    above, below = around(y, ny, even_ref[...], odd_ref[...])

    def branch(h):
        keep_region(inner(h, own_value(h, core, tile_ref, above, below)), cols - 1, high_ref, low_ref)

    by_half(half, branch)
    left_dft(cols - 1, range(rows), high_ref, low_ref, left_ref, free_ref)


def other_parts(rows, other_ref, strips_ref):
    tiles, edge = unpacked_wide(other_ref[...], rows * STRIDE)
    more_tiles, more_edge = unpacked_wide(strips_ref[...], 2 * HALF)
    return (jnp.concatenate([more[:HALF], middle, more[HALF:]], axis=0)
            for more, middle in ((more_tiles, tiles), (more_edge, edge)))


def free_kernel(rows, cols, own_ref, other_ref, strips_ref, left_ref, right_ref, back_ref, flow_ref,
                high_ref, low_ref, half_ref, *stats):
    section, _, _, half = where_am_i()
    tiles, _ = other_parts(rows, other_ref, strips_ref)
    keep_region(tiles, cols - 1, high_ref, low_ref)
    left_dft(cols - 1, range(rows), high_ref, low_ref, left_ref, half_ref)

    def put(c, i, row):
        flow_ref[c * rows + i:c * rows + i + 1, :] = row

    sign = jnp.where(section == 0, 1.0, -1.0)
    count = rows * (cols - 1)
    correlate(rows, cols - 1, count, sign, own_ref, half_ref, right_ref, back_ref, 1 - half, put, *stats)


def border_kernel(rows, cols, ny, nx, tile_ref, even_ref, odd_ref, side_ref, other_ref, strips_ref, cross_ref,
                  before_ref, left_ref, right_ref, back_ref, flow_ref,
                  own_high, own_low, high_ref, low_ref, own_half, half_ref, *stats):
    section, y, x, half = where_am_i()
    core = cols * STRIDE + HALF
    above, below = around(y, ny, even_ref[...], odd_ref[...])
    tiles, edge = other_parts(rows, other_ref, strips_ref)
    own_side, side = masked_side(half, x, nx, side_ref), masked_side(half, x, nx, cross_ref)

    def branch(h):
        own = own_value(h, core, tile_ref, above, below)
        keep_region(border_patches(h, own_side, outer(h, own), inner(h, own)), 1, own_high, own_low)
        keep_region(border_patches(h, side, edge, tiles), 1, high_ref, low_ref)

    by_half(half, branch)
    left_dft(1, range(rows), own_high, own_low, left_ref, own_half)
    left_dft(1, range(rows), high_ref, low_ref, left_ref, half_ref)

    def put(c, i, row):
        at = slice(c * rows + i, c * rows + i + 1)
        flow_ref[at, :] = before_ref[at, :] + row

    sign = jnp.where(section == 0, 1.0, -1.0)
    lane = (cols - 1) * half
    correlate(rows, 1, rows, sign, own_half, half_ref, right_ref, back_ref, lane, put, *stats)


def window_kernel(width, nx, own_ref, mate_ref, near_ref, far_ref, out_ref):
    _, _, x, place = where_am_i()
    half = place == 1
    own, other, close, beyond = own_ref[...], mate_ref[...], near_ref[...], far_ref[...]
    lane = lax.broadcasted_iota(jnp.int32, own.shape, 1)
    begin = jnp.where(x == 0, 0.0, jnp.where(half, beyond, close))
    left = jnp.where(half, other, own)
    right = jnp.where(half, own, other)
    end = jnp.where(x == nx - 1, 0.0, jnp.where(half, close, beyond))
    begin, left = pltpu.roll(begin, PATCH + 2 - width, 1), pltpu.roll(left, 2, 1)
    right, end = pltpu.roll(right, 2 + width, 1), pltpu.roll(end, 2 + 2 * width, 1)
    value = jnp.where(lane < 2, begin, jnp.where(lane < 2 + width, left, right))
    value = jnp.where(lane < 2 + 2 * width, value, jnp.where(lane < 4 + 2 * width, end, 0.0))
    out_ref[...] = value


def relax_kernel(rows, cols, ny, nx, own_ref, even_ref, odd_ref, mesh_ref, earlier_ref):
    section, y, x, _ = where_am_i()
    above, below = around(y, ny, even_ref[...], odd_ref[...])
    own = own_ref[...]
    tall = rows + 4
    shape = (tall, PATCH)
    row = lax.broadcasted_iota(jnp.int32, shape, 0) - 2 + y * rows
    col = lax.broadcasted_iota(jnp.int32, shape, 1) - 2 + x * cols
    inside = (row >= 0) & (row < ny * rows) & (col >= 0) & (col < nx * cols)

    def step(mesh, flow):
        nearby = (
            pltpu.roll(mesh, 1, 0) + pltpu.roll(mesh, tall - 1, 0)
            + pltpu.roll(mesh, 1, 1) + pltpu.roll(mesh, PATCH - 1, 1)
        )
        lap = nearby - 4.0 * mesh
        return jnp.where(inside, mesh + rate * (stiffness * lap + flow - mesh), 0.0)

    for c in range(2):
        flow = jnp.concatenate(
            [above[(c + 1) * rows - 2:(c + 1) * rows], own[c * rows:(c + 1) * rows],
             below[c * rows:c * rows + 2]], axis=0)
        flow = jnp.where(inside, flow, 0.0)
        mesh = step(step(flow, flow), flow)
        mesh = pltpu.roll(pltpu.roll(mesh, tall - 2, 0), PATCH - 2, 1)[:rows, :cols]
        mesh_ref[0, c] = jnp.where(section == 0, mesh, 0.0)
        earlier_ref[0, c] = jnp.where(section == 0, 0.0, mesh)


def shared_section(images):
    tile = images[0]
    ny, nx = lax.axis_size("ty"), lax.axis_size("tx")
    rows, cols = tile.shape[0] // STRIDE, tile.shape[1] // STRIDE
    half = cols // 2
    core, tall = half * STRIDE + HALF, tile.shape[0]

    strip = floats(HALF, tile.shape[1])
    other, even, odd = kernel_call(
        functools.partial(cut_kernel, core), (floats(tall * core // PATCH, PATCH), strip, strip), tile,
    )
    other = along(other, mate)
    even, odd = pairs_even(even), pairs_odd(odd)
    edge = floats((tall + 2 * HALF) // 4, PATCH)
    strips, side, cross = kernel_call(
        functools.partial(borders_kernel, core, ny), (floats(2 * HALF * core // PATCH, PATCH), edge, edge),
        tile, even, odd,
    )
    side, cross = along(side, near), along(cross, past)
    strips = along(strips, mate)
    left, right, back = tables()
    free, border = half_shape(rows, half - 1), half_shape(rows, 1)
    own = kernel_call(
        functools.partial(own_kernel, rows, half, ny), floats(*free), tile, even, odd, left,
        scratch=region_scratch(rows, half - 1),
    )
    flow = kernel_call(
        functools.partial(free_kernel, rows, half), floats(2 * rows, PATCH),
        own, other, strips, left, right, back,
        scratch=region_scratch(rows, half - 1) + [pltpu.VMEM(free, jnp.float32)] + stats_scratch(rows, half - 1),
    )
    flow = kernel_call(
        functools.partial(border_kernel, rows, half, ny, nx), floats(2 * rows, PATCH),
        tile, even, odd, side, other, strips, cross, flow, left, right, back,
        scratch=region_scratch(rows, 1) * 2 + [pltpu.VMEM(border, jnp.float32)] * 2 + stats_scratch(rows, 1),
    )
    window = kernel_call(
        functools.partial(window_kernel, half, nx), floats(*flow.shape),
        flow, along(flow, mate), along(flow, near),
        along(flow, far),
    )
    out = floats(1, 2, rows, cols)
    return kernel_call(
        functools.partial(relax_kernel, rows, cols, ny, nx), (out, out),
        window, pairs_even(window), pairs_odd(window), last=True,
    )


def solution(mesh):
    in_specs = (P("sec", "ty", "tx"),)
    out_specs = (P("sec", None, "ty", "tx"), P("sec", None, "ty", "tx"))
    even = mesh.shape["ty"] % 2 == 0 and mesh.shape["tx"] % 2 == 0
    shared = mesh.shape["sec"] == 2 and even

    def body(images):
        return (shared_section if shared else whole_sections)(images)

    return jax.shard_map(body, mesh=mesh, in_specs=in_specs, out_specs=out_specs, check_vma=False)
```
